32 devices in a mesh: dp: 4 (over y, x), row: 4 (over z), col: 2 (over core).
Axes of the slice: x: 2, y: 2, z: 4, core: 2. Of those that a mesh axis runs over, the one named last changes fastest.
Arguments:
- tokens: bfloat16 [8, 2048, 1024], P('dp', 'row', 'col'), may hold values from -6 to 6
- segment: int32 [8, 2048], P('dp'), may hold values from 0 to 9, never falling along the last dimension, each value on 1 to 1024 neighbouring positions
- w_query: bfloat16 [1024, 1024], P(('dp', 'row'), 'col'), may hold values from -0.1875 to 0.1875
- w_key: bfloat16 [1024, 1024], P(('dp', 'row'), 'col'), may hold values from -0.1875 to 0.1875
- w_value: bfloat16 [1024, 1024], P(('dp', 'row'), 'col'), may hold values from -0.1875 to 0.1875
- w_out: bfloat16 [1024, 1024], P(('dp', 'row'), 'col'), may hold values from -0.75 to 0.75
- w_up: bfloat16 [1024, 4096], P(('dp', 'row'), 'col'), may hold values from -0.1875 to 0.1875
- w_down: bfloat16 [1024, 4096], P(('dp', 'row'), 'col'), may hold values from -0.09375 to 0.09375
- inner_gain: float32 [1024], P('col'), may hold values from 0.1 to 1.9
- inner_shift: float32 [1024], P('col'), may hold values from -3 to 3
- outer_gain: float32 [1024], P('col'), may hold values from 0.1 to 1.9
- outer_shift: float32 [1024], P('col'), may hold values from -3 to 3
- cotangent: float32 [8, 2048, 1024], P('dp', 'row', 'col'), may hold values from -10 to 10
Outputs:
- layer_out: bfloat16 [8, 2048, 1024], P('dp', 'row', 'col')
- input_grad: float32 [8, 2048, 1024], P('dp', 'row', 'col')
- grad_query: float32 [1024, 1024], P(('dp', 'row'), 'col')
- grad_key: float32 [1024, 1024], P(('dp', 'row'), 'col')
- grad_value: float32 [1024, 1024], P(('dp', 'row'), 'col')
- grad_out: float32 [1024, 1024], P(('dp', 'row'), 'col')
- grad_up: float32 [1024, 4096], P(('dp', 'row'), 'col')
- grad_down: float32 [1024, 4096], P(('dp', 'row'), 'col')
- norm_grads: float32 [4, 1024], P(None, 'col')
The draws below stay inside these ranges and needn't reach their ends.
All inputs are finite; a program needn't handle non-finite values.
Results may differ from the reference program's by a relative error of at most 0.013.
Values may be sent and summed in bfloat16 or wider, within the bound.
No kernel may reach another device: no remote copies, remote signals or barrier semaphores. Data moves between devices by JAX's collectives and lax.ppermute only.
A program may use at most 320 MiB of HBM per device.

```python
import math
import jax
import jax.numpy as jnp
import numpy as np
from jax import lax

D = 1024
HEADS = 16
HEAD_DIM = 64
FF = 4096
L = 2048
SEQS = 8


def draw_cotangent(key, part):
    order = (jnp.arange(SEQS * L, dtype=jnp.float32) / (SEQS * L)).reshape(SEQS, L, 1)
    rising = 0.5 + 1.5 * order
    jitter = jnp.clip(jax.random.normal(key, (SEQS, L, D), jnp.float32), -5.0, 5.0)
    return jitter * rising


def block_levels(own_key, extent, cuts, smallest, high):
    gain = 1.0
    for dim, shards_of in cuts:
        steps = jax.random.uniform(jax.random.fold_in(jax.random.fold_in(own_key, 6), dim), (shards_of,), jnp.float32, smallest / len(cuts), high / len(cuts))
        gain = gain * jnp.repeat(jnp.exp(steps), extent[dim] // shards_of).reshape((-1,) + (1,) * (len(extent) - 1 - dim))
    return gain


def split_up(count, total, limit, lean):
    loads = [(1 << 20) // math.isqrt(rank ** lean) + 1 for rank in range(2, count + 1)]
    surplus, given = total - limit - (count - 1), [1] * (count - 1)
    while surplus > 0:
        free = [i for i in range(count - 1) if given[i] < limit]
        mass, remaining = sum([loads[i] for i in free]), surplus
        for i in free:
            more = min(limit - given[i], max(1, remaining * loads[i] // mass), surplus)
            given[i] = given[i] + more
            surplus = surplus - more
    return np.array([limit] + given)


def ragged(own_key, number_of, total, bound, skew):
    if number_of == 2:
        one = jax.random.randint(own_key, (), max(1, total - bound), min(bound, total - 1) + 1)
        return jnp.stack([one, total - one])
    sizes = jnp.asarray(split_up(number_of, total, bound, skew), jnp.int32)
    pairs = (number_of - 1) // 2
    source_of, taker = sizes[1:1 + 2 * pairs:2], sizes[2:2 + 2 * pairs:2]
    slack = jnp.minimum(source_of - 1, bound - taker)
    passed = jax.random.randint(jax.random.fold_in(own_key, 1), (pairs,), 0, 1 << 20) % (slack + 1)
    sizes = sizes.at[1:1 + 2 * pairs:2].set(source_of - passed).at[2:2 + 2 * pairs:2].set(taker + passed)
    return sizes[jax.random.permutation(jax.random.fold_in(own_key, 2), number_of)]


def gaussian(stream_key, dims, width, bound, pieces=(), kind=jnp.bfloat16):
    factor_of = block_levels(stream_key, dims, pieces, -0.22, 0.18) if pieces else 1.0
    array = jax.random.normal(stream_key, dims, jnp.float32) * width * factor_of
    return jnp.minimum(jnp.maximum(array, -bound), bound).astype(kind)


def setup_inputs(seed: int = 0) -> dict:
    keys = jax.random.split(jax.random.key(seed), 14)
    return {
        "tokens": gaussian(keys[0], (SEQS, L, D), 1.0, 6.0, ((0, 4), (1, 4), (2, 2))),
        "segment": jax.vmap(lambda own: jnp.searchsorted(jnp.cumsum(ragged(own, 10, L, L // 2, 1)), jnp.arange(L), side="right"))(jax.random.split(keys[1], SEQS)).reshape((SEQS, L)).astype(jnp.int32),
        "w_query": gaussian(keys[2], (D, D), D ** -0.5, 0.1875, ((0, 16), (1, 2))),
        "w_key": gaussian(keys[3], (D, D), D ** -0.5, 0.1875, ((0, 16), (1, 2))),
        "w_value": gaussian(keys[4], (D, D), D ** -0.5, 0.1875, ((0, 16), (1, 2))),
        "w_out": gaussian(keys[5], (D, D), 64 ** -0.5, 0.75, ((0, 16), (1, 2))),
        "w_up": gaussian(keys[6], (D, FF), D ** -0.5, 0.1875, ((0, 16), (1, 2))),
        "w_down": gaussian(keys[7], (D, FF), FF ** -0.5, 0.09375, ((0, 16), (1, 2))),
        "inner_gain": jnp.clip(1.0 + 0.18 * jax.random.normal(keys[8], (D,), jnp.float32), 0.1, 1.9),
        "inner_shift": gaussian(keys[9], (D,), 0.5, 3.0, ((0, 2),), jnp.float32),
        "outer_gain": jnp.clip(1.0 + 0.18 * jax.random.normal(keys[10], (D,), jnp.float32), 0.1, 1.9),
        "outer_shift": gaussian(keys[11], (D,), 0.5, 3.0, ((0, 2),), jnp.float32),
        "cotangent": draw_cotangent(jax.random.fold_in(keys[13], 71), 0),
    }


EPS = 1e-05
ROOT_HALF = 0.7071067811865476
INV_ROOT_TAU = 0.3989422804014327

def gelu_value(inputs):
    return 0.5 * inputs * (1.0 + lax.erf(inputs * ROOT_HALF))

def gelu_slope(inputs):
    return 0.5 * (1.0 + lax.erf(inputs * ROOT_HALF)) + inputs * jnp.exp(-0.5 * inputs * inputs) * INV_ROOT_TAU

def rounded(values):
    return lax.optimization_barrier(values.astype(jnp.bfloat16))

def norm_forward(summed, norm_gain, norm_shift):
    average = lax.optimization_barrier(jnp.mean(summed, axis=-1, keepdims=True))
    spread = lax.optimization_barrier(jnp.mean(summed * summed, axis=-1, keepdims=True)) - average * average
    scaling = lax.rsqrt(spread + EPS)
    normed = (summed - average) * scaling
    return (normed * norm_gain + norm_shift, normed, scaling)

def norm_backward(upstream, normed, scaling, norm_gain):
    scaled = upstream * norm_gain
    offset_mean = lax.optimization_barrier(jnp.mean(scaled, axis=-1, keepdims=True))
    slope_mean = lax.optimization_barrier(jnp.mean(scaled * normed, axis=-1, keepdims=True))
    return scaling * (scaled - offset_mean - normed * slope_mean)

def split_heads(values):
    return values.reshape(values.shape[0], HEADS, HEAD_DIM).astype(jnp.float32)

def merge_heads(values):
    return values.reshape(values.shape[0], HEADS * HEAD_DIM)

def reference(tokens, segment, w_query, w_key, w_value, w_out, w_up, w_down, inner_gain, inner_shift, outer_gain, outer_shift, cotangent):
    scale_factor = HEAD_DIM ** (-0.5)
    f32 = jnp.float32

    def sequence(totals, inputs):
        series, labels, upstream = inputs
        queries = rounded(jnp.dot(series, w_query, preferred_element_type=f32))
        key_rows = rounded(jnp.dot(series, w_key, preferred_element_type=f32))
        value_rows = rounded(jnp.dot(series, w_value, preferred_element_type=f32))
        head_query = split_heads(queries)
        head_key = split_heads(key_rows)
        head_value = split_heads(value_rows)
        inside = labels[:, None] == labels[None, :]
        scores = jnp.einsum('qhe,khe->hqk', head_query, head_key) * scale_factor
        scores = jnp.where(inside[None], scores, -jnp.inf)
        highest = lax.optimization_barrier(jnp.max(scores, axis=-1, keepdims=True))
        log_total = highest + jnp.log(lax.optimization_barrier(jnp.sum(jnp.exp(scores - highest), axis=-1, keepdims=True)))
        chance = jnp.exp(scores - log_total)
        attention = rounded(chance).astype(f32)
        mixture = rounded(merge_heads(jnp.einsum('hqk,khe->qhe', attention, head_value)))
        summed = series.astype(f32) + jnp.dot(mixture, w_out.T, preferred_element_type=f32)
        middle, inner_normed, inner_scaling = norm_forward(summed, inner_gain, inner_shift)
        middle_half = rounded(middle)
        hidden = jnp.dot(middle_half, w_up, preferred_element_type=f32)
        active = rounded(gelu_value(hidden))
        second_sum = middle + jnp.dot(active, w_down.T, preferred_element_type=f32)
        result, outer_normed, outer_scaling = norm_forward(second_sum, outer_gain, outer_shift)
        layer_out = result.astype(jnp.bfloat16)
        outer_gain_grad = lax.optimization_barrier(jnp.sum(upstream * outer_normed, axis=0))
        outer_shift_grad = lax.optimization_barrier(jnp.sum(upstream, axis=0))
        second_grad = norm_backward(upstream, outer_normed, outer_scaling, outer_gain)
        second_half = rounded(second_grad)
        grad_down = jnp.dot(second_half.T, active, preferred_element_type=f32)
        active_grad = rounded(jnp.dot(second_half, w_down, preferred_element_type=f32) * gelu_slope(hidden))
        grad_up = jnp.dot(middle_half.T, active_grad, preferred_element_type=f32)
        middle_grad = second_grad + jnp.dot(active_grad, w_up.T, preferred_element_type=f32)
        inner_gain_grad = lax.optimization_barrier(jnp.sum(middle_grad * inner_normed, axis=0))
        inner_shift_grad = lax.optimization_barrier(jnp.sum(middle_grad, axis=0))
        summed_grad = norm_backward(middle_grad, inner_normed, inner_scaling, inner_gain)
        summed_half = rounded(summed_grad)
        grad_out = jnp.dot(summed_half.T, mixture, preferred_element_type=f32)
        mixture_grad = rounded(jnp.dot(summed_half, w_out, preferred_element_type=f32))
        head_grad = split_heads(mixture_grad)
        chance_grad = jnp.einsum('qhe,khe->hqk', head_grad, head_value)
        within = lax.optimization_barrier(jnp.sum(chance * chance_grad, axis=-1, keepdims=True))
        score_grad = rounded(chance * (chance_grad - within) * scale_factor).astype(f32)
        query_grad = rounded(merge_heads(jnp.einsum('hqk,khe->qhe', score_grad, head_key)))
        key_grad = rounded(merge_heads(jnp.einsum('hqk,qhe->khe', score_grad, head_query)))
        value_grad = rounded(merge_heads(jnp.einsum('hqk,qhe->khe', attention, head_grad)))
        grad_query = jnp.dot(series.T, query_grad, preferred_element_type=f32)
        grad_key = jnp.dot(series.T, key_grad, preferred_element_type=f32)
        grad_value = jnp.dot(series.T, value_grad, preferred_element_type=f32)
        input_grad = summed_grad + jnp.dot(query_grad, w_query.T, preferred_element_type=f32)
        input_grad = input_grad + jnp.dot(key_grad, w_key.T, preferred_element_type=f32)
        input_grad = input_grad + jnp.dot(value_grad, w_value.T, preferred_element_type=f32)
        norm_terms = jnp.stack([inner_gain_grad, inner_shift_grad, outer_gain_grad, outer_shift_grad])
        fresh = (grad_query, grad_key, grad_value, grad_out, grad_up, grad_down, norm_terms)
        return (jax.tree.map(jnp.add, totals, fresh), (layer_out, input_grad))
    starting = (jnp.zeros((D, D), f32), jnp.zeros((D, D), f32), jnp.zeros((D, D), f32), jnp.zeros((D, D), f32), jnp.zeros((D, FF), f32), jnp.zeros((D, FF), f32), jnp.zeros((4, D), f32))
    totals, stacked = lax.scan(sequence, starting, (tokens, segment, cotangent))
    return (stacked[0], stacked[1], totals[0], totals[1], totals[2], totals[3], totals[4], totals[5], totals[6])
```

```python
import jax
import jax.numpy as jnp
from jax import lax
from jax.experimental import pallas as pl
from jax.experimental.pallas import tpu as pltpu
from jax.sharding import PartitionSpec as P

D = 1024
HEAD_DIM = 64


EPS = 1e-05
ROOT_HALF = 0.7071067811865476
INV_ROOT_TAU = 0.3989422804014327


def gelu_value(inputs):
    return 0.5 * inputs * (1.0 + lax.erf(inputs * ROOT_HALF))


def gelu_slope(inputs):
    return (
        0.5 * (1.0 + lax.erf(inputs * ROOT_HALF))
        + inputs * jnp.exp(-0.5 * inputs * inputs) * INV_ROOT_TAU
    )


def widen(values):
    return lax.all_gather(values, "col", axis=2, tiled=True)


def narrow(partial_value):
    return lax.psum_scatter(partial_value, "col", scatter_dimension=2, tiled=True)


def norm_forward(summed, norm_gain, norm_shift):
    row_sums, squares = lax.psum(
        (jnp.sum(summed, axis=-1, keepdims=True), jnp.sum(summed * summed, axis=-1, keepdims=True)),
        "col",
    )
    average = row_sums / D
    spread = squares / D - average * average
    scaling = lax.rsqrt(spread + EPS)
    normed = (summed - average) * scaling
    return (normed * norm_gain + norm_shift, normed, scaling)


def norm_backward(upstream, normed, scaling, norm_gain):
    scaled = upstream * norm_gain
    offset_sum, slope_sum = lax.psum(
        (jnp.sum(scaled, axis=-1, keepdims=True), jnp.sum(scaled * normed, axis=-1, keepdims=True)),
        "col",
    )
    return scaling * (scaled - offset_sum / D - normed * (slope_sum / D))


def head_view(values):
    return values.reshape(values.shape[0], values.shape[1] // HEAD_DIM, HEAD_DIM)


def masked_scores(queries, key_rows, own_labels, all_labels):
    scores = jnp.einsum(
        "qhe,khe->hqk", head_view(queries), head_view(key_rows), preferred_element_type=jnp.float32
    ) * HEAD_DIM ** (-0.5)
    inside = own_labels[:, None] == all_labels[None, :]
    return jnp.where(inside[None], scores, -jnp.inf)


def attend_forward(inputs):
    queries, key_rows, value_rows, own_labels, all_labels = inputs
    scores = masked_scores(queries, key_rows, own_labels, all_labels)
    highest = jnp.max(scores, axis=-1, keepdims=True)
    log_total = highest + jnp.log(jnp.sum(jnp.exp(scores - highest), axis=-1, keepdims=True))
    attention = jnp.exp(scores - log_total).astype(jnp.bfloat16)
    mixture = jnp.einsum(
        "hqk,khe->qhe", attention, head_view(value_rows), preferred_element_type=jnp.float32
    )
    return (mixture.reshape(queries.shape).astype(jnp.bfloat16), log_total)


def attend_backward(inputs):
    queries, key_rows, value_rows, own_labels, all_labels, log_total, mixture_grad = inputs
    scores = masked_scores(queries, key_rows, own_labels, all_labels)
    chance = jnp.exp(scores - log_total)
    attention = chance.astype(jnp.bfloat16)
    chance_grad = jnp.einsum(
        "qhe,khe->hqk",
        head_view(mixture_grad),
        head_view(value_rows),
        preferred_element_type=jnp.float32,
    )
    within = jnp.sum(chance * chance_grad, axis=-1, keepdims=True)
    score_grad = (chance * (chance_grad - within) * HEAD_DIM ** (-0.5)).astype(jnp.bfloat16)
    query_grad = jnp.einsum(
        "hqk,khe->qhe", score_grad, head_view(key_rows), preferred_element_type=jnp.float32
    )
    key_part = jnp.einsum(
        "hqk,qhe->khe", score_grad, head_view(queries), preferred_element_type=jnp.float32
    )
    value_part = jnp.einsum(
        "hqk,qhe->khe", attention, head_view(mixture_grad), preferred_element_type=jnp.float32
    )
    return (
        query_grad.reshape(queries.shape).astype(jnp.bfloat16),
        key_part.reshape(key_rows.shape),
        value_part.reshape(value_rows.shape),
    )


def local(
    tokens,
    segment,
    w_query,
    w_key,
    w_value,
    w_out,
    w_up,
    w_down,
    inner_gain,
    inner_shift,
    outer_gain,
    outer_shift,
    cotangent,
):
    f32 = jnp.float32
    half = jnp.bfloat16
    gathered = (
        lax.all_gather(w_query, ("dp", "row"), axis=0, tiled=True),
        lax.all_gather(w_key, ("dp", "row"), axis=0, tiled=True),
        lax.all_gather(w_value, ("dp", "row"), axis=0, tiled=True),
        lax.all_gather(w_out, ("dp", "row"), axis=0, tiled=True),
        lax.all_gather(w_up, ("dp", "row"), axis=0, tiled=True),
        lax.all_gather(w_down, ("dp", "row"), axis=0, tiled=True),
    )
    full_query, full_key, full_value, full_out, full_up, full_down = gathered
    row_count = tokens.shape[1]
    own_labels = lax.dynamic_slice_in_dim(segment, lax.axis_index("row") * row_count, row_count, 1)
    wide_tokens = widen(tokens)
    queries = jnp.einsum("sqd,de->sqe", wide_tokens, full_query, preferred_element_type=f32).astype(
        half
    )
    key_rows = jnp.einsum("sqd,de->sqe", wide_tokens, full_key, preferred_element_type=f32).astype(
        half
    )
    value_rows = jnp.einsum(
        "sqd,de->sqe", wide_tokens, full_value, preferred_element_type=f32
    ).astype(half)
    all_keys, all_values = (
        lax.all_gather(key_rows, "row", axis=1, tiled=True),
        lax.all_gather(value_rows, "row", axis=1, tiled=True),
    )
    mixture, log_total = lax.map(
        attend_forward, (queries, all_keys, all_values, own_labels, segment)
    )
    summed = tokens.astype(f32) + narrow(
        jnp.einsum("sqe,de->sqd", mixture, full_out, preferred_element_type=f32)
    )
    middle, inner_normed, inner_scaling = norm_forward(summed, inner_gain, inner_shift)
    wide_middle = widen(middle.astype(half))
    hidden = jnp.einsum("sqd,df->sqf", wide_middle, full_up, preferred_element_type=f32)
    active = gelu_value(hidden).astype(half)
    second_sum = middle + narrow(
        jnp.einsum("sqf,df->sqd", active, full_down, preferred_element_type=f32)
    )
    result, outer_normed, outer_scaling = norm_forward(second_sum, outer_gain, outer_shift)
    layer_out = result.astype(half)
    outer_gain_grad = jnp.sum(cotangent * outer_normed, axis=(0, 1))
    outer_shift_grad = jnp.sum(cotangent, axis=(0, 1))
    second_grad = norm_backward(cotangent, outer_normed, outer_scaling, outer_gain)
    wide_second = widen(second_grad.astype(half))
    grad_down = jnp.einsum("sqd,sqf->df", wide_second, active, preferred_element_type=f32)
    active_grad = (
        jnp.einsum("sqd,df->sqf", wide_second, full_down, preferred_element_type=f32)
        * gelu_slope(hidden)
    ).astype(half)
    grad_up = jnp.einsum("sqd,sqf->df", wide_middle, active_grad, preferred_element_type=f32)
    middle_grad = second_grad + narrow(
        jnp.einsum("sqf,df->sqd", active_grad, full_up, preferred_element_type=f32)
    )
    inner_gain_grad = jnp.sum(middle_grad * inner_normed, axis=(0, 1))
    inner_shift_grad = jnp.sum(middle_grad, axis=(0, 1))
    summed_grad = norm_backward(middle_grad, inner_normed, inner_scaling, inner_gain)
    wide_summed = widen(summed_grad.astype(half))
    grad_out = jnp.einsum("sqd,sqe->de", wide_summed, mixture, preferred_element_type=f32)
    mixture_grad = jnp.einsum(
        "sqd,de->sqe", wide_summed, full_out, preferred_element_type=f32
    ).astype(half)
    query_grad, key_part, value_part = lax.map(
        attend_backward,
        (queries, all_keys, all_values, own_labels, segment, log_total, mixture_grad),
    )
    key_sums, value_sums = (
        lax.psum_scatter(key_part, "row", scatter_dimension=1, tiled=True),
        lax.psum_scatter(value_part, "row", scatter_dimension=1, tiled=True),
    )
    key_grad = key_sums.astype(half)
    value_grad = value_sums.astype(half)
    grad_query = jnp.einsum("sqd,sqe->de", wide_tokens, query_grad, preferred_element_type=f32)
    grad_key = jnp.einsum("sqd,sqe->de", wide_tokens, key_grad, preferred_element_type=f32)
    grad_value = jnp.einsum("sqd,sqe->de", wide_tokens, value_grad, preferred_element_type=f32)
    back_sum = jnp.einsum("sqe,de->sqd", query_grad, full_query, preferred_element_type=f32)
    back_sum = back_sum + jnp.einsum("sqe,de->sqd", key_grad, full_key, preferred_element_type=f32)
    back_sum = back_sum + jnp.einsum(
        "sqe,de->sqd", value_grad, full_value, preferred_element_type=f32
    )
    input_grad = summed_grad + narrow(back_sum)
    norm_local = jnp.stack([inner_gain_grad, inner_shift_grad, outer_gain_grad, outer_shift_grad])
    weight_grads = (
        lax.psum_scatter(grad_query, ("dp", "row"), scatter_dimension=0, tiled=True),
        lax.psum_scatter(grad_key, ("dp", "row"), scatter_dimension=0, tiled=True),
        lax.psum_scatter(grad_value, ("dp", "row"), scatter_dimension=0, tiled=True),
        lax.psum_scatter(grad_out, ("dp", "row"), scatter_dimension=0, tiled=True),
        lax.psum_scatter(grad_up, ("dp", "row"), scatter_dimension=0, tiled=True),
        lax.psum_scatter(grad_down, ("dp", "row"), scatter_dimension=0, tiled=True),
    )
    norm_grads = lax.psum(norm_local, ("dp", "row"))
    return (
        layer_out,
        input_grad,
        weight_grads[0],
        weight_grads[1],
        weight_grads[2],
        weight_grads[3],
        weight_grads[4],
        weight_grads[5],
        norm_grads,
    )


PAIR = 128
BLOCK = 256
NEG = -1e30
HEADS = 16
SCALE = HEAD_DIM ** (-0.5)
VMEM_LIMIT = 48 << 20


def fits(mesh):
    sizes = dict(mesh.shape)
    return sizes["col"] == 2 and sizes["dp"] == 4 and sizes["row"] == 4


def head_mask(values, head):
    lane = lax.broadcasted_iota(jnp.int32, values.shape, 1)
    keep = (lane < HEAD_DIM) if head == 0 else (lane >= HEAD_DIM)
    return jnp.where(keep, values, jnp.zeros_like(values))


def dot(left, right):
    return jnp.dot(left, right, preferred_element_type=jnp.float32)


def forward_kernel(low, high, q_t, k, v_t, own, others, out_t, log_total):
    step = pl.program_id(1)
    queries = q_t[...]
    own_labels = own[...]

    def body(j, carry):
        start = pl.multiple_of(j * BLOCK, BLOCK)
        keys = k[pl.ds(start, BLOCK), :]
        labels = others[pl.ds(start, BLOCK), :]
        inside = jnp.concatenate([labels] * (BLOCK // PAIR), axis=1) == own_labels
        state = []
        for head in range(2):
            highest, total, mixed = carry[head]
            scores = jnp.where(inside, dot(head_mask(keys, head), queries), NEG)
            fresh = jnp.maximum(highest, jnp.max(scores, axis=0, keepdims=True))
            chance = jnp.exp(scores - fresh)
            fade = jnp.exp(highest - fresh)
            values = v_t[head * HEAD_DIM : (head + 1) * HEAD_DIM, pl.ds(start, BLOCK)]
            state.append(
                (
                    fresh,
                    total * fade + jnp.sum(chance, axis=0, keepdims=True),
                    mixed * fade + dot(values, chance.astype(jnp.bfloat16)),
                )
            )
        return tuple(state)

    one = (
        jnp.full((1, BLOCK), NEG, jnp.float32),
        jnp.zeros((1, BLOCK), jnp.float32),
        jnp.zeros((HEAD_DIM, BLOCK), jnp.float32),
    )
    final = lax.fori_loop(low[step], high[step], body, (one, one))
    for head in range(2):
        highest, total, mixed = final[head]
        out_t[0, head * HEAD_DIM : (head + 1) * HEAD_DIM, :] = (mixed / total).astype(jnp.bfloat16)
        log_total[0, head : head + 1, :] = highest + jnp.log(total)


def backward_kernel(
    low, high, q, q_t, g, g_t, out_t, log_total, k, v, k_t, own, others, dq, dk, dv, dk_sum, dv_sum
):
    step = pl.program_id(1)

    @pl.when(step == 0)
    def _():
        dk_sum[...] = jnp.zeros_like(dk_sum)
        dv_sum[...] = jnp.zeros_like(dv_sum)

    half = jnp.bfloat16
    queries_t = q_t[...]
    grads_t = g_t[...]
    own_labels = own[...]
    product = grads_t.astype(jnp.float32) * out_t[0].astype(jnp.float32)
    heads = []
    for head in range(2):
        rows = slice(head * HEAD_DIM, (head + 1) * HEAD_DIM)
        heads.append(
            (
                head_mask(q[...], head),
                head_mask(g[...], head),
                jnp.sum(product[rows], axis=0, keepdims=True),
                log_total[0, head : head + 1, :],
            )
        )

    def body(j, carry):
        start = pl.multiple_of(j * BLOCK, BLOCK)
        keys = k[pl.ds(start, BLOCK), :]
        values = v[pl.ds(start, BLOCK), :]
        labels = others[pl.ds(start, BLOCK), :]
        inside = jnp.concatenate([labels] * (BLOCK // PAIR), axis=1) == own_labels
        sums, key_part, value_part = [], None, None
        for head in range(2):
            own_q, own_g, within, total = heads[head]
            scores = dot(head_mask(keys, head), queries_t)
            chance = jnp.where(inside, jnp.exp(scores - total), 0.0)
            chance_grad = dot(head_mask(values, head), grads_t)
            score_grad = (chance * (chance_grad - within)).astype(half)
            value_new = dot(chance.astype(half), own_g)
            key_new = dot(score_grad, own_q)
            keys_t = k_t[head * HEAD_DIM : (head + 1) * HEAD_DIM, pl.ds(start, BLOCK)]
            sums.append(carry[head] + dot(keys_t, score_grad))
            key_part = key_new if key_part is None else key_part + key_new
            value_part = value_new if value_part is None else value_part + value_new
        dk_sum[pl.ds(start, BLOCK), :] += key_part
        dv_sum[pl.ds(start, BLOCK), :] += value_part
        return tuple(sums)

    zero = jnp.zeros((HEAD_DIM, BLOCK), jnp.float32)
    first, second = lax.fori_loop(low[step], high[step], body, (zero, zero))
    both = jnp.concatenate([first, second], axis=0) * SCALE
    dq[...] = jnp.transpose(both).astype(half)

    @pl.when(step == pl.num_programs(1) - 1)
    def _():
        dk[...] = dk_sum[...].astype(half)
        dv[...] = dv_sum[...].astype(half)


def key_ranges(labels):
    blocks = labels.reshape(-1, BLOCK)
    first, last = blocks[:, :1], blocks[:, -1:]
    before = jnp.sum((labels[None, :] < first).astype(jnp.int32), axis=1)
    upto = jnp.sum((labels[None, :] <= last).astype(jnp.int32), axis=1)
    return before // BLOCK, (upto + BLOCK - 1) // BLOCK


def attend(qkv, qkv_t, labels, ranges, wide_labels, row_count):
    length, width = qkv.shape
    width = width // 3
    pairs = width // PAIR
    inner = row_count // BLOCK
    grid = (pairs, length // BLOCK)
    area = 4 * pairs * length * length // 2
    out_t, log_total = pl.pallas_call(
        forward_kernel,
        out_shape=(
            jax.ShapeDtypeStruct((length // row_count, width, row_count), jnp.bfloat16),
            jax.ShapeDtypeStruct((pairs, 8, length), jnp.float32),
        ),
        grid_spec=pltpu.PrefetchScalarGridSpec(
            num_scalar_prefetch=2,
            grid=grid,
            in_specs=[
                pl.BlockSpec((PAIR, BLOCK), lambda h, i, lo, hi: (h, i)),
                pl.BlockSpec((length, PAIR), lambda h, i, lo, hi: (0, pairs + h)),
                pl.BlockSpec((PAIR, length), lambda h, i, lo, hi: (2 * pairs + h, 0)),
                pl.BlockSpec((1, BLOCK), lambda h, i, lo, hi: (0, i)),
                pl.BlockSpec((length, PAIR), lambda h, i, lo, hi: (0, 0)),
            ],
            out_specs=(
                pl.BlockSpec((1, PAIR, BLOCK), lambda h, i, lo, hi: (i // inner, h, i % inner)),
                pl.BlockSpec((1, 8, BLOCK), lambda h, i, lo, hi: (h, 0, i)),
            ),
        ),
        compiler_params=pltpu.CompilerParams(vmem_limit_bytes=VMEM_LIMIT),
        cost_estimate=pl.CostEstimate(
            flops=area * 256 * 2, bytes_accessed=8 << 20, transcendentals=area // 2
        ),
    )(*ranges, qkv_t, qkv, qkv_t, labels, wide_labels)
    return out_t, log_total


def attend_back(qkv, qkv_t, labels, ranges, wide_labels, row_count, out_t, log_total, grads, grads_t):
    length, width = grads.shape
    pairs = width // PAIR
    inner = row_count // BLOCK
    grid = (pairs, length // BLOCK)
    area = 4 * pairs * length * length // 2
    shape = jax.ShapeDtypeStruct((length, width), jnp.bfloat16)
    return pl.pallas_call(
        backward_kernel,
        out_shape=(shape, shape, shape),
        grid_spec=pltpu.PrefetchScalarGridSpec(
            num_scalar_prefetch=2,
            grid=grid,
            in_specs=[
                pl.BlockSpec((BLOCK, PAIR), lambda h, i, lo, hi: (i, h)),
                pl.BlockSpec((PAIR, BLOCK), lambda h, i, lo, hi: (h, i)),
                pl.BlockSpec((BLOCK, PAIR), lambda h, i, lo, hi: (i, h)),
                pl.BlockSpec((PAIR, BLOCK), lambda h, i, lo, hi: (h, i)),
                pl.BlockSpec((1, PAIR, BLOCK), lambda h, i, lo, hi: (i // inner, h, i % inner)),
                pl.BlockSpec((1, 8, BLOCK), lambda h, i, lo, hi: (h, 0, i)),
                pl.BlockSpec((length, PAIR), lambda h, i, lo, hi: (0, pairs + h)),
                pl.BlockSpec((length, PAIR), lambda h, i, lo, hi: (0, 2 * pairs + h)),
                pl.BlockSpec((PAIR, length), lambda h, i, lo, hi: (pairs + h, 0)),
                pl.BlockSpec((1, BLOCK), lambda h, i, lo, hi: (0, i)),
                pl.BlockSpec((length, PAIR), lambda h, i, lo, hi: (0, 0)),
            ],
            out_specs=(
                pl.BlockSpec((BLOCK, PAIR), lambda h, i, lo, hi: (i, h)),
                pl.BlockSpec((length, PAIR), lambda h, i, lo, hi: (0, h)),
                pl.BlockSpec((length, PAIR), lambda h, i, lo, hi: (0, h)),
            ),
            scratch_shapes=[
                pltpu.VMEM((length, PAIR), jnp.float32),
                pltpu.VMEM((length, PAIR), jnp.float32),
            ],
        ),
        compiler_params=pltpu.CompilerParams(vmem_limit_bytes=VMEM_LIMIT),
        cost_estimate=pl.CostEstimate(
            flops=area * 256 * 5, bytes_accessed=12 << 20, transcendentals=area // 2
        ),
    )(
        *ranges, qkv, qkv_t, grads, grads_t, out_t, log_total, qkv, qkv, qkv_t, labels, wide_labels
    )


def swap(values):
    return lax.ppermute(values, "col", [(0, 1), (1, 0)])


def flip(values, axis, bit, size=4):
    return lax.ppermute(values, axis, [(i, i ^ bit) for i in range(size)])


def pick(values, index, axis=0):
    return lax.dynamic_index_in_dim(values, index, axis, keepdims=False)


def gather_plane(block, parts):
    me = lax.axis_index("dp")
    rows = block.shape[0] // 2
    top, low = block[:rows], block[rows:]
    top_x = flip(top, "dp", 1)
    low_y = flip(low, "dp", 2)
    top_y = flip(jnp.concatenate([top, top_x]), "dp", 2)
    low_x = flip(jnp.concatenate([low, low_y]), "dp", 1)
    pieces = (
        (0, 0, top),
        (1, 0, top_x),
        (2, 0, top_y[:rows]),
        (3, 0, top_y[rows:]),
        (0, 1, low),
        (2, 1, low_y),
        (1, 1, low_x[:rows]),
        (3, 1, low_x[rows:]),
    )
    outs = []
    for start, stop in parts:
        whole = jnp.zeros((8 * rows, stop - start), block.dtype)
        for bit, second, piece in pieces:
            at = (me ^ bit) * (2 * rows) + second * rows
            whole = lax.dynamic_update_slice_in_dim(whole, piece[:, start:stop], at, 0)
        outs.append(whole)
    return outs


def scatter_plane(grads):
    me = lax.axis_index("dp")
    half, f32 = jnp.bfloat16, jnp.float32
    rows = grads.shape[0] // 8

    def part(bit, second):
        at = (me ^ bit) * (2 * rows) + second * rows
        return lax.dynamic_slice_in_dim(grads, at, rows, 0)

    top_y = flip(jnp.concatenate([part(2, 0), part(3, 0)]), "dp", 2)
    low_x = flip(jnp.concatenate([part(1, 1), part(3, 1)]), "dp", 1)
    top_pass = (part(1, 0).astype(f32) + top_y[rows:].astype(f32)).astype(half)
    low_pass = (part(2, 1).astype(f32) + low_x[rows:].astype(f32)).astype(half)
    top_x = flip(top_pass, "dp", 1)
    low_y = flip(low_pass, "dp", 2)
    top = part(0, 0).astype(f32) + top_y[:rows].astype(f32) + top_x.astype(f32)
    low = part(0, 1).astype(f32) + low_x[:rows].astype(f32) + low_y.astype(f32)
    return jnp.concatenate([top, low])


def whole_norm(summed, gain, shift):
    average = jnp.mean(summed, axis=-1, keepdims=True)
    spread = jnp.mean(summed * summed, axis=-1, keepdims=True) - average * average
    scaling = lax.rsqrt(spread + EPS)
    normed = (summed - average) * scaling
    return (normed * gain + shift, normed, scaling)


def whole_norm_back(upstream, normed, scaling, gain):
    scaled = upstream * gain
    offset = jnp.mean(scaled, axis=-1, keepdims=True)
    slope = jnp.mean(scaled * normed, axis=-1, keepdims=True)
    return scaling * (scaled - offset - normed * slope)


def fast_local(
    tokens,
    segment,
    w_query,
    w_key,
    w_value,
    w_out,
    w_up,
    w_down,
    inner_gain,
    inner_shift,
    outer_gain,
    outer_shift,
    cotangent,
):
    f32 = jnp.float32
    half = jnp.bfloat16
    me = lax.axis_index("dp")
    core = lax.axis_index("col")
    first_core = core == 0
    n_row = lax.axis_size("row")
    row_count = tokens.shape[1]
    length = segment.shape[1]
    block_rows, half_width = w_query.shape
    width = D // n_row
    hidden_half = w_up.shape[1]

    def join(mine, other, axis):
        return jnp.where(
            first_core,
            jnp.concatenate([mine, other], axis=axis),
            jnp.concatenate([other, mine], axis=axis),
        )

    def own_sequence(values):
        return join(pick(values, core), swap(pick(values, 1 - core)), 1)

    def own_columns(values):
        parts = values.reshape(values.shape[0], 2, values.shape[1] // 2)
        return pick(parts, core, 1), pick(parts, 1 - core, 1)

    own_tokens = own_sequence(tokens)
    series = lax.all_gather(own_tokens, "row", axis=0, tiled=True)
    labels = pick(segment, core)
    ranges = key_ranges(labels)
    wide_labels = jnp.broadcast_to(labels[:, None], (length, PAIR))
    labels = labels[None]

    split = block_rows // 2
    thirds = jnp.stack([w_query, w_key, w_value]).reshape(3, 2, split, half_width)
    strip = join(pick(thirds, core, 1), swap(pick(thirds, 1 - core, 1)), 2)
    strip = strip.reshape(3, split, n_row, width).transpose(2, 0, 1, 3)
    strip = lax.all_to_all(strip, "row", 0, 0, tiled=True)
    planes = jnp.zeros((4,) + strip.shape, half)
    for bit in range(4):
        piece = strip if bit == 0 else flip(strip, "dp", bit)
        planes = lax.dynamic_update_slice_in_dim(planes, piece[None], me ^ bit, 0)
    both = join(planes[None], swap(planes)[None], 0)
    w_qkv = both.transpose(1, 2, 0, 4, 3, 5).reshape(D, 3 * width)
    exact_scale = jnp.where(jnp.arange(3 * width) < width, SCALE, 1.0).astype(half)

    out_up = lax.all_gather(jnp.concatenate([w_out, w_up], axis=1), "row", axis=0, tiled=True)
    down_rows = lax.all_gather(w_down, "row", axis=0, tiled=True)
    out_half, up = gather_plane(out_up, ((0, half_width), (half_width, half_width + hidden_half)))
    full_out = join(out_half, swap(out_half), 1)
    (down,) = gather_plane(down_rows, ((0, hidden_half),))

    vectors = jnp.stack([inner_gain, inner_shift, outer_gain, outer_shift])
    vectors = join(vectors, swap(vectors), 1)
    inner_gain, inner_shift, outer_gain, outer_shift = (vectors[i : i + 1] for i in range(4))
    upstream = own_sequence(cotangent)

    qkv = jnp.dot(series, w_qkv * exact_scale, preferred_element_type=f32).astype(half)
    qkv_t = qkv.T
    out_t, log_total = attend(qkv, qkv_t, labels, ranges, wide_labels, row_count)
    mixture_t = lax.all_to_all(out_t, "row", 0, 0, tiled=True).reshape(D, row_count)

    summed = own_tokens.astype(f32) + jnp.einsum(
        "eq,de->qd", mixture_t, full_out, preferred_element_type=f32
    )
    middle, inner_normed, inner_scaling = whole_norm(summed, inner_gain, inner_shift)

    middle_own = middle.astype(half)
    middle_other = swap(middle_own)
    hidden_own = dot(middle_own, up)
    hidden_other = dot(middle_other, up)
    active_own = gelu_value(hidden_own).astype(half)
    active_other = gelu_value(hidden_other).astype(half)
    down_other = jnp.einsum("qf,df->qd", active_other, down, preferred_element_type=f32)
    down_swapped = swap(down_other.astype(half))
    down_own = jnp.einsum("qf,df->qd", active_own, down, preferred_element_type=f32)
    second_sum = middle + (down_own + down_swapped.astype(f32))
    result, outer_normed, outer_scaling = whole_norm(second_sum, outer_gain, outer_shift)
    kept, passed = own_columns(result.astype(half))
    layer_out = join(kept[None], swap(passed)[None], 0)

    outer_gain_grad = jnp.sum(upstream * outer_normed, axis=0)
    outer_shift_grad = jnp.sum(upstream, axis=0)
    second_grad = whole_norm_back(upstream, outer_normed, outer_scaling, outer_gain)
    second_own = second_grad.astype(half)
    second_other = swap(second_own)
    active_grad_own = (dot(second_own, down) * gelu_slope(hidden_own)).astype(half)
    active_grad_other = (dot(second_other, down) * gelu_slope(hidden_other)).astype(half)
    middle_grad_other = jnp.einsum("qf,df->qd", active_grad_other, up, preferred_element_type=f32)
    middle_swapped = swap(middle_grad_other.astype(half))
    middle_grad_own = jnp.einsum("qf,df->qd", active_grad_own, up, preferred_element_type=f32)

    def weight_grad(left, right):
        return jnp.einsum("qd,qf->df", left, right, preferred_element_type=f32)

    grad_down = weight_grad(second_own, active_own) + weight_grad(second_other, active_other)
    down_plane = scatter_plane(grad_down.astype(half)).astype(half)
    grad_down = lax.psum_scatter(down_plane, "row", scatter_dimension=0, tiled=True).astype(f32)

    middle_grad = second_grad + (middle_grad_own + middle_swapped.astype(f32))
    inner_gain_grad = jnp.sum(middle_grad * inner_normed, axis=0)
    inner_shift_grad = jnp.sum(middle_grad, axis=0)
    summed_grad = whole_norm_back(middle_grad, inner_normed, inner_scaling, inner_gain)
    summed_half = summed_grad.astype(half)
    mixture_grad = dot(summed_half, full_out).astype(half)
    mixture_grad = mixture_grad.reshape(row_count, n_row, width).transpose(1, 0, 2)
    mixture_grad = lax.all_to_all(mixture_grad, "row", 0, 0, tiled=True).reshape(length, width)

    grad_up = weight_grad(middle_own, active_grad_own) + weight_grad(
        middle_other, active_grad_other
    )
    kept, passed = own_columns(
        jnp.einsum("qd,eq->de", summed_half, mixture_t, preferred_element_type=f32)
    )
    grad_out = kept + swap(passed.astype(half)).astype(f32)
    out_up_plane = scatter_plane(jnp.concatenate([grad_out, grad_up], axis=1).astype(half))
    out_up_grad = lax.psum_scatter(
        out_up_plane.astype(half), "row", scatter_dimension=0, tiled=True
    ).astype(f32)
    grad_out, grad_up = out_up_grad[:, :half_width], out_up_grad[:, half_width:]

    query_grad, key_grad, value_grad = attend_back(
        qkv,
        qkv_t,
        labels,
        ranges,
        wide_labels,
        row_count,
        out_t,
        log_total,
        mixture_grad,
        mixture_grad.T,
    )
    qkv_grad = jnp.concatenate([query_grad, key_grad, value_grad], axis=1)
    back = jnp.einsum("le,de->ld", qkv_grad, w_qkv, preferred_element_type=f32)
    back = lax.psum_scatter(back.astype(half), "row", scatter_dimension=0, tiled=True)

    grads = jnp.einsum("ld,le->de", series, qkv_grad, preferred_element_type=f32)
    grads = grads.reshape(4, n_row, 2, split, 3 * width)
    kept, passed = pick(grads, core, 2), pick(grads, 1 - core, 2).astype(half)
    grads = kept + swap(passed).astype(f32)
    total = pick(grads, me)
    for bit in range(1, 4):
        total = total + flip(pick(grads, me ^ bit).astype(half), "dp", bit).astype(f32)
    strip = lax.all_to_all(total.astype(half), "row", 0, 0, tiled=True)
    strip = strip.reshape(n_row, split, 3, width).transpose(2, 1, 0, 3).reshape(3, split, 2, -1)
    kept, passed = pick(strip, core, 2), pick(strip, 1 - core, 2)
    qkv_grads = join(kept, swap(passed), 1).astype(f32)

    kept, passed = own_columns(summed_grad + back.astype(f32))
    input_grad = join(kept[None], swap(passed)[None], 0)

    norm_local = jnp.stack([inner_gain_grad, inner_shift_grad, outer_gain_grad, outer_shift_grad])
    kept, passed = own_columns(norm_local)
    norm_grads = kept + swap(passed)
    for axis in ("dp", "row"):
        for bit in (1, 2):
            norm_grads = norm_grads + flip(norm_grads, axis, bit)
    return (
        layer_out,
        input_grad,
        qkv_grads[0],
        qkv_grads[1],
        qkv_grads[2],
        grad_out,
        grad_up,
        grad_down,
        norm_grads,
    )


def solution(mesh):
    placed = (
        P("dp", "row", "col"),
        P("dp", None),
        P(("dp", "row"), "col"),
        P(("dp", "row"), "col"),
        P(("dp", "row"), "col"),
        P(("dp", "row"), "col"),
        P(("dp", "row"), "col"),
        P(("dp", "row"), "col"),
        P("col"),
        P("col"),
        P("col"),
        P("col"),
        P("dp", "row", "col"),
    )
    body = fast_local if fits(mesh) else local
    return jax.shard_map(
        body,
        mesh=mesh,
        in_specs=placed,
        out_specs=(
            P("dp", "row", "col"),
            P("dp", "row", "col"),
            P(("dp", "row"), "col"),
            P(("dp", "row"), "col"),
            P(("dp", "row"), "col"),
            P(("dp", "row"), "col"),
            P(("dp", "row"), "col"),
            P(("dp", "row"), "col"),
            P(None, "col"),
        ),
        check_vma=False,
    )
```

```python
import jax
import jax.numpy as jnp
from jax import lax
from jax.experimental import pallas as pl
from jax.experimental.pallas import tpu as pltpu
from jax.sharding import PartitionSpec as P

D = 1024
HEAD_DIM = 64


EPS = 1e-05
ROOT_HALF = 0.7071067811865476
INV_ROOT_TAU = 0.3989422804014327


def gelu_value(inputs):
    return 0.5 * inputs * (1.0 + lax.erf(inputs * ROOT_HALF))


def gelu_slope(inputs):
    return (
        0.5 * (1.0 + lax.erf(inputs * ROOT_HALF))
        + inputs * jnp.exp(-0.5 * inputs * inputs) * INV_ROOT_TAU
    )


def widen(values):
    return lax.all_gather(values, "col", axis=2, tiled=True)


def narrow(partial_value):
    return lax.psum_scatter(partial_value, "col", scatter_dimension=2, tiled=True)


def norm_forward(summed, norm_gain, norm_shift):
    row_sums, squares = lax.psum(
        (jnp.sum(summed, axis=-1, keepdims=True), jnp.sum(summed * summed, axis=-1, keepdims=True)),
        "col",
    )
    average = row_sums / D
    spread = squares / D - average * average
    scaling = lax.rsqrt(spread + EPS)
    normed = (summed - average) * scaling
    return (normed * norm_gain + norm_shift, normed, scaling)


def norm_backward(upstream, normed, scaling, norm_gain):
    scaled = upstream * norm_gain
    offset_sum, slope_sum = lax.psum(
        (jnp.sum(scaled, axis=-1, keepdims=True), jnp.sum(scaled * normed, axis=-1, keepdims=True)),
        "col",
    )
    return scaling * (scaled - offset_sum / D - normed * (slope_sum / D))


def head_view(values):
    return values.reshape(values.shape[0], values.shape[1] // HEAD_DIM, HEAD_DIM)


def masked_scores(queries, key_rows, own_labels, all_labels):
    scores = jnp.einsum(
        "qhe,khe->hqk", head_view(queries), head_view(key_rows), preferred_element_type=jnp.float32
    ) * HEAD_DIM ** (-0.5)
    inside = own_labels[:, None] == all_labels[None, :]
    return jnp.where(inside[None], scores, -jnp.inf)


def attend_forward(inputs):
    queries, key_rows, value_rows, own_labels, all_labels = inputs
    scores = masked_scores(queries, key_rows, own_labels, all_labels)
    highest = jnp.max(scores, axis=-1, keepdims=True)
    log_total = highest + jnp.log(jnp.sum(jnp.exp(scores - highest), axis=-1, keepdims=True))
    attention = jnp.exp(scores - log_total).astype(jnp.bfloat16)
    mixture = jnp.einsum(
        "hqk,khe->qhe", attention, head_view(value_rows), preferred_element_type=jnp.float32
    )
    return (mixture.reshape(queries.shape).astype(jnp.bfloat16), log_total)


def attend_backward(inputs):
    queries, key_rows, value_rows, own_labels, all_labels, log_total, mixture_grad = inputs
    scores = masked_scores(queries, key_rows, own_labels, all_labels)
    chance = jnp.exp(scores - log_total)
    attention = chance.astype(jnp.bfloat16)
    chance_grad = jnp.einsum(
        "qhe,khe->hqk",
        head_view(mixture_grad),
        head_view(value_rows),
        preferred_element_type=jnp.float32,
    )
    within = jnp.sum(chance * chance_grad, axis=-1, keepdims=True)
    score_grad = (chance * (chance_grad - within) * HEAD_DIM ** (-0.5)).astype(jnp.bfloat16)
    query_grad = jnp.einsum(
        "hqk,khe->qhe", score_grad, head_view(key_rows), preferred_element_type=jnp.float32
    )
    key_part = jnp.einsum(
        "hqk,qhe->khe", score_grad, head_view(queries), preferred_element_type=jnp.float32
    )
    value_part = jnp.einsum(
        "hqk,qhe->khe", attention, head_view(mixture_grad), preferred_element_type=jnp.float32
    )
    return (
        query_grad.reshape(queries.shape).astype(jnp.bfloat16),
        key_part.reshape(key_rows.shape),
        value_part.reshape(value_rows.shape),
    )


def local(
    tokens,
    segment,
    w_query,
    w_key,
    w_value,
    w_out,
    w_up,
    w_down,
    inner_gain,
    inner_shift,
    outer_gain,
    outer_shift,
    cotangent,
):
    f32 = jnp.float32
    half = jnp.bfloat16
    gathered = (
        lax.all_gather(w_query, ("dp", "row"), axis=0, tiled=True),
        lax.all_gather(w_key, ("dp", "row"), axis=0, tiled=True),
        lax.all_gather(w_value, ("dp", "row"), axis=0, tiled=True),
        lax.all_gather(w_out, ("dp", "row"), axis=0, tiled=True),
        lax.all_gather(w_up, ("dp", "row"), axis=0, tiled=True),
        lax.all_gather(w_down, ("dp", "row"), axis=0, tiled=True),
    )
    full_query, full_key, full_value, full_out, full_up, full_down = gathered
    row_count = tokens.shape[1]
    own_labels = lax.dynamic_slice_in_dim(segment, lax.axis_index("row") * row_count, row_count, 1)
    wide_tokens = widen(tokens)
    queries = jnp.einsum("sqd,de->sqe", wide_tokens, full_query, preferred_element_type=f32).astype(
        half
    )
    key_rows = jnp.einsum("sqd,de->sqe", wide_tokens, full_key, preferred_element_type=f32).astype(
        half
    )
    value_rows = jnp.einsum(
        "sqd,de->sqe", wide_tokens, full_value, preferred_element_type=f32
    ).astype(half)
    all_keys, all_values = (
        lax.all_gather(key_rows, "row", axis=1, tiled=True),
        lax.all_gather(value_rows, "row", axis=1, tiled=True),
    )
    mixture, log_total = lax.map(
        attend_forward, (queries, all_keys, all_values, own_labels, segment)
    )
    summed = tokens.astype(f32) + narrow(
        jnp.einsum("sqe,de->sqd", mixture, full_out, preferred_element_type=f32)
    )
    middle, inner_normed, inner_scaling = norm_forward(summed, inner_gain, inner_shift)
    wide_middle = widen(middle.astype(half))
    hidden = jnp.einsum("sqd,df->sqf", wide_middle, full_up, preferred_element_type=f32)
    active = gelu_value(hidden).astype(half)
    second_sum = middle + narrow(
        jnp.einsum("sqf,df->sqd", active, full_down, preferred_element_type=f32)
    )
    result, outer_normed, outer_scaling = norm_forward(second_sum, outer_gain, outer_shift)
    layer_out = result.astype(half)
    outer_gain_grad = jnp.sum(cotangent * outer_normed, axis=(0, 1))
    outer_shift_grad = jnp.sum(cotangent, axis=(0, 1))
    second_grad = norm_backward(cotangent, outer_normed, outer_scaling, outer_gain)
    wide_second = widen(second_grad.astype(half))
    grad_down = jnp.einsum("sqd,sqf->df", wide_second, active, preferred_element_type=f32)
    active_grad = (
        jnp.einsum("sqd,df->sqf", wide_second, full_down, preferred_element_type=f32)
        * gelu_slope(hidden)
    ).astype(half)
    grad_up = jnp.einsum("sqd,sqf->df", wide_middle, active_grad, preferred_element_type=f32)
    middle_grad = second_grad + narrow(
        jnp.einsum("sqf,df->sqd", active_grad, full_up, preferred_element_type=f32)
    )
    inner_gain_grad = jnp.sum(middle_grad * inner_normed, axis=(0, 1))
    inner_shift_grad = jnp.sum(middle_grad, axis=(0, 1))
    summed_grad = norm_backward(middle_grad, inner_normed, inner_scaling, inner_gain)
    wide_summed = widen(summed_grad.astype(half))
    grad_out = jnp.einsum("sqd,sqe->de", wide_summed, mixture, preferred_element_type=f32)
    mixture_grad = jnp.einsum(
        "sqd,de->sqe", wide_summed, full_out, preferred_element_type=f32
    ).astype(half)
    query_grad, key_part, value_part = lax.map(
        attend_backward,
        (queries, all_keys, all_values, own_labels, segment, log_total, mixture_grad),
    )
    key_sums, value_sums = (
        lax.psum_scatter(key_part, "row", scatter_dimension=1, tiled=True),
        lax.psum_scatter(value_part, "row", scatter_dimension=1, tiled=True),
    )
    key_grad = key_sums.astype(half)
    value_grad = value_sums.astype(half)
    grad_query = jnp.einsum("sqd,sqe->de", wide_tokens, query_grad, preferred_element_type=f32)
    grad_key = jnp.einsum("sqd,sqe->de", wide_tokens, key_grad, preferred_element_type=f32)
    grad_value = jnp.einsum("sqd,sqe->de", wide_tokens, value_grad, preferred_element_type=f32)
    back_sum = jnp.einsum("sqe,de->sqd", query_grad, full_query, preferred_element_type=f32)
    back_sum = back_sum + jnp.einsum("sqe,de->sqd", key_grad, full_key, preferred_element_type=f32)
    back_sum = back_sum + jnp.einsum(
        "sqe,de->sqd", value_grad, full_value, preferred_element_type=f32
    )
    input_grad = summed_grad + narrow(back_sum)
    norm_local = jnp.stack([inner_gain_grad, inner_shift_grad, outer_gain_grad, outer_shift_grad])
    weight_grads = (
        lax.psum_scatter(grad_query, ("dp", "row"), scatter_dimension=0, tiled=True),
        lax.psum_scatter(grad_key, ("dp", "row"), scatter_dimension=0, tiled=True),
        lax.psum_scatter(grad_value, ("dp", "row"), scatter_dimension=0, tiled=True),
        lax.psum_scatter(grad_out, ("dp", "row"), scatter_dimension=0, tiled=True),
        lax.psum_scatter(grad_up, ("dp", "row"), scatter_dimension=0, tiled=True),
        lax.psum_scatter(grad_down, ("dp", "row"), scatter_dimension=0, tiled=True),
    )
    norm_grads = lax.psum(norm_local, ("dp", "row"))
    return (
        layer_out,
        input_grad,
        weight_grads[0],
        weight_grads[1],
        weight_grads[2],
        weight_grads[3],
        weight_grads[4],
        weight_grads[5],
        norm_grads,
    )


PAIR = 128
BLOCK = 256
NEG = -1e30
HEADS = 16
SCALE = HEAD_DIM ** (-0.5)
VMEM_LIMIT = 48 << 20


def fits(mesh):
    sizes = dict(mesh.shape)
    return sizes["col"] == 2 and sizes["dp"] == 4 and sizes["row"] == 4


def head_mask(values, head):
    lane = lax.broadcasted_iota(jnp.int32, values.shape, 1)
    keep = (lane < HEAD_DIM) if head == 0 else (lane >= HEAD_DIM)
    return jnp.where(keep, values, jnp.zeros_like(values))


def dot(left, right):
    return jnp.dot(left, right, preferred_element_type=jnp.float32)


def forward_kernel(low, high, twist, q_t, k, v_t, own, others, *refs):
    out_t, log_total = refs[-2:]
    step = pl.program_id(0)
    queries = q_t[...]
    own_labels = own[...]
    inner = out_t.shape[2]
    per = k.shape[0] // 4 // BLOCK

    def body(j, carry):
        place = pl.multiple_of(j * BLOCK, BLOCK)
        start = pl.multiple_of((((j // per) ^ twist[0]) * per + j % per) * BLOCK, BLOCK)
        keys = k[pl.ds(start, BLOCK), :]
        labels = others[pl.ds(place, BLOCK), :]
        inside = jnp.concatenate([labels] * (BLOCK // PAIR), axis=1) == own_labels
        state = []
        for head in range(2):
            highest, total, mixed = carry[head]
            scores = jnp.where(inside, dot(head_mask(keys, head), queries), NEG)
            fresh = jnp.maximum(highest, jnp.max(scores, axis=0, keepdims=True))
            chance = jnp.exp(scores - fresh)
            fade = jnp.exp(highest - fresh)
            values = v_t[head * HEAD_DIM : (head + 1) * HEAD_DIM, pl.ds(start, BLOCK)]
            state.append(
                (
                    fresh,
                    total * fade + jnp.sum(chance, axis=0, keepdims=True),
                    mixed * fade + dot(values, chance.astype(jnp.bfloat16)),
                )
            )
        return tuple(state)

    one = (
        jnp.full((1, inner), NEG, jnp.float32),
        jnp.zeros((1, inner), jnp.float32),
        jnp.zeros((HEAD_DIM, inner), jnp.float32),
    )
    final = lax.fori_loop(low[step], high[step], body, (one, one))
    for head in range(2):
        highest, total, mixed = final[head]
        out_t[0, head * HEAD_DIM : (head + 1) * HEAD_DIM, :] = (mixed / total).astype(jnp.bfloat16)
        log_total[head : head + 1, :] = highest + jnp.log(total)


def backward_kernel(
    low,
    high,
    twist,
    q,
    q_t,
    g,
    g_t,
    out_t,
    log_total,
    k,
    v,
    k_t,
    own,
    others,
    *refs,
):
    result, dk_sum, dv_sum = refs[-3:]
    step = pl.program_id(0)
    per = k.shape[0] // 4 // BLOCK

    @pl.when(step == 0)
    def _():
        dk_sum[...] = jnp.zeros_like(dk_sum)
        dv_sum[...] = jnp.zeros_like(dv_sum)

    half = jnp.bfloat16
    queries_t = q_t[...]
    grads_t = g_t[0]
    own_labels = own[...]
    product = grads_t.astype(jnp.float32) * out_t[0].astype(jnp.float32)
    heads = []
    for head in range(2):
        rows = slice(head * HEAD_DIM, (head + 1) * HEAD_DIM)
        heads.append(
            (
                head_mask(q[...], head),
                head_mask(g[...], head),
                jnp.sum(product[rows], axis=0, keepdims=True),
                log_total[head : head + 1, :],
            )
        )

    def body(j, carry):
        place = pl.multiple_of(j * BLOCK, BLOCK)
        start = pl.multiple_of((((j // per) ^ twist[0]) * per + j % per) * BLOCK, BLOCK)
        keys = k[pl.ds(start, BLOCK), :]
        values = v[pl.ds(start, BLOCK), :]
        labels = others[pl.ds(place, BLOCK), :]
        inside = jnp.concatenate([labels] * (BLOCK // PAIR), axis=1) == own_labels
        sums, key_part, value_part = [], None, None
        for head in range(2):
            own_q, own_g, within, total = heads[head]
            scores = dot(head_mask(keys, head), queries_t)
            chance = jnp.where(inside, jnp.exp(scores - total), 0.0)
            chance_grad = dot(head_mask(values, head), grads_t)
            score_grad = (chance * (chance_grad - within)).astype(half)
            value_new = dot(chance.astype(half), own_g)
            key_new = dot(score_grad, own_q)
            keys_t = k_t[head * HEAD_DIM : (head + 1) * HEAD_DIM, pl.ds(start, BLOCK)]
            sums.append(carry[head] + dot(keys_t, score_grad))
            key_part = key_new if key_part is None else key_part + key_new
            value_part = value_new if value_part is None else value_part + value_new
        dk_sum[pl.ds(start, BLOCK), :] += key_part
        dv_sum[pl.ds(start, BLOCK), :] += value_part
        return tuple(sums)

    zero = jnp.zeros((HEAD_DIM, own_labels.shape[1]), jnp.float32)
    first, second = lax.fori_loop(low[step], high[step], body, (zero, zero))
    both = jnp.concatenate([first, second], axis=0) * SCALE
    held = pl.multiple_of((((step // per) ^ twist[0]) * per + step % per) * BLOCK, BLOCK)
    result[pl.ds(held, BLOCK), :PAIR] = jnp.transpose(both).astype(half)

    @pl.when(step == pl.num_programs(0) - 1)
    def _():
        result[:, PAIR : 2 * PAIR] = dk_sum[...].astype(half)
        result[:, 2 * PAIR :] = dv_sum[...].astype(half)


def key_ranges(labels):
    blocks = labels.reshape(-1, BLOCK)
    first, last = blocks[:, :1], blocks[:, -1:]
    before = jnp.sum((labels[None, :] < first).astype(jnp.int32), axis=1)
    upto = jnp.sum((labels[None, :] <= last).astype(jnp.int32), axis=1)
    return before // BLOCK, (upto + BLOCK - 1) // BLOCK


def attend(pair, qkv, qkv_t, labels, wide_labels, scalars, before=()):
    length, width = qkv.shape
    pairs = width // 3 // PAIR
    row_count = length // 4
    inner = row_count // BLOCK

    def held(i, twist):
        return ((i // inner) ^ twist[0]) * inner + i % inner

    area = length * length
    return pl.pallas_call(
        forward_kernel,
        out_shape=(
            jax.ShapeDtypeStruct((4, pairs * PAIR, row_count), jnp.bfloat16),
            jax.ShapeDtypeStruct((8, length), jnp.float32),
        ),
        grid_spec=pltpu.PrefetchScalarGridSpec(
            num_scalar_prefetch=3,
            grid=(length // BLOCK,),
            in_specs=[
                pl.BlockSpec((PAIR, BLOCK), lambda i, lo, hi, tw: (3 * pair, held(i, tw))),
                pl.BlockSpec((length, PAIR), lambda i, lo, hi, tw: (0, 3 * pair + 1)),
                pl.BlockSpec((PAIR, length), lambda i, lo, hi, tw: (3 * pair + 2, 0)),
                pl.BlockSpec((1, BLOCK), lambda i, lo, hi, tw: (0, i)),
                pl.BlockSpec((length, PAIR), lambda i, lo, hi, tw: (0, 0)),
            ]
            + [pl.BlockSpec(memory_space=pl.ANY) for _ in before],
            out_specs=(
                pl.BlockSpec((1, PAIR, BLOCK), lambda i, lo, hi, tw: (i // inner, pair, i % inner)),
                pl.BlockSpec((8, BLOCK), lambda i, lo, hi, tw: (0, i)),
            ),
        ),
        input_output_aliases={8: 0} if before else {},
        compiler_params=pltpu.CompilerParams(vmem_limit_bytes=VMEM_LIMIT),
        cost_estimate=pl.CostEstimate(
            flops=area * 256 * 24, bytes_accessed=4 << 20, transcendentals=2 * area
        ),
    )(*scalars, qkv_t, qkv, qkv_t, labels, wide_labels, *before)


def attend_back(
    pair, qkv, qkv_t, labels, wide_labels, scalars, out_t, log_total, grads, grads_t, before=()
):
    length, width = grads.shape
    pairs = width // PAIR
    row_count = length // 4
    inner = row_count // BLOCK

    def held(i, twist):
        return ((i // inner) ^ twist[0]) * inner + i % inner

    area = length * length
    return pl.pallas_call(
        backward_kernel,
        out_shape=jax.ShapeDtypeStruct(qkv.shape, jnp.bfloat16),
        grid_spec=pltpu.PrefetchScalarGridSpec(
            num_scalar_prefetch=3,
            grid=(length // BLOCK,),
            in_specs=[
                pl.BlockSpec((BLOCK, PAIR), lambda i, lo, hi, tw: (held(i, tw), 3 * pair)),
                pl.BlockSpec((PAIR, BLOCK), lambda i, lo, hi, tw: (3 * pair, held(i, tw))),
                pl.BlockSpec((BLOCK, PAIR), lambda i, lo, hi, tw: (i, pair)),
                pl.BlockSpec((1, PAIR, BLOCK), lambda i, lo, hi, tw: (i // inner, pair, i % inner)),
                pl.BlockSpec((1, PAIR, BLOCK), lambda i, lo, hi, tw: (i // inner, pair, i % inner)),
                pl.BlockSpec((8, BLOCK), lambda i, lo, hi, tw: (0, i)),
                pl.BlockSpec((length, PAIR), lambda i, lo, hi, tw: (0, 3 * pair + 1)),
                pl.BlockSpec((length, PAIR), lambda i, lo, hi, tw: (0, 3 * pair + 2)),
                pl.BlockSpec((PAIR, length), lambda i, lo, hi, tw: (3 * pair + 1, 0)),
                pl.BlockSpec((1, BLOCK), lambda i, lo, hi, tw: (0, i)),
                pl.BlockSpec((length, PAIR), lambda i, lo, hi, tw: (0, 0)),
            ]
            + [pl.BlockSpec(memory_space=pl.ANY) for _ in before],
            out_specs=pl.BlockSpec((length, 3 * PAIR), lambda i, lo, hi, tw: (0, pair)),
            scratch_shapes=[
                pltpu.VMEM((length, PAIR), jnp.float32),
                pltpu.VMEM((length, PAIR), jnp.float32),
            ],
        ),
        input_output_aliases={14: 0} if before else {},
        compiler_params=pltpu.CompilerParams(vmem_limit_bytes=VMEM_LIMIT),
        cost_estimate=pl.CostEstimate(
            flops=area * 256 * 24, bytes_accessed=6 << 20, transcendentals=2 * area
        ),
    )(
        *scalars,
        qkv,
        qkv_t,
        grads,
        grads_t,
        out_t,
        log_total,
        qkv,
        qkv,
        qkv_t,
        labels,
        wide_labels,
        *before,
    )


def assemble(pieces, shapes, moves):
    count = len(shapes)

    def kernel(*refs):
        sources, rest = refs[: len(pieces)], refs[len(pieces) :]
        outs, held, arrived, left = rest[:count], rest[count : 2 * count], rest[-2], rest[-1]
        inward, outward = [], []
        for n, (piece, rows, columns, out, row, column) in enumerate(moves):
            at = (pl.ds(row, rows[1] - rows[0]), pl.ds(column, columns[1] - columns[0]))
            source = sources[piece].at[rows[0] : rows[1], columns[0] : columns[1]]
            inward.append(pltpu.make_async_copy(source, held[out].at[at], arrived.at[n]))
            outward.append(pltpu.make_async_copy(held[out].at[at], outs[out].at[at], left.at[n]))
        for copy in inward:
            copy.start()
        for copy, onward in zip(inward, outward):
            copy.wait()
            onward.start()
        for copy in outward:
            copy.wait()

    any_space = pl.BlockSpec(memory_space=pl.ANY)
    total = sum(2 * a * b for a, b in shapes)
    return pl.pallas_call(
        kernel,
        out_shape=tuple(jax.ShapeDtypeStruct(shape, jnp.bfloat16) for shape in shapes),
        in_specs=[any_space] * len(pieces),
        out_specs=(any_space,) * len(shapes),
        scratch_shapes=[pltpu.VMEM(shape, jnp.bfloat16) for shape in shapes]
        + [pltpu.SemaphoreType.DMA((len(moves),))] * 2,
        compiler_params=pltpu.CompilerParams(vmem_limit_bytes=16 << 20),
        cost_estimate=pl.CostEstimate(flops=0, bytes_accessed=2 * total, transcendentals=0),
    )(*pieces)


def swap(values):
    return lax.ppermute(values, "col", [(0, 1), (1, 0)])


def flip(values, axis, bit, size=4):
    return lax.ppermute(values, axis, [(i, i ^ bit) for i in range(size)])


def pick(values, index, axis=0):
    return lax.dynamic_index_in_dim(values, index, axis, keepdims=False)


def together(*values):
    return lax.optimization_barrier(values)


def gather_start(block):
    rows = block.shape[0] // 2
    top, low = block[:rows], block[rows:]
    return top, low, flip(top, "dp", 1), flip(low, "dp", 2)


def gather_second(state):
    top, low, top_x, low_y = state
    top_y = flip(jnp.concatenate([top, top_x]), "dp", 2)
    low_x = flip(jnp.concatenate([low, low_y]), "dp", 1)
    return top_y, low_x


def gather_end(state, second, parts):
    pieces = (*state, *second)
    rows = pieces[0].shape[0]
    whole, head, tail = (0, rows), (0, rows), (rows, 2 * rows)
    order = ((0, whole), (1, whole), (2, whole), (5, head), (4, head), (3, whole), (4, tail), (5, tail))
    moves = [
        (piece, span, part, n, place * rows, 0)
        for place, (piece, span) in enumerate(order)
        for n, part in enumerate(parts)
    ]
    return assemble(pieces, [(8 * rows, stop - start) for start, stop in parts], moves)


def scatter_start(*grads):
    rows = grads[0].shape[0] // 8

    def part(block, second):
        at = (2 * block + second) * rows
        return jnp.concatenate([array[at : at + rows] for array in grads], axis=1)

    top_y = flip(jnp.concatenate([part(2, 0), part(3, 0)]), "dp", 2)
    low_x = flip(jnp.concatenate([part(1, 1), part(3, 1)]), "dp", 1)
    return part(0, 0), part(1, 0), part(0, 1), part(2, 1), top_y, low_x


def scatter_second(state):
    f32, half = jnp.float32, jnp.bfloat16
    top, top_pass, low, low_pass, top_y, low_x = state
    rows = top.shape[0]
    top_x = flip((top_pass.astype(f32) + top_y[rows:].astype(f32)).astype(half), "dp", 1)
    low_y = flip((low_pass.astype(f32) + low_x[rows:].astype(f32)).astype(half), "dp", 2)
    return top_x, low_y


def scatter_end(state, second):
    f32, half = jnp.float32, jnp.bfloat16
    top, _, low, _, top_y, low_x = state
    top_x, low_y = second
    rows = top.shape[0]
    top = top.astype(f32) + top_y[:rows].astype(f32) + top_x.astype(f32)
    low = low.astype(f32) + low_x[:rows].astype(f32) + low_y.astype(f32)
    return jnp.concatenate([top, low]).astype(half)


def whole_norm(summed, gain, shift):
    average = jnp.mean(summed, axis=-1, keepdims=True)
    spread = jnp.mean(summed * summed, axis=-1, keepdims=True) - average * average
    scaling = lax.rsqrt(spread + EPS)
    normed = (summed - average) * scaling
    return (normed * gain + shift, normed, scaling)


def whole_norm_back(upstream, normed, scaling, gain):
    scaled = upstream * gain
    offset = jnp.mean(scaled, axis=-1, keepdims=True)
    slope = jnp.mean(scaled * normed, axis=-1, keepdims=True)
    return scaling * (scaled - offset - normed * slope)


def fast_local(
    tokens,
    segment,
    w_query,
    w_key,
    w_value,
    w_out,
    w_up,
    w_down,
    inner_gain,
    inner_shift,
    outer_gain,
    outer_shift,
    cotangent,
):
    f32 = jnp.float32
    half = jnp.bfloat16
    me = lax.axis_index("dp")
    core = lax.axis_index("col")
    row = lax.axis_index("row")
    which, parity = row // 2, row % 2
    first_core = core == 0
    crossed = me % 2 == 1
    leading = core == me // 2
    row_count = tokens.shape[1]
    length = segment.shape[1]
    block_rows, half_width = w_query.shape
    width = D // 4
    hidden_half = w_up.shape[1]
    stack, cat = jnp.stack, jnp.concatenate

    def turn(values):
        left, right = values[..., :width], values[..., width:]
        return jnp.where(crossed, cat([right, left], axis=-1), values)

    def merge(mine, other):
        return jnp.where(leading, cat([mine, other], axis=-1), cat([other, mine], axis=-1))

    def divide(values):
        left, right = values[..., :half_width], values[..., half_width:]
        return jnp.where(leading, left, right), jnp.where(leading, right, left)

    def by_core(mine, other):
        return jnp.where(first_core, stack([mine, other]), stack([other, mine]))

    tokens = turn(tokens)
    near_0 = pick(tokens, which)
    near_2 = flip(pick(tokens, 1 - which), "row", 2)
    near_1 = flip(near_0, "row", 1)
    near_3 = flip(near_2, "row", 1)
    pieces = [near_0, near_1, near_2, near_3]
    pieces += [swap(piece) for piece in pieces]
    whole = (0, row_count), (0, half_width)
    (series,) = assemble(
        pieces,
        [(length, D)],
        [(n, *whole, 0, n % 4 * row_count, n // 4 * half_width) for n in range(8)],
    )
    own_tokens = merge(pick(tokens, core), swap(pick(tokens, 1 - core)))
    labels = pick(segment, which)
    scalars = (*key_ranges(labels), row.reshape(1))
    wide_labels = jnp.broadcast_to(labels[:, None], (length, PAIR))
    labels = labels[None]

    thirds = stack([w_query, w_key, w_value]).reshape(3, block_rows, 2, width)
    blocks = by_core(pick(thirds, core, 2), swap(pick(thirds, 1 - core, 2)))
    same, cross = pick(blocks, parity), pick(blocks, 1 - parity)
    near = [same] + [flip(same if bit == 2 else cross, "row", bit) for bit in (1, 2, 3)]
    odd = row % 2 == 1
    lower = jnp.where(odd, stack([near[1], near[0]]), stack([near[0], near[1]]))
    upper = jnp.where(odd, stack([near[3], near[2]]), stack([near[2], near[3]]))
    strips = jnp.where(row >= 2, cat([upper, lower]), cat([lower, upper]))
    planes = [strips] + [flip(strips, "dp", bit) for bit in (1, 2, 3)]

    def rows_of(first, second):
        rows = stack([first, second]).reshape(2, 4, 3, block_rows, width // PAIR, PAIR)
        return rows.transpose(0, 1, 3, 4, 2, 5).reshape(half_width, 3 * width)

    head_rows, tail_rows = rows_of(*planes[:2]), rows_of(*planes[2:])
    w_mine = jnp.where(leading, head_rows, tail_rows)
    w_other = jnp.where(leading, tail_rows, head_rows)
    exact_scale = jnp.where(jnp.arange(3 * width) % (3 * PAIR) < PAIR, SCALE, 1.0).astype(half)
    w_qkv = cat([w_mine, w_other])

    packed, plain_down, _, _ = together(cat([w_out, w_up], axis=1), w_down, near_3, strips)
    out_up_rows = lax.all_gather(packed, "row", axis=0, tiled=True)
    down_rows = lax.all_gather(plain_down, "row", axis=0, tiled=True)

    vectors = turn(stack([inner_gain, inner_shift, outer_gain, outer_shift]))
    vectors = merge(vectors, swap(vectors))
    inner_gain, inner_shift, outer_gain, outer_shift = (vectors[i : i + 1] for i in range(4))
    cotangent = turn(cotangent)
    upstream = merge(pick(cotangent, core), swap(pick(cotangent, 1 - core)))

    qkv = dot(series, w_qkv * exact_scale).astype(half)
    qkv_t = qkv.T
    out_0, total_0 = attend(0, qkv, qkv_t, labels, wide_labels, scalars)
    out_t, total_1 = attend(1, qkv, qkv_t, labels, wide_labels, scalars, (out_0,))
    out_up = gather_start(out_up_rows)
    out_up_second = gather_second(out_up)
    down_first = gather_start(down_rows)
    out_half, up = gather_end(
        out_up, out_up_second, ((0, half_width), (half_width, half_width + hidden_half))
    )
    full_out = cat([out_half, swap(out_half)], axis=1)
    (down,) = gather_end(down_first, gather_second(down_first), ((0, hidden_half),))
    mixed = lax.all_to_all(out_t, "row", 0, 0, tiled=True)
    mixed = mixed.reshape(2, 2, width, row_count)
    kept, passed = pick(mixed, core), swap(pick(mixed, 1 - core))
    mixture_t = jnp.where(
        first_core,
        cat([kept[0], passed[0], kept[1], passed[1]]),
        cat([passed[1], kept[1], passed[0], kept[0]]),
    )

    summed = own_tokens.astype(f32) + jnp.einsum(
        "eq,de->qd", mixture_t, full_out, preferred_element_type=f32
    )
    middle, inner_normed, inner_scaling = whole_norm(summed, inner_gain, inner_shift)

    middle_own = middle.astype(half)
    middle_other = swap(middle_own)
    hidden_own = dot(middle_own, up)
    hidden_other = dot(middle_other, up)
    active_own = gelu_value(hidden_own).astype(half)
    active_other = gelu_value(hidden_other).astype(half)
    down_other = jnp.einsum("qf,df->qd", active_other, down, preferred_element_type=f32)
    down_swapped = swap(down_other.astype(half))
    down_own = jnp.einsum("qf,df->qd", active_own, down, preferred_element_type=f32)
    second_sum = middle + (down_own + down_swapped.astype(f32))
    result, outer_normed, outer_scaling = whole_norm(second_sum, outer_gain, outer_shift)
    kept, passed = divide(result.astype(half))
    layer_out = turn(by_core(kept, swap(passed)))

    outer_gain_grad = jnp.sum(upstream * outer_normed, axis=0)
    outer_shift_grad = jnp.sum(upstream, axis=0)
    second_grad = whole_norm_back(upstream, outer_normed, outer_scaling, outer_gain)
    second_own = second_grad.astype(half)
    second_other = swap(second_own)

    def weight_grad(left, right):
        return jnp.einsum("qd,qf->df", left, right, preferred_element_type=f32)

    grad_down = weight_grad(second_own, active_own) + weight_grad(second_other, active_other)
    down_first = scatter_start(grad_down.astype(half))
    active_grad_own = (dot(second_own, down) * gelu_slope(hidden_own)).astype(half)
    active_grad_other = (dot(second_other, down) * gelu_slope(hidden_other)).astype(half)
    middle_grad_other = jnp.einsum("qf,df->qd", active_grad_other, up, preferred_element_type=f32)
    middle_swapped = swap(middle_grad_other.astype(half))
    middle_grad_own = jnp.einsum("qf,df->qd", active_grad_own, up, preferred_element_type=f32)

    middle_grad = second_grad + (middle_grad_own + middle_swapped.astype(f32))
    inner_gain_grad = jnp.sum(middle_grad * inner_normed, axis=0)
    inner_shift_grad = jnp.sum(middle_grad, axis=0)
    summed_grad = whole_norm_back(middle_grad, inner_normed, inner_scaling, inner_gain)
    summed_half = summed_grad.astype(half)
    grads_t = jnp.einsum("qd,de->eq", summed_half, full_out, preferred_element_type=f32)
    grads_t = grads_t.astype(half).reshape(4, width, row_count)
    kept = jnp.where(
        first_core, stack([grads_t[0], grads_t[2]]), stack([grads_t[3], grads_t[1]])
    )
    passed = jnp.where(
        first_core, stack([grads_t[1], grads_t[3]]), stack([grads_t[2], grads_t[0]])
    )
    grads_t = by_core(kept, swap(passed)).reshape(4, width, row_count)
    grads_t = lax.all_to_all(grads_t, "row", 0, 0, tiled=True)

    grad_up = weight_grad(middle_own, active_grad_own) + weight_grad(
        middle_other, active_grad_other
    )
    grad_out = jnp.einsum("qd,eq->de", summed_half, mixture_t, preferred_element_type=f32)
    grad_out = grad_out[:, :half_width] + swap(grad_out[:, half_width:].astype(half)).astype(f32)
    out_up_first = scatter_start(grad_out.astype(half), grad_up.astype(half))
    grads_t, down_first = together(grads_t, down_first)
    grads = grads_t.transpose(0, 2, 1).reshape(length, width)
    qkv_grad = attend_back(
        0, qkv, qkv_t, labels, wide_labels, scalars, out_t, total_0, grads, grads_t
    )
    down_second = scatter_second(down_first)
    scalars_1, down_second, out_up_first, qkv_grad = together(
        scalars, down_second, out_up_first, qkv_grad
    )
    grad_down = lax.psum_scatter(
        scatter_end(down_first, down_second), "row", scatter_dimension=0, tiled=True
    )
    qkv_grad = attend_back(
        1, qkv, qkv_t, labels, wide_labels, scalars_1, out_t, total_1, grads, grads_t, (qkv_grad,)
    )
    out_up_second = scatter_second(out_up_first)
    out_up_plane = scatter_end(out_up_first, out_up_second)
    qkv_grad, grad_down, out_up_plane = together(qkv_grad, grad_down, out_up_plane)
    out_up_grad = lax.psum_scatter(out_up_plane, "row", scatter_dimension=0, tiled=True)
    grad_down = grad_down.astype(f32)

    def back_part(rows):
        return jnp.einsum("le,de->ld", qkv_grad, rows, preferred_element_type=f32)

    back_other = swap(back_part(w_other).astype(half))
    back = back_part(w_mine) + back_other.astype(f32)
    qkv_grad, back = together(qkv_grad, back)
    back = back.reshape(4, row_count, half_width)
    pass_on = back[2] + flip(back[3].astype(half), "row", 1).astype(f32)
    pass_on, out_up_grad = together(pass_on.astype(half), out_up_grad)
    out_up_grad = out_up_grad.astype(f32)
    grad_out, grad_up = out_up_grad[:, :half_width], out_up_grad[:, half_width:]
    from_far = flip(pass_on, "row", 2).astype(f32)
    from_near = back[0] + flip(back[1].astype(half), "row", 1).astype(f32)
    grads = jnp.einsum("ld,le->de", series, qkv_grad, preferred_element_type=f32)
    grads_mine, grads_other = grads[:half_width], grads[half_width:]

    def plane_part(j):
        rows = slice((j % 2) * width, (j % 2 + 1) * width)
        if j < 2:
            return jnp.where(leading, grads_mine[rows], grads_other[rows])
        return jnp.where(leading, grads_other[rows], grads_mine[rows])

    total = plane_part(0)
    for bit in range(1, 4):
        total = total + flip(plane_part(bit).astype(half), "dp", bit).astype(f32)
    total = total.reshape(4, block_rows, 3 * width)
    sent = stack([pick(total, row ^ 2), pick(total, row ^ 3)]).astype(half)
    sent, from_near = together(sent, from_near)
    sent = flip(sent, "row", 2).astype(f32)
    own_part = (pick(total, row) + sent[0]).astype(half)
    other_part = flip((pick(total, row ^ 1) + sent[1]).astype(half), "row", 1)
    strip = jnp.where(odd, stack([other_part, own_part]), stack([own_part, other_part]))
    kept, passed = pick(strip, core), swap(pick(strip, 1 - core))

    def three(values):
        values = values.reshape(block_rows, width // PAIR, 3, PAIR).transpose(2, 0, 1, 3)
        return values.reshape(3, block_rows, width)

    kept, passed = three(kept), three(passed)
    qkv_grads = jnp.where(first_core, cat([kept, passed], axis=2), cat([passed, kept], axis=2))
    qkv_grads = qkv_grads.astype(f32)

    back = jnp.where(which == 0, stack([from_near, from_far]), stack([from_far, from_near]))
    kept, passed = divide(summed_grad)
    input_grad = turn(by_core(kept, swap(passed)) + back)

    norm_local = stack([inner_gain_grad, inner_shift_grad, outer_gain_grad, outer_shift_grad])
    kept, passed = divide(norm_local)
    norm_grads = turn(kept + swap(passed))
    for axis in ("row", "dp"):
        for bit in (1, 2):
            norm_grads = norm_grads + flip(norm_grads, axis, bit)
    return (
        layer_out,
        input_grad,
        qkv_grads[0],
        qkv_grads[1],
        qkv_grads[2],
        grad_out,
        grad_up,
        grad_down,
        norm_grads,
    )


def solution(mesh):
    placed = (
        P("dp", "row", "col"),
        P("dp", None),
        P(("dp", "row"), "col"),
        P(("dp", "row"), "col"),
        P(("dp", "row"), "col"),
        P(("dp", "row"), "col"),
        P(("dp", "row"), "col"),
        P(("dp", "row"), "col"),
        P("col"),
        P("col"),
        P("col"),
        P("col"),
        P("dp", "row", "col"),
    )
    body = fast_local if fits(mesh) else local
    return jax.shard_map(
        body,
        mesh=mesh,
        in_specs=placed,
        out_specs=(
            P("dp", "row", "col"),
            P("dp", "row", "col"),
            P(("dp", "row"), "col"),
            P(("dp", "row"), "col"),
            P(("dp", "row"), "col"),
            P(("dp", "row"), "col"),
            P(("dp", "row"), "col"),
            P(("dp", "row"), "col"),
            P(None, "col"),
        ),
        check_vma=False,
    )
```

```python
import jax
import jax.numpy as jnp
from jax import lax
from jax.experimental import pallas as pl
from jax.experimental.pallas import tpu as pltpu
from jax.sharding import PartitionSpec as P

D = 1024
HEAD_DIM = 64


EPS = 1e-05
ROOT_HALF = 0.7071067811865476
INV_ROOT_TAU = 0.3989422804014327


def gelu_value(inputs):
    return 0.5 * inputs * (1.0 + lax.erf(inputs * ROOT_HALF))


def gelu_slope(inputs):
    return (
        0.5 * (1.0 + lax.erf(inputs * ROOT_HALF))
        + inputs * jnp.exp(-0.5 * inputs * inputs) * INV_ROOT_TAU
    )


def widen(values):
    return lax.all_gather(values, "col", axis=2, tiled=True)


def narrow(partial_value):
    return lax.psum_scatter(partial_value, "col", scatter_dimension=2, tiled=True)


def norm_forward(summed, norm_gain, norm_shift):
    row_sums, squares = lax.psum(
        (jnp.sum(summed, axis=-1, keepdims=True), jnp.sum(summed * summed, axis=-1, keepdims=True)),
        "col",
    )
    average = row_sums / D
    spread = squares / D - average * average
    scaling = lax.rsqrt(spread + EPS)
    normed = (summed - average) * scaling
    return (normed * norm_gain + norm_shift, normed, scaling)


def norm_backward(upstream, normed, scaling, norm_gain):
    scaled = upstream * norm_gain
    offset_sum, slope_sum = lax.psum(
        (jnp.sum(scaled, axis=-1, keepdims=True), jnp.sum(scaled * normed, axis=-1, keepdims=True)),
        "col",
    )
    return scaling * (scaled - offset_sum / D - normed * (slope_sum / D))


def head_view(values):
    return values.reshape(values.shape[0], values.shape[1] // HEAD_DIM, HEAD_DIM)


def masked_scores(queries, key_rows, own_labels, all_labels):
    scores = jnp.einsum(
        "qhe,khe->hqk", head_view(queries), head_view(key_rows), preferred_element_type=jnp.float32
    ) * HEAD_DIM ** (-0.5)
    inside = own_labels[:, None] == all_labels[None, :]
    return jnp.where(inside[None], scores, -jnp.inf)


def attend_forward(inputs):
    queries, key_rows, value_rows, own_labels, all_labels = inputs
    scores = masked_scores(queries, key_rows, own_labels, all_labels)
    highest = jnp.max(scores, axis=-1, keepdims=True)
    log_total = highest + jnp.log(jnp.sum(jnp.exp(scores - highest), axis=-1, keepdims=True))
    attention = jnp.exp(scores - log_total).astype(jnp.bfloat16)
    mixture = jnp.einsum(
        "hqk,khe->qhe", attention, head_view(value_rows), preferred_element_type=jnp.float32
    )
    return (mixture.reshape(queries.shape).astype(jnp.bfloat16), log_total)


def attend_backward(inputs):
    queries, key_rows, value_rows, own_labels, all_labels, log_total, mixture_grad = inputs
    scores = masked_scores(queries, key_rows, own_labels, all_labels)
    chance = jnp.exp(scores - log_total)
    attention = chance.astype(jnp.bfloat16)
    chance_grad = jnp.einsum(
        "qhe,khe->hqk",
        head_view(mixture_grad),
        head_view(value_rows),
        preferred_element_type=jnp.float32,
    )
    within = jnp.sum(chance * chance_grad, axis=-1, keepdims=True)
    score_grad = (chance * (chance_grad - within) * HEAD_DIM ** (-0.5)).astype(jnp.bfloat16)
    query_grad = jnp.einsum(
        "hqk,khe->qhe", score_grad, head_view(key_rows), preferred_element_type=jnp.float32
    )
    key_part = jnp.einsum(
        "hqk,qhe->khe", score_grad, head_view(queries), preferred_element_type=jnp.float32
    )
    value_part = jnp.einsum(
        "hqk,qhe->khe", attention, head_view(mixture_grad), preferred_element_type=jnp.float32
    )
    return (
        query_grad.reshape(queries.shape).astype(jnp.bfloat16),
        key_part.reshape(key_rows.shape),
        value_part.reshape(value_rows.shape),
    )


def local(
    tokens,
    segment,
    w_query,
    w_key,
    w_value,
    w_out,
    w_up,
    w_down,
    inner_gain,
    inner_shift,
    outer_gain,
    outer_shift,
    cotangent,
):
    f32 = jnp.float32
    half = jnp.bfloat16
    gathered = (
        lax.all_gather(w_query, ("dp", "row"), axis=0, tiled=True),
        lax.all_gather(w_key, ("dp", "row"), axis=0, tiled=True),
        lax.all_gather(w_value, ("dp", "row"), axis=0, tiled=True),
        lax.all_gather(w_out, ("dp", "row"), axis=0, tiled=True),
        lax.all_gather(w_up, ("dp", "row"), axis=0, tiled=True),
        lax.all_gather(w_down, ("dp", "row"), axis=0, tiled=True),
    )
    full_query, full_key, full_value, full_out, full_up, full_down = gathered
    row_count = tokens.shape[1]
    own_labels = lax.dynamic_slice_in_dim(segment, lax.axis_index("row") * row_count, row_count, 1)
    wide_tokens = widen(tokens)
    queries = jnp.einsum("sqd,de->sqe", wide_tokens, full_query, preferred_element_type=f32).astype(
        half
    )
    key_rows = jnp.einsum("sqd,de->sqe", wide_tokens, full_key, preferred_element_type=f32).astype(
        half
    )
    value_rows = jnp.einsum(
        "sqd,de->sqe", wide_tokens, full_value, preferred_element_type=f32
    ).astype(half)
    all_keys, all_values = (
        lax.all_gather(key_rows, "row", axis=1, tiled=True),
        lax.all_gather(value_rows, "row", axis=1, tiled=True),
    )
    mixture, log_total = lax.map(
        attend_forward, (queries, all_keys, all_values, own_labels, segment)
    )
    summed = tokens.astype(f32) + narrow(
        jnp.einsum("sqe,de->sqd", mixture, full_out, preferred_element_type=f32)
    )
    middle, inner_normed, inner_scaling = norm_forward(summed, inner_gain, inner_shift)
    wide_middle = widen(middle.astype(half))
    hidden = jnp.einsum("sqd,df->sqf", wide_middle, full_up, preferred_element_type=f32)
    active = gelu_value(hidden).astype(half)
    second_sum = middle + narrow(
        jnp.einsum("sqf,df->sqd", active, full_down, preferred_element_type=f32)
    )
    result, outer_normed, outer_scaling = norm_forward(second_sum, outer_gain, outer_shift)
    layer_out = result.astype(half)
    outer_gain_grad = jnp.sum(cotangent * outer_normed, axis=(0, 1))
    outer_shift_grad = jnp.sum(cotangent, axis=(0, 1))
    second_grad = norm_backward(cotangent, outer_normed, outer_scaling, outer_gain)
    wide_second = widen(second_grad.astype(half))
    grad_down = jnp.einsum("sqd,sqf->df", wide_second, active, preferred_element_type=f32)
    active_grad = (
        jnp.einsum("sqd,df->sqf", wide_second, full_down, preferred_element_type=f32)
        * gelu_slope(hidden)
    ).astype(half)
    grad_up = jnp.einsum("sqd,sqf->df", wide_middle, active_grad, preferred_element_type=f32)
    middle_grad = second_grad + narrow(
        jnp.einsum("sqf,df->sqd", active_grad, full_up, preferred_element_type=f32)
    )
    inner_gain_grad = jnp.sum(middle_grad * inner_normed, axis=(0, 1))
    inner_shift_grad = jnp.sum(middle_grad, axis=(0, 1))
    summed_grad = norm_backward(middle_grad, inner_normed, inner_scaling, inner_gain)
    wide_summed = widen(summed_grad.astype(half))
    grad_out = jnp.einsum("sqd,sqe->de", wide_summed, mixture, preferred_element_type=f32)
    mixture_grad = jnp.einsum(
        "sqd,de->sqe", wide_summed, full_out, preferred_element_type=f32
    ).astype(half)
    query_grad, key_part, value_part = lax.map(
        attend_backward,
        (queries, all_keys, all_values, own_labels, segment, log_total, mixture_grad),
    )
    key_sums, value_sums = (
        lax.psum_scatter(key_part, "row", scatter_dimension=1, tiled=True),
        lax.psum_scatter(value_part, "row", scatter_dimension=1, tiled=True),
    )
    key_grad = key_sums.astype(half)
    value_grad = value_sums.astype(half)
    grad_query = jnp.einsum("sqd,sqe->de", wide_tokens, query_grad, preferred_element_type=f32)
    grad_key = jnp.einsum("sqd,sqe->de", wide_tokens, key_grad, preferred_element_type=f32)
    grad_value = jnp.einsum("sqd,sqe->de", wide_tokens, value_grad, preferred_element_type=f32)
    back_sum = jnp.einsum("sqe,de->sqd", query_grad, full_query, preferred_element_type=f32)
    back_sum = back_sum + jnp.einsum("sqe,de->sqd", key_grad, full_key, preferred_element_type=f32)
    back_sum = back_sum + jnp.einsum(
        "sqe,de->sqd", value_grad, full_value, preferred_element_type=f32
    )
    input_grad = summed_grad + narrow(back_sum)
    norm_local = jnp.stack([inner_gain_grad, inner_shift_grad, outer_gain_grad, outer_shift_grad])
    weight_grads = (
        lax.psum_scatter(grad_query, ("dp", "row"), scatter_dimension=0, tiled=True),
        lax.psum_scatter(grad_key, ("dp", "row"), scatter_dimension=0, tiled=True),
        lax.psum_scatter(grad_value, ("dp", "row"), scatter_dimension=0, tiled=True),
        lax.psum_scatter(grad_out, ("dp", "row"), scatter_dimension=0, tiled=True),
        lax.psum_scatter(grad_up, ("dp", "row"), scatter_dimension=0, tiled=True),
        lax.psum_scatter(grad_down, ("dp", "row"), scatter_dimension=0, tiled=True),
    )
    norm_grads = lax.psum(norm_local, ("dp", "row"))
    return (
        layer_out,
        input_grad,
        weight_grads[0],
        weight_grads[1],
        weight_grads[2],
        weight_grads[3],
        weight_grads[4],
        weight_grads[5],
        norm_grads,
    )


PAIR = 128
BLOCK = 256
NEG = -1e30
HEADS = 16
SCALE = HEAD_DIM ** (-0.5)
VMEM_LIMIT = 48 << 20


def fits(mesh):
    sizes = dict(mesh.shape)
    return sizes["col"] == 2 and sizes["dp"] == 4 and sizes["row"] == 4


def head_mask(values, head):
    lane = lax.broadcasted_iota(jnp.int32, values.shape, 1)
    keep = (lane < HEAD_DIM) if head == 0 else (lane >= HEAD_DIM)
    return jnp.where(keep, values, jnp.zeros_like(values))


def dot(left, right):
    return jnp.dot(left, right, preferred_element_type=jnp.float32)


def forward_kernel(low, high, twist, q_t, k, v_t, own, others, *refs):
    out_t, log_total = refs[-2:]
    step = pl.program_id(0)
    queries = q_t[...]
    own_labels = own[...]
    inner = out_t.shape[2]
    per = k.shape[0] // 4 // BLOCK

    def block_at(j):
        start = ((j // per) ^ twist[0]) * per + j % per
        return pl.multiple_of(start * BLOCK, BLOCK)

    def body(n, carry):
        j = low[step] + 2 * n
        later = jnp.minimum(j + 1, high[step] - 1)
        starts = block_at(j), block_at(later)
        masks = []
        for index, extra in ((j, False), (later, later == j)):
            labels = others[pl.ds(pl.multiple_of(index * BLOCK, BLOCK), BLOCK), :]
            labels = jnp.where(extra, -1, labels)
            masks.append(jnp.concatenate([labels] * (BLOCK // PAIR), axis=1) == own_labels)
        keys = [k[pl.ds(start, BLOCK), :] for start in starts]
        state = []
        for head in range(2):
            highest, total, mixed = carry[head]
            scores = [
                jnp.where(inside, dot(head_mask(part, head), queries), NEG)
                for part, inside in zip(keys, masks)
            ]
            fresh = jnp.max(jnp.maximum(*scores), axis=0, keepdims=True)
            fresh = jnp.maximum(highest, fresh)
            fade = jnp.exp(highest - fresh)
            total, mixed = total * fade, mixed * fade
            for part, start in zip(scores, starts):
                chance = jnp.exp(part - fresh)
                values = v_t[head * HEAD_DIM : (head + 1) * HEAD_DIM, pl.ds(start, BLOCK)]
                total = total + jnp.sum(chance, axis=0, keepdims=True)
                mixed = mixed + dot(values, chance.astype(jnp.bfloat16))
            state.append((fresh, total, mixed))
        return tuple(state)

    one = (
        jnp.full((1, inner), NEG, jnp.float32),
        jnp.zeros((1, inner), jnp.float32),
        jnp.zeros((HEAD_DIM, inner), jnp.float32),
    )
    final = lax.fori_loop(0, (high[step] - low[step] + 1) // 2, body, (one, one))
    for head in range(2):
        highest, total, mixed = final[head]
        out_t[0, head * HEAD_DIM : (head + 1) * HEAD_DIM, :] = (mixed / total).astype(jnp.bfloat16)
        log_total[head : head + 1, :] = highest + jnp.log(total)


def backward_kernel(
    low,
    high,
    twist,
    q,
    q_t,
    g,
    g_t,
    out_t,
    log_total,
    k,
    v,
    k_t,
    own,
    others,
    *refs,
):
    result, dk_sum, dv_sum = refs[-3:]
    step = pl.program_id(0)
    per = k.shape[0] // 4 // BLOCK

    @pl.when(step == 0)
    def _():
        dk_sum[...] = jnp.zeros_like(dk_sum)
        dv_sum[...] = jnp.zeros_like(dv_sum)

    half = jnp.bfloat16
    queries_t = q_t[...]
    grads_t = g_t[0]
    own_labels = own[...]
    product = grads_t.astype(jnp.float32) * out_t[0].astype(jnp.float32)
    heads = []
    for head in range(2):
        rows = slice(head * HEAD_DIM, (head + 1) * HEAD_DIM)
        heads.append(
            (
                head_mask(q[...], head),
                head_mask(g[...], head),
                jnp.sum(product[rows], axis=0, keepdims=True),
                log_total[head : head + 1, :],
            )
        )

    def block_at(j):
        start = ((j // per) ^ twist[0]) * per + j % per
        return pl.multiple_of(start * BLOCK, BLOCK)

    def body(n, carry):
        j = low[step] + 2 * n
        later = jnp.minimum(j + 1, high[step] - 1)
        sums = list(carry)
        parts = []
        for index, extra in ((j, False), (later, later == j)):
            start = block_at(index)
            keys = k[pl.ds(start, BLOCK), :]
            values = v[pl.ds(start, BLOCK), :]
            labels = others[pl.ds(pl.multiple_of(index * BLOCK, BLOCK), BLOCK), :]
            labels = jnp.where(extra, -1, labels)
            inside = jnp.concatenate([labels] * (BLOCK // PAIR), axis=1) == own_labels
            key_part, value_part = None, None
            for head in range(2):
                own_q, own_g, within, total = heads[head]
                scores = dot(head_mask(keys, head), queries_t)
                chance = jnp.where(inside, jnp.exp(scores - total), 0.0)
                chance_grad = dot(head_mask(values, head), grads_t)
                score_grad = (chance * (chance_grad - within)).astype(half)
                value_new = dot(chance.astype(half), own_g)
                key_new = dot(score_grad, own_q)
                keys_t = k_t[head * HEAD_DIM : (head + 1) * HEAD_DIM, pl.ds(start, BLOCK)]
                sums[head] = sums[head] + dot(keys_t, score_grad)
                key_part = key_new if key_part is None else key_part + key_new
                value_part = value_new if value_part is None else value_part + value_new
            parts.append((start, key_part, value_part))
        for start, key_part, value_part in parts:
            dk_sum[pl.ds(start, BLOCK), :] += key_part
            dv_sum[pl.ds(start, BLOCK), :] += value_part
        return tuple(sums)

    zero = jnp.zeros((HEAD_DIM, own_labels.shape[1]), jnp.float32)
    first, second = lax.fori_loop(0, (high[step] - low[step] + 1) // 2, body, (zero, zero))
    both = jnp.concatenate([first, second], axis=0) * SCALE
    held = pl.multiple_of((((step // per) ^ twist[0]) * per + step % per) * BLOCK, BLOCK)
    result[pl.ds(held, BLOCK), :PAIR] = jnp.transpose(both).astype(half)

    @pl.when(step == pl.num_programs(0) - 1)
    def _():
        result[:, PAIR : 2 * PAIR] = dk_sum[...].astype(half)
        result[:, 2 * PAIR :] = dv_sum[...].astype(half)


def key_ranges(labels):
    blocks = labels.reshape(-1, BLOCK)
    first, last = blocks[:, :1], blocks[:, -1:]
    before = jnp.sum((labels[None, :] < first).astype(jnp.int32), axis=1)
    upto = jnp.sum((labels[None, :] <= last).astype(jnp.int32), axis=1)
    return before // BLOCK, (upto + BLOCK - 1) // BLOCK


def attend(pair, qkv, qkv_t, labels, wide_labels, scalars, before=()):
    length, width = qkv.shape
    pairs = width // 3 // PAIR
    row_count = length // 4
    inner = row_count // BLOCK

    def held(i, twist):
        return ((i // inner) ^ twist[0]) * inner + i % inner

    area = length * length
    return pl.pallas_call(
        forward_kernel,
        out_shape=(
            jax.ShapeDtypeStruct((4, pairs * PAIR, row_count), jnp.bfloat16),
            jax.ShapeDtypeStruct((8, length), jnp.float32),
        ),
        grid_spec=pltpu.PrefetchScalarGridSpec(
            num_scalar_prefetch=3,
            grid=(length // BLOCK,),
            in_specs=[
                pl.BlockSpec((PAIR, BLOCK), lambda i, lo, hi, tw: (3 * pair, held(i, tw))),
                pl.BlockSpec((length, PAIR), lambda i, lo, hi, tw: (0, 3 * pair + 1)),
                pl.BlockSpec((PAIR, length), lambda i, lo, hi, tw: (3 * pair + 2, 0)),
                pl.BlockSpec((1, BLOCK), lambda i, lo, hi, tw: (0, i)),
                pl.BlockSpec((length, PAIR), lambda i, lo, hi, tw: (0, 0)),
            ]
            + [pl.BlockSpec(memory_space=pl.ANY) for _ in before],
            out_specs=(
                pl.BlockSpec((1, PAIR, BLOCK), lambda i, lo, hi, tw: (i // inner, pair, i % inner)),
                pl.BlockSpec((8, BLOCK), lambda i, lo, hi, tw: (0, i)),
            ),
        ),
        input_output_aliases={8: 0} if before else {},
        compiler_params=pltpu.CompilerParams(vmem_limit_bytes=VMEM_LIMIT),
        cost_estimate=pl.CostEstimate(
            flops=area * 256 * 24, bytes_accessed=4 << 20, transcendentals=2 * area
        ),
    )(*scalars, qkv_t, qkv, qkv_t, labels, wide_labels, *before)


def attend_back(
    pair, qkv, qkv_t, labels, wide_labels, scalars, out_t, log_total, grads, grads_t, before=()
):
    length, width = grads.shape
    pairs = width // PAIR
    row_count = length // 4
    inner = row_count // BLOCK

    def held(i, twist):
        return ((i // inner) ^ twist[0]) * inner + i % inner

    area = length * length
    return pl.pallas_call(
        backward_kernel,
        out_shape=jax.ShapeDtypeStruct(qkv.shape, jnp.bfloat16),
        grid_spec=pltpu.PrefetchScalarGridSpec(
            num_scalar_prefetch=3,
            grid=(length // BLOCK,),
            in_specs=[
                pl.BlockSpec((BLOCK, PAIR), lambda i, lo, hi, tw: (held(i, tw), 3 * pair)),
                pl.BlockSpec((PAIR, BLOCK), lambda i, lo, hi, tw: (3 * pair, held(i, tw))),
                pl.BlockSpec((BLOCK, PAIR), lambda i, lo, hi, tw: (i, pair)),
                pl.BlockSpec((1, PAIR, BLOCK), lambda i, lo, hi, tw: (i // inner, pair, i % inner)),
                pl.BlockSpec((1, PAIR, BLOCK), lambda i, lo, hi, tw: (i // inner, pair, i % inner)),
                pl.BlockSpec((8, BLOCK), lambda i, lo, hi, tw: (0, i)),
                pl.BlockSpec((length, PAIR), lambda i, lo, hi, tw: (0, 3 * pair + 1)),
                pl.BlockSpec((length, PAIR), lambda i, lo, hi, tw: (0, 3 * pair + 2)),
                pl.BlockSpec((PAIR, length), lambda i, lo, hi, tw: (3 * pair + 1, 0)),
                pl.BlockSpec((1, BLOCK), lambda i, lo, hi, tw: (0, i)),
                pl.BlockSpec((length, PAIR), lambda i, lo, hi, tw: (0, 0)),
            ]
            + [pl.BlockSpec(memory_space=pl.ANY) for _ in before],
            out_specs=pl.BlockSpec((length, 3 * PAIR), lambda i, lo, hi, tw: (0, pair)),
            scratch_shapes=[
                pltpu.VMEM((length, PAIR), jnp.float32),
                pltpu.VMEM((length, PAIR), jnp.float32),
            ],
        ),
        input_output_aliases={14: 0} if before else {},
        compiler_params=pltpu.CompilerParams(vmem_limit_bytes=VMEM_LIMIT),
        cost_estimate=pl.CostEstimate(
            flops=area * 256 * 24, bytes_accessed=6 << 20, transcendentals=2 * area
        ),
    )(
        *scalars,
        qkv,
        qkv_t,
        grads,
        grads_t,
        out_t,
        log_total,
        qkv,
        qkv,
        qkv_t,
        labels,
        wide_labels,
        *before,
    )


def assemble(pieces, shapes, moves):
    count = len(shapes)

    def kernel(*refs):
        sources, rest = refs[: len(pieces)], refs[len(pieces) :]
        outs, held, arrived, left = rest[:count], rest[count : 2 * count], rest[-2], rest[-1]
        inward, outward = [], []
        for n, (piece, rows, columns, out, row, column) in enumerate(moves):
            at = (pl.ds(row, rows[1] - rows[0]), pl.ds(column, columns[1] - columns[0]))
            source = sources[piece].at[rows[0] : rows[1], columns[0] : columns[1]]
            inward.append(pltpu.make_async_copy(source, held[out].at[at], arrived.at[n]))
            outward.append(pltpu.make_async_copy(held[out].at[at], outs[out].at[at], left.at[n]))
        for copy in inward:
            copy.start()
        for copy, onward in zip(inward, outward):
            copy.wait()
            onward.start()
        for copy in outward:
            copy.wait()

    any_space = pl.BlockSpec(memory_space=pl.ANY)
    total = sum(2 * a * b for a, b in shapes)
    return pl.pallas_call(
        kernel,
        out_shape=tuple(jax.ShapeDtypeStruct(shape, jnp.bfloat16) for shape in shapes),
        in_specs=[any_space] * len(pieces),
        out_specs=(any_space,) * len(shapes),
        scratch_shapes=[pltpu.VMEM(shape, jnp.bfloat16) for shape in shapes]
        + [pltpu.SemaphoreType.DMA((len(moves),))] * 2,
        compiler_params=pltpu.CompilerParams(vmem_limit_bytes=16 << 20),
        cost_estimate=pl.CostEstimate(flops=0, bytes_accessed=2 * total, transcendentals=0),
    )(*pieces)


def projections(planes, row, late):
    _, kinds, rows, width = planes[0].shape
    pairs = width // PAIR

    def kernel(row_ref, late_ref, *refs):
        plain, scaled = refs[-2:]
        for j, plane in enumerate(refs[:-2]):
            for i in range(4):
                base = ((j // 2) ^ late_ref[0]) * 2 + j % 2
                at = pl.multiple_of((base * 4 + (i ^ row_ref[0])) * rows, rows)
                for kind in range(kinds):
                    for pair in range(pairs):
                        column = (pair * kinds + kind) * PAIR
                        part = plane[i, kind, :, pair * PAIR : (pair + 1) * PAIR]
                        plain[pl.ds(at, rows), column : column + PAIR] = part
                        if kind == 0:
                            part = part * jnp.asarray(SCALE, part.dtype)
                        scaled[pl.ds(at, rows), column : column + PAIR] = part

    shape = jax.ShapeDtypeStruct((16 * rows, kinds * width), jnp.bfloat16)
    held = pl.BlockSpec(memory_space=pltpu.VMEM)
    return pl.pallas_call(
        kernel,
        out_shape=(shape, shape),
        in_specs=[pl.BlockSpec(memory_space=pltpu.SMEM)] * 2 + [held] * 4,
        out_specs=(held, held),
        compiler_params=pltpu.CompilerParams(vmem_limit_bytes=24 << 20),
        cost_estimate=pl.CostEstimate(flops=0, bytes_accessed=6 << 20, transcendentals=0),
    )(row.reshape(1), late.reshape(1), *planes)


def swap(values):
    return lax.ppermute(values, "col", [(0, 1), (1, 0)])


def flip(values, axis, bit, size=4):
    return lax.ppermute(values, axis, [(i, i ^ bit) for i in range(size)])


def pick(values, index, axis=0):
    return lax.dynamic_index_in_dim(values, index, axis, keepdims=False)


def together(*values):
    return lax.optimization_barrier(values)


def gather_start(block):
    rows = block.shape[0] // 2
    top, low = block[:rows], block[rows:]
    return top, low, flip(top, "dp", 1), flip(low, "dp", 2)


def gather_second(state):
    top, low, top_x, low_y = state
    top_y = flip(jnp.concatenate([top, top_x]), "dp", 2)
    low_x = flip(jnp.concatenate([low, low_y]), "dp", 1)
    return top_y, low_x


def gather_end(state, second, parts):
    pieces = (*state, *second)
    rows = pieces[0].shape[0]
    whole, head, tail = (0, rows), (0, rows), (rows, 2 * rows)
    order = ((0, whole), (1, whole), (2, whole), (5, head), (4, head), (3, whole), (4, tail), (5, tail))
    moves = [
        (piece, span, part, n, place * rows, 0)
        for place, (piece, span) in enumerate(order)
        for n, part in enumerate(parts)
    ]
    return assemble(pieces, [(8 * rows, stop - start) for start, stop in parts], moves)


def scatter_split(*grads):
    rows = grads[0].shape[0] // 8
    moves, column = [], 0
    order = (((0, 0),), ((1, 0),), ((0, 1),), ((2, 1),), ((2, 0), (3, 0)), ((1, 1), (3, 1)))
    for piece, array in enumerate(grads):
        columns = array.shape[1]
        for out, parts in enumerate(order):
            for place, (block, second) in enumerate(parts):
                at = (2 * block + second) * rows
                moves.append((piece, (at, at + rows), (0, columns), out, place * rows, column))
        column += columns
    shapes = [(len(parts) * rows, column) for parts in order]
    return assemble(grads, shapes, moves)


def scatter_start(parts):
    *kept, send_y, send_x = parts
    return *kept, flip(send_y, "dp", 2), flip(send_x, "dp", 1)


def scatter_second(state):
    f32, half = jnp.float32, jnp.bfloat16
    top, top_pass, low, low_pass, top_y, low_x = state
    rows = top.shape[0]
    top_x = flip((top_pass.astype(f32) + top_y[rows:].astype(f32)).astype(half), "dp", 1)
    low_y = flip((low_pass.astype(f32) + low_x[rows:].astype(f32)).astype(half), "dp", 2)
    return top_x, low_y


def scatter_end(state, second):
    f32, half = jnp.float32, jnp.bfloat16
    top, _, low, _, top_y, low_x = state
    top_x, low_y = second
    rows = top.shape[0]
    top = top.astype(f32) + top_y[:rows].astype(f32) + top_x.astype(f32)
    low = low.astype(f32) + low_x[:rows].astype(f32) + low_y.astype(f32)
    return jnp.concatenate([top, low]).astype(half)


def whole_norm(summed, gain, shift):
    average = jnp.mean(summed, axis=-1, keepdims=True)
    spread = jnp.mean(summed * summed, axis=-1, keepdims=True) - average * average
    scaling = lax.rsqrt(spread + EPS)
    normed = (summed - average) * scaling
    return (normed * gain + shift, normed, scaling)


def whole_norm_back(upstream, normed, scaling, gain):
    scaled = upstream * gain
    offset = jnp.mean(scaled, axis=-1, keepdims=True)
    slope = jnp.mean(scaled * normed, axis=-1, keepdims=True)
    return scaling * (scaled - offset - normed * slope)


def fast_local(
    tokens,
    segment,
    w_query,
    w_key,
    w_value,
    w_out,
    w_up,
    w_down,
    inner_gain,
    inner_shift,
    outer_gain,
    outer_shift,
    cotangent,
):
    f32 = jnp.float32
    half = jnp.bfloat16
    me = lax.axis_index("dp")
    core = lax.axis_index("col")
    row = lax.axis_index("row")
    which, parity = row // 2, row % 2
    first_core = core == 0
    crossed = me % 2 == 1
    leading = core == me // 2
    row_count = tokens.shape[1]
    length = segment.shape[1]
    block_rows, half_width = w_query.shape
    width = D // 4
    hidden_half = w_up.shape[1]
    stack, cat = jnp.stack, jnp.concatenate

    def turn(values):
        left, right = values[..., :width], values[..., width:]
        return jnp.where(crossed, cat([right, left], axis=-1), values)

    def merge(mine, other):
        return jnp.where(leading, cat([mine, other], axis=-1), cat([other, mine], axis=-1))

    def divide(values):
        left, right = values[..., :half_width], values[..., half_width:]
        return jnp.where(leading, left, right), jnp.where(leading, right, left)

    def by_core(mine, other):
        return jnp.where(first_core, stack([mine, other]), stack([other, mine]))

    tokens = turn(tokens)
    near_0 = pick(tokens, which)
    near_2 = flip(pick(tokens, 1 - which), "row", 2)
    near_1 = flip(near_0, "row", 1)
    own_tokens = merge(pick(tokens, core), swap(pick(tokens, 1 - core)))
    labels = pick(segment, which)
    scalars = (*key_ranges(labels), row.reshape(1))
    wide_labels = jnp.broadcast_to(labels[:, None], (length, PAIR))
    labels = labels[None]

    thirds = stack([w_query, w_key, w_value]).reshape(3, block_rows, 2, width)
    blocks = by_core(pick(thirds, core, 2), swap(pick(thirds, 1 - core, 2)))
    same, cross = pick(blocks, parity), pick(blocks, 1 - parity)
    near = [same] + [flip(same if bit == 2 else cross, "row", bit) for bit in (1, 2, 3)]
    odd = row % 2 == 1
    strips = stack(near)
    packed, plain_down, near_1, near_2, strips = together(
        cat([w_out, w_up], axis=1), w_down, near_1, near_2, strips
    )
    near_3 = flip(near_2, "row", 1)
    out_up_rows = lax.all_gather(packed, "row", axis=0, tiled=True)
    down_rows = lax.all_gather(plain_down, "row", axis=0, tiled=True)
    out_up = gather_start(out_up_rows)
    planes = [strips] + [flip(strips, "dp", bit) for bit in (1, 2, 3)]
    pieces = [near_0, near_1, near_2, near_3]
    pieces += [swap(piece) for piece in pieces]
    whole = (0, row_count), (0, half_width)
    (series,) = assemble(
        pieces,
        [(length, D)],
        [(n, *whole, 0, n % 4 * row_count, n // 4 * half_width) for n in range(8)],
    )
    w_qkv, w_scaled = projections(planes, row, core ^ (me // 2))
    w_mine, w_other = w_qkv[:half_width], w_qkv[half_width:]

    vectors = turn(stack([inner_gain, inner_shift, outer_gain, outer_shift]))
    vectors = merge(vectors, swap(vectors))
    inner_gain, inner_shift, outer_gain, outer_shift = (vectors[i : i + 1] for i in range(4))
    cotangent = turn(cotangent)
    upstream = merge(pick(cotangent, core), swap(pick(cotangent, 1 - core)))

    qkv = dot(series, w_scaled).astype(half)
    qkv_t = qkv.T
    out_0, total_0 = attend(0, qkv, qkv_t, labels, wide_labels, scalars)
    scalars_1, out_up, out_0 = together(scalars, out_up, out_0)
    out_t, total_1 = attend(1, qkv, qkv_t, labels, wide_labels, scalars_1, (out_0,))
    out_up_second = gather_second(out_up)
    down_first = gather_start(down_rows)
    down_second = gather_second(down_first)
    out_t, out_up_second = together(out_t, out_up_second)
    mixed = lax.all_to_all(out_t, "row", 0, 0, tiled=True)
    out_half, up = gather_end(
        out_up, out_up_second, ((0, half_width), (half_width, half_width + hidden_half))
    )
    full_out = cat([out_half, swap(out_half)], axis=1)
    mixed, down_second = together(mixed, down_second)
    (down,) = gather_end(down_first, down_second, ((0, hidden_half),))
    mixed = mixed.reshape(2, 2, width, row_count)
    kept, passed = pick(mixed, core), swap(pick(mixed, 1 - core))
    mixture_t = jnp.where(
        first_core,
        cat([kept[0], passed[0], kept[1], passed[1]]),
        cat([passed[1], kept[1], passed[0], kept[0]]),
    )

    summed = own_tokens.astype(f32) + jnp.einsum(
        "eq,de->qd", mixture_t, full_out, preferred_element_type=f32
    )
    middle, inner_normed, inner_scaling = whole_norm(summed, inner_gain, inner_shift)

    middle_own = middle.astype(half)
    middle_other = swap(middle_own)
    hidden_own = dot(middle_own, up)
    hidden_other = dot(middle_other, up)
    active_own = gelu_value(hidden_own).astype(half)
    active_other = gelu_value(hidden_other).astype(half)
    down_other = jnp.einsum("qf,df->qd", active_other, down, preferred_element_type=f32)
    down_swapped = swap(down_other.astype(half))
    down_own = jnp.einsum("qf,df->qd", active_own, down, preferred_element_type=f32)
    second_sum = middle + (down_own + down_swapped.astype(f32))
    result, outer_normed, outer_scaling = whole_norm(second_sum, outer_gain, outer_shift)
    kept, passed = divide(result.astype(half))
    layer_out = turn(by_core(kept, swap(passed)))

    outer_gain_grad = jnp.sum(upstream * outer_normed, axis=0)
    outer_shift_grad = jnp.sum(upstream, axis=0)
    second_grad = whole_norm_back(upstream, outer_normed, outer_scaling, outer_gain)
    second_own = second_grad.astype(half)
    second_other = swap(second_own)

    def weight_grad(left, right):
        return jnp.einsum("qd,qf->df", left, right, preferred_element_type=f32)

    grad_down = weight_grad(second_own, active_own) + weight_grad(second_other, active_other)
    down_parts = scatter_split(grad_down.astype(half))
    down_parts, second_own, second_other = together(down_parts, second_own, second_other)
    down_first = scatter_start(down_parts)
    active_grad_own = (dot(second_own, down) * gelu_slope(hidden_own)).astype(half)
    active_grad_other = (dot(second_other, down) * gelu_slope(hidden_other)).astype(half)
    middle_grad_other = jnp.einsum("qf,df->qd", active_grad_other, up, preferred_element_type=f32)
    middle_swapped = swap(middle_grad_other.astype(half))
    middle_swapped, down_first = together(middle_swapped, down_first)
    middle_grad_own = jnp.einsum("qf,df->qd", active_grad_own, up, preferred_element_type=f32)

    middle_grad = second_grad + (middle_grad_own + middle_swapped.astype(f32))
    inner_gain_grad = jnp.sum(middle_grad * inner_normed, axis=0)
    inner_shift_grad = jnp.sum(middle_grad, axis=0)
    summed_grad = whole_norm_back(middle_grad, inner_normed, inner_scaling, inner_gain)
    summed_half = summed_grad.astype(half)
    grads_t = jnp.einsum("qd,de->eq", summed_half, full_out, preferred_element_type=f32)
    grads_t = grads_t.astype(half).reshape(4, width, row_count)
    kept = jnp.where(
        first_core, stack([grads_t[0], grads_t[2]]), stack([grads_t[3], grads_t[1]])
    )
    passed = jnp.where(
        first_core, stack([grads_t[1], grads_t[3]]), stack([grads_t[2], grads_t[0]])
    )
    grads_t = by_core(kept, swap(passed)).reshape(4, width, row_count)
    down_second = scatter_second(down_first)
    grads_t, down_second = together(grads_t, down_second)
    grads_t = lax.all_to_all(grads_t, "row", 0, 0, tiled=True)

    grad_up = weight_grad(middle_own, active_grad_own) + weight_grad(
        middle_other, active_grad_other
    )
    grad_out = jnp.einsum("qd,eq->de", summed_half, mixture_t, preferred_element_type=f32)
    grad_out = grad_out[:, :half_width] + swap(grad_out[:, half_width:].astype(half)).astype(f32)
    out_up_parts = scatter_split(grad_out.astype(half), grad_up.astype(half))
    kept, passed = divide(summed_grad)
    base = turn(by_core(kept, swap(passed)))
    out_up_first = scatter_start(out_up_parts)
    grads_t, down_second, out_up_first = together(grads_t, down_second, out_up_first)
    grads = grads_t.transpose(0, 2, 1).reshape(length, width)
    qkv_grad = attend_back(
        0, qkv, qkv_t, labels, wide_labels, scalars, out_t, total_0, grads, grads_t
    )
    grad_down = lax.psum_scatter(
        scatter_end(down_first, down_second), "row", scatter_dimension=0, tiled=True
    )
    out_up_second = scatter_second(out_up_first)
    out_up_plane = scatter_end(out_up_first, out_up_second)
    scalars_1, grad_down, out_up_plane, qkv_grad, base, layer_out = together(
        scalars, grad_down, out_up_plane, qkv_grad, base, layer_out
    )
    out_up_grad = lax.psum_scatter(out_up_plane, "row", scatter_dimension=0, tiled=True)
    qkv_grad = attend_back(
        1, qkv, qkv_t, labels, wide_labels, scalars_1, out_t, total_1, grads, grads_t, (qkv_grad,)
    )
    qkv_grad, out_up_grad = together(qkv_grad, out_up_grad)
    grad_down, out_up_grad = grad_down.astype(f32), out_up_grad.astype(f32)
    grad_out, grad_up = out_up_grad[:, :half_width], out_up_grad[:, half_width:]

    def back_part(rows):
        return jnp.einsum("le,de->ld", qkv_grad, rows, preferred_element_type=f32)

    back_other = swap(back_part(w_other).astype(half))
    norm_local = stack([inner_gain_grad, inner_shift_grad, outer_gain_grad, outer_shift_grad])
    back = back_part(w_mine) + back_other.astype(f32)
    back = back.reshape(4, row_count, half_width)
    pass_on = turn(back[2] + flip(back[3].astype(half), "row", 1).astype(f32)).astype(half)
    pass_on, qkv_grad, norm_local = together(pass_on, qkv_grad, norm_local)
    from_far = flip(pass_on, "row", 2)
    from_near = turn(back[0] + flip(back[1].astype(half), "row", 1).astype(f32))
    slot = jnp.arange(2).reshape(2, 1, 1)
    base = base + jnp.where(slot == which, from_near[None], 0.0)

    grads = jnp.einsum("ld,le->de", series, qkv_grad, preferred_element_type=f32)
    grads_mine, grads_other = grads[:half_width], grads[half_width:]

    def plane_part(j):
        rows = slice((j % 2) * width, (j % 2 + 1) * width)
        if j < 2:
            return jnp.where(leading, grads_mine[rows], grads_other[rows])
        return jnp.where(leading, grads_other[rows], grads_mine[rows])

    total = plane_part(0)
    for bit in range(1, 4):
        total = total + flip(plane_part(bit).astype(half), "dp", bit).astype(f32)
    total = total.reshape(4, block_rows, 3 * width)
    sends = tuple(pick(total, row ^ bit).astype(half) for bit in (1, 2, 3))
    sends, base, from_far = together(sends, base, from_far)
    near_1, near_2, near_3 = (flip(part, "row", bit) for bit, part in zip((1, 2, 3), sends))
    own_part = (pick(total, row) + near_2.astype(f32)).astype(half)
    other_part = (near_1.astype(f32) + near_3.astype(f32)).astype(half)
    strip = jnp.where(odd, stack([other_part, own_part]), stack([own_part, other_part]))
    kept, passed = pick(strip, core), swap(pick(strip, 1 - core))

    def by_kind(values):
        values = values.reshape(block_rows, width // PAIR, 3, PAIR).transpose(2, 0, 1, 3)
        return values.reshape(3, block_rows, width)

    kept, passed = by_kind(kept), by_kind(passed)
    qkv_grads = jnp.where(first_core, cat([kept, passed], axis=2), cat([passed, kept], axis=2))
    qkv_grads = qkv_grads.astype(f32)

    input_grad = base + jnp.where(slot == which, 0.0, from_far[None].astype(f32))

    kept, passed = divide(norm_local)
    norm_grads = turn(kept + swap(passed))
    for axis in ("row", "dp"):
        one, two, three = (flip(norm_grads, axis, bit) for bit in (1, 2, 3))
        norm_grads = (norm_grads + one) + (two + three)
    return (
        layer_out,
        input_grad,
        qkv_grads[0],
        qkv_grads[1],
        qkv_grads[2],
        grad_out,
        grad_up,
        grad_down,
        norm_grads,
    )


def solution(mesh):
    placed = (
        P("dp", "row", "col"),
        P("dp", None),
        P(("dp", "row"), "col"),
        P(("dp", "row"), "col"),
        P(("dp", "row"), "col"),
        P(("dp", "row"), "col"),
        P(("dp", "row"), "col"),
        P(("dp", "row"), "col"),
        P("col"),
        P("col"),
        P("col"),
        P("col"),
        P("dp", "row", "col"),
    )
    body = fast_local if fits(mesh) else local
    return jax.shard_map(
        body,
        mesh=mesh,
        in_specs=placed,
        out_specs=(
            P("dp", "row", "col"),
            P("dp", "row", "col"),
            P(("dp", "row"), "col"),
            P(("dp", "row"), "col"),
            P(("dp", "row"), "col"),
            P(("dp", "row"), "col"),
            P(("dp", "row"), "col"),
            P(("dp", "row"), "col"),
            P(None, "col"),
        ),
        check_vma=False,
    )
```

```python
import jax
import jax.numpy as jnp
from jax import lax
from jax.experimental import pallas as pl
from jax.experimental.pallas import tpu as pltpu
from jax.sharding import PartitionSpec as P

D = 1024
HEAD_DIM = 64


EPS = 1e-05
ROOT_HALF = 0.7071067811865476
INV_ROOT_TAU = 0.3989422804014327


def gelu_value(inputs):
    return 0.5 * inputs * (1.0 + lax.erf(inputs * ROOT_HALF))


def gelu_slope(inputs):
    return (
        0.5 * (1.0 + lax.erf(inputs * ROOT_HALF))
        + inputs * jnp.exp(-0.5 * inputs * inputs) * INV_ROOT_TAU
    )


def widen(values):
    return lax.all_gather(values, "col", axis=2, tiled=True)


def narrow(partial_value):
    return lax.psum_scatter(partial_value, "col", scatter_dimension=2, tiled=True)


def norm_forward(summed, norm_gain, norm_shift):
    row_sums, squares = lax.psum(
        (jnp.sum(summed, axis=-1, keepdims=True), jnp.sum(summed * summed, axis=-1, keepdims=True)),
        "col",
    )
    average = row_sums / D
    spread = squares / D - average * average
    scaling = lax.rsqrt(spread + EPS)
    normed = (summed - average) * scaling
    return (normed * norm_gain + norm_shift, normed, scaling)


def norm_backward(upstream, normed, scaling, norm_gain):
    scaled = upstream * norm_gain
    offset_sum, slope_sum = lax.psum(
        (jnp.sum(scaled, axis=-1, keepdims=True), jnp.sum(scaled * normed, axis=-1, keepdims=True)),
        "col",
    )
    return scaling * (scaled - offset_sum / D - normed * (slope_sum / D))


def head_view(values):
    return values.reshape(values.shape[0], values.shape[1] // HEAD_DIM, HEAD_DIM)


def masked_scores(queries, key_rows, own_labels, all_labels):
    scores = jnp.einsum(
        "qhe,khe->hqk", head_view(queries), head_view(key_rows), preferred_element_type=jnp.float32
    ) * HEAD_DIM ** (-0.5)
    inside = own_labels[:, None] == all_labels[None, :]
    return jnp.where(inside[None], scores, -jnp.inf)


def attend_forward(inputs):
    queries, key_rows, value_rows, own_labels, all_labels = inputs
    scores = masked_scores(queries, key_rows, own_labels, all_labels)
    highest = jnp.max(scores, axis=-1, keepdims=True)
    log_total = highest + jnp.log(jnp.sum(jnp.exp(scores - highest), axis=-1, keepdims=True))
    attention = jnp.exp(scores - log_total).astype(jnp.bfloat16)
    mixture = jnp.einsum(
        "hqk,khe->qhe", attention, head_view(value_rows), preferred_element_type=jnp.float32
    )
    return (mixture.reshape(queries.shape).astype(jnp.bfloat16), log_total)


def attend_backward(inputs):
    queries, key_rows, value_rows, own_labels, all_labels, log_total, mixture_grad = inputs
    scores = masked_scores(queries, key_rows, own_labels, all_labels)
    chance = jnp.exp(scores - log_total)
    attention = chance.astype(jnp.bfloat16)
    chance_grad = jnp.einsum(
        "qhe,khe->hqk",
        head_view(mixture_grad),
        head_view(value_rows),
        preferred_element_type=jnp.float32,
    )
    within = jnp.sum(chance * chance_grad, axis=-1, keepdims=True)
    score_grad = (chance * (chance_grad - within) * HEAD_DIM ** (-0.5)).astype(jnp.bfloat16)
    query_grad = jnp.einsum(
        "hqk,khe->qhe", score_grad, head_view(key_rows), preferred_element_type=jnp.float32
    )
    key_part = jnp.einsum(
        "hqk,qhe->khe", score_grad, head_view(queries), preferred_element_type=jnp.float32
    )
    value_part = jnp.einsum(
        "hqk,qhe->khe", attention, head_view(mixture_grad), preferred_element_type=jnp.float32
    )
    return (
        query_grad.reshape(queries.shape).astype(jnp.bfloat16),
        key_part.reshape(key_rows.shape),
        value_part.reshape(value_rows.shape),
    )


def local(
    tokens,
    segment,
    w_query,
    w_key,
    w_value,
    w_out,
    w_up,
    w_down,
    inner_gain,
    inner_shift,
    outer_gain,
    outer_shift,
    cotangent,
):
    f32 = jnp.float32
    half = jnp.bfloat16
    gathered = (
        lax.all_gather(w_query, ("dp", "row"), axis=0, tiled=True),
        lax.all_gather(w_key, ("dp", "row"), axis=0, tiled=True),
        lax.all_gather(w_value, ("dp", "row"), axis=0, tiled=True),
        lax.all_gather(w_out, ("dp", "row"), axis=0, tiled=True),
        lax.all_gather(w_up, ("dp", "row"), axis=0, tiled=True),
        lax.all_gather(w_down, ("dp", "row"), axis=0, tiled=True),
    )
    full_query, full_key, full_value, full_out, full_up, full_down = gathered
    row_count = tokens.shape[1]
    own_labels = lax.dynamic_slice_in_dim(segment, lax.axis_index("row") * row_count, row_count, 1)
    wide_tokens = widen(tokens)
    queries = jnp.einsum("sqd,de->sqe", wide_tokens, full_query, preferred_element_type=f32).astype(
        half
    )
    key_rows = jnp.einsum("sqd,de->sqe", wide_tokens, full_key, preferred_element_type=f32).astype(
        half
    )
    value_rows = jnp.einsum(
        "sqd,de->sqe", wide_tokens, full_value, preferred_element_type=f32
    ).astype(half)
    all_keys, all_values = (
        lax.all_gather(key_rows, "row", axis=1, tiled=True),
        lax.all_gather(value_rows, "row", axis=1, tiled=True),
    )
    mixture, log_total = lax.map(
        attend_forward, (queries, all_keys, all_values, own_labels, segment)
    )
    summed = tokens.astype(f32) + narrow(
        jnp.einsum("sqe,de->sqd", mixture, full_out, preferred_element_type=f32)
    )
    middle, inner_normed, inner_scaling = norm_forward(summed, inner_gain, inner_shift)
    wide_middle = widen(middle.astype(half))
    hidden = jnp.einsum("sqd,df->sqf", wide_middle, full_up, preferred_element_type=f32)
    active = gelu_value(hidden).astype(half)
    second_sum = middle + narrow(
        jnp.einsum("sqf,df->sqd", active, full_down, preferred_element_type=f32)
    )
    result, outer_normed, outer_scaling = norm_forward(second_sum, outer_gain, outer_shift)
    layer_out = result.astype(half)
    outer_gain_grad = jnp.sum(cotangent * outer_normed, axis=(0, 1))
    outer_shift_grad = jnp.sum(cotangent, axis=(0, 1))
    second_grad = norm_backward(cotangent, outer_normed, outer_scaling, outer_gain)
    wide_second = widen(second_grad.astype(half))
    grad_down = jnp.einsum("sqd,sqf->df", wide_second, active, preferred_element_type=f32)
    active_grad = (
        jnp.einsum("sqd,df->sqf", wide_second, full_down, preferred_element_type=f32)
        * gelu_slope(hidden)
    ).astype(half)
    grad_up = jnp.einsum("sqd,sqf->df", wide_middle, active_grad, preferred_element_type=f32)
    middle_grad = second_grad + narrow(
        jnp.einsum("sqf,df->sqd", active_grad, full_up, preferred_element_type=f32)
    )
    inner_gain_grad = jnp.sum(middle_grad * inner_normed, axis=(0, 1))
    inner_shift_grad = jnp.sum(middle_grad, axis=(0, 1))
    summed_grad = norm_backward(middle_grad, inner_normed, inner_scaling, inner_gain)
    wide_summed = widen(summed_grad.astype(half))
    grad_out = jnp.einsum("sqd,sqe->de", wide_summed, mixture, preferred_element_type=f32)
    mixture_grad = jnp.einsum(
        "sqd,de->sqe", wide_summed, full_out, preferred_element_type=f32
    ).astype(half)
    query_grad, key_part, value_part = lax.map(
        attend_backward,
        (queries, all_keys, all_values, own_labels, segment, log_total, mixture_grad),
    )
    key_sums, value_sums = (
        lax.psum_scatter(key_part, "row", scatter_dimension=1, tiled=True),
        lax.psum_scatter(value_part, "row", scatter_dimension=1, tiled=True),
    )
    key_grad = key_sums.astype(half)
    value_grad = value_sums.astype(half)
    grad_query = jnp.einsum("sqd,sqe->de", wide_tokens, query_grad, preferred_element_type=f32)
    grad_key = jnp.einsum("sqd,sqe->de", wide_tokens, key_grad, preferred_element_type=f32)
    grad_value = jnp.einsum("sqd,sqe->de", wide_tokens, value_grad, preferred_element_type=f32)
    back_sum = jnp.einsum("sqe,de->sqd", query_grad, full_query, preferred_element_type=f32)
    back_sum = back_sum + jnp.einsum("sqe,de->sqd", key_grad, full_key, preferred_element_type=f32)
    back_sum = back_sum + jnp.einsum(
        "sqe,de->sqd", value_grad, full_value, preferred_element_type=f32
    )
    input_grad = summed_grad + narrow(back_sum)
    norm_local = jnp.stack([inner_gain_grad, inner_shift_grad, outer_gain_grad, outer_shift_grad])
    weight_grads = (
        lax.psum_scatter(grad_query, ("dp", "row"), scatter_dimension=0, tiled=True),
        lax.psum_scatter(grad_key, ("dp", "row"), scatter_dimension=0, tiled=True),
        lax.psum_scatter(grad_value, ("dp", "row"), scatter_dimension=0, tiled=True),
        lax.psum_scatter(grad_out, ("dp", "row"), scatter_dimension=0, tiled=True),
        lax.psum_scatter(grad_up, ("dp", "row"), scatter_dimension=0, tiled=True),
        lax.psum_scatter(grad_down, ("dp", "row"), scatter_dimension=0, tiled=True),
    )
    norm_grads = lax.psum(norm_local, ("dp", "row"))
    return (
        layer_out,
        input_grad,
        weight_grads[0],
        weight_grads[1],
        weight_grads[2],
        weight_grads[3],
        weight_grads[4],
        weight_grads[5],
        norm_grads,
    )


PAIR = 128
BLOCK = 256
NEG = -1e30
HEADS = 16
SCALE = HEAD_DIM ** (-0.5)
VMEM_LIMIT = 48 << 20


def fits(mesh):
    sizes = dict(mesh.shape)
    return sizes["col"] == 2 and sizes["dp"] == 4 and sizes["row"] == 4


def head_mask(values, head):
    lane = lax.broadcasted_iota(jnp.int32, values.shape, 1)
    keep = (lane < HEAD_DIM) if head == 0 else (lane >= HEAD_DIM)
    return jnp.where(keep, values, jnp.zeros_like(values))


def dot(left, right):
    return jnp.dot(left, right, preferred_element_type=jnp.float32)


def forward_kernel(low, high, twist, q_t, k, v_t, own, others, *refs):
    out_t, log_total = refs[-2:]
    step = pl.program_id(0)
    queries = q_t[...]
    own_labels = own[...]
    inner = out_t.shape[2]
    per = k.shape[0] // 4 // BLOCK

    def block_at(j):
        start = ((j // per) ^ twist[0]) * per + j % per
        return pl.multiple_of(start * BLOCK, BLOCK)

    def body(n, carry):
        j = low[step] + 2 * n
        later = jnp.minimum(j + 1, high[step] - 1)
        starts = block_at(j), block_at(later)
        masks = []
        for index, extra in ((j, False), (later, later == j)):
            labels = others[pl.ds(pl.multiple_of(index * BLOCK, BLOCK), BLOCK), :]
            labels = jnp.where(extra, -1, labels)
            masks.append(jnp.concatenate([labels] * (BLOCK // PAIR), axis=1) == own_labels)
        keys = [k[pl.ds(start, BLOCK), :] for start in starts]
        state = []
        for head in range(2):
            highest, total, mixed = carry[head]
            scores = [
                jnp.where(inside, dot(head_mask(part, head), queries), NEG)
                for part, inside in zip(keys, masks)
            ]
            fresh = jnp.max(jnp.maximum(*scores), axis=0, keepdims=True)
            fresh = jnp.maximum(highest, fresh)
            fade = jnp.exp(highest - fresh)
            total, mixed = total * fade, mixed * fade
            for part, start in zip(scores, starts):
                chance = jnp.exp(part - fresh)
                values = v_t[head * HEAD_DIM : (head + 1) * HEAD_DIM, pl.ds(start, BLOCK)]
                total = total + jnp.sum(chance, axis=0, keepdims=True)
                mixed = mixed + dot(values, chance.astype(jnp.bfloat16))
            state.append((fresh, total, mixed))
        return tuple(state)

    one = (
        jnp.full((1, inner), NEG, jnp.float32),
        jnp.zeros((1, inner), jnp.float32),
        jnp.zeros((HEAD_DIM, inner), jnp.float32),
    )
    final = lax.fori_loop(0, (high[step] - low[step] + 1) // 2, body, (one, one))
    for head in range(2):
        highest, total, mixed = final[head]
        out_t[0, head * HEAD_DIM : (head + 1) * HEAD_DIM, :] = (mixed / total).astype(jnp.bfloat16)
        log_total[head : head + 1, :] = highest + jnp.log(total)


def backward_kernel(
    low,
    high,
    twist,
    q,
    q_t,
    g,
    g_t,
    out_t,
    log_total,
    k,
    v,
    k_t,
    own,
    others,
    *refs,
):
    result, dk_sum, dv_sum = refs[-3:]
    step = pl.program_id(0)
    per = k.shape[0] // 4 // BLOCK

    @pl.when(step == 0)
    def _():
        dk_sum[...] = jnp.zeros_like(dk_sum)
        dv_sum[...] = jnp.zeros_like(dv_sum)

    half = jnp.bfloat16
    queries_t = q_t[...]
    grads_t = g_t[0]
    own_labels = own[...]
    product = grads_t.astype(jnp.float32) * out_t[0].astype(jnp.float32)
    heads = []
    for head in range(2):
        rows = slice(head * HEAD_DIM, (head + 1) * HEAD_DIM)
        heads.append(
            (
                head_mask(q[...], head),
                head_mask(g[...], head),
                jnp.sum(product[rows], axis=0, keepdims=True),
                log_total[head : head + 1, :],
            )
        )

    def block_at(j):
        start = ((j // per) ^ twist[0]) * per + j % per
        return pl.multiple_of(start * BLOCK, BLOCK)

    def body(n, carry):
        j = low[step] + 2 * n
        later = jnp.minimum(j + 1, high[step] - 1)
        sums = list(carry)
        parts = []
        for index, extra in ((j, False), (later, later == j)):
            start = block_at(index)
            keys = k[pl.ds(start, BLOCK), :]
            values = v[pl.ds(start, BLOCK), :]
            labels = others[pl.ds(pl.multiple_of(index * BLOCK, BLOCK), BLOCK), :]
            labels = jnp.where(extra, -1, labels)
            inside = jnp.concatenate([labels] * (BLOCK // PAIR), axis=1) == own_labels
            key_part, value_part = None, None
            for head in range(2):
                own_q, own_g, within, total = heads[head]
                scores = dot(head_mask(keys, head), queries_t)
                chance = jnp.where(inside, jnp.exp(scores - total), 0.0)
                chance_grad = dot(head_mask(values, head), grads_t)
                score_grad = (chance * (chance_grad - within)).astype(half)
                value_new = dot(chance.astype(half), own_g)
                key_new = dot(score_grad, own_q)
                keys_t = k_t[head * HEAD_DIM : (head + 1) * HEAD_DIM, pl.ds(start, BLOCK)]
                sums[head] = sums[head] + dot(keys_t, score_grad)
                key_part = key_new if key_part is None else key_part + key_new
                value_part = value_new if value_part is None else value_part + value_new
            parts.append((start, key_part, value_part))
        for start, key_part, value_part in parts:
            dk_sum[pl.ds(start, BLOCK), :] += key_part
            dv_sum[pl.ds(start, BLOCK), :] += value_part
        return tuple(sums)

    zero = jnp.zeros((HEAD_DIM, own_labels.shape[1]), jnp.float32)
    first, second = lax.fori_loop(0, (high[step] - low[step] + 1) // 2, body, (zero, zero))
    both = jnp.concatenate([first, second], axis=0) * SCALE
    held = pl.multiple_of((((step // per) ^ twist[0]) * per + step % per) * BLOCK, BLOCK)
    result[pl.ds(held, BLOCK), :PAIR] = jnp.transpose(both).astype(half)

    @pl.when(step == pl.num_programs(0) - 1)
    def _():
        result[:, PAIR : 2 * PAIR] = dk_sum[...].astype(half)
        result[:, 2 * PAIR :] = dv_sum[...].astype(half)


def key_ranges(labels):
    blocks = labels.reshape(-1, BLOCK)
    first, last = blocks[:, :1], blocks[:, -1:]
    before = jnp.sum((labels[None, :] < first).astype(jnp.int32), axis=1)
    upto = jnp.sum((labels[None, :] <= last).astype(jnp.int32), axis=1)
    return before // BLOCK, (upto + BLOCK - 1) // BLOCK


def attend(pair, qkv, qkv_t, labels, wide_labels, scalars, before=()):
    length, width = qkv.shape
    pairs = width // 3 // PAIR
    row_count = length // 4
    inner = row_count // BLOCK

    def held(i, twist):
        return ((i // inner) ^ twist[0]) * inner + i % inner

    area = length * length
    return pl.pallas_call(
        forward_kernel,
        out_shape=(
            jax.ShapeDtypeStruct((4, pairs * PAIR, row_count), jnp.bfloat16),
            jax.ShapeDtypeStruct((8, length), jnp.float32),
        ),
        grid_spec=pltpu.PrefetchScalarGridSpec(
            num_scalar_prefetch=3,
            grid=(length // BLOCK,),
            in_specs=[
                pl.BlockSpec((PAIR, BLOCK), lambda i, lo, hi, tw: (3 * pair, held(i, tw))),
                pl.BlockSpec((length, PAIR), lambda i, lo, hi, tw: (0, 3 * pair + 1)),
                pl.BlockSpec((PAIR, length), lambda i, lo, hi, tw: (3 * pair + 2, 0)),
                pl.BlockSpec((1, BLOCK), lambda i, lo, hi, tw: (0, i)),
                pl.BlockSpec((length, PAIR), lambda i, lo, hi, tw: (0, 0)),
            ]
            + [pl.BlockSpec(memory_space=pl.ANY) for _ in before],
            out_specs=(
                pl.BlockSpec((1, PAIR, BLOCK), lambda i, lo, hi, tw: (i // inner, pair, i % inner)),
                pl.BlockSpec((8, BLOCK), lambda i, lo, hi, tw: (0, i)),
            ),
        ),
        input_output_aliases={8: 0} if before else {},
        compiler_params=pltpu.CompilerParams(vmem_limit_bytes=VMEM_LIMIT),
        cost_estimate=pl.CostEstimate(
            flops=area * 256 * 24, bytes_accessed=4 << 20, transcendentals=2 * area
        ),
    )(*scalars, qkv_t, qkv, qkv_t, labels, wide_labels, *before)


def attend_back(
    pair, qkv, qkv_t, labels, wide_labels, scalars, out_t, log_total, grads, grads_t, before=()
):
    length, width = grads.shape
    pairs = width // PAIR
    row_count = length // 4
    inner = row_count // BLOCK

    def held(i, twist):
        return ((i // inner) ^ twist[0]) * inner + i % inner

    area = length * length
    return pl.pallas_call(
        backward_kernel,
        out_shape=jax.ShapeDtypeStruct(qkv.shape, jnp.bfloat16),
        grid_spec=pltpu.PrefetchScalarGridSpec(
            num_scalar_prefetch=3,
            grid=(length // BLOCK,),
            in_specs=[
                pl.BlockSpec((BLOCK, PAIR), lambda i, lo, hi, tw: (held(i, tw), 3 * pair)),
                pl.BlockSpec((PAIR, BLOCK), lambda i, lo, hi, tw: (3 * pair, held(i, tw))),
                pl.BlockSpec((BLOCK, PAIR), lambda i, lo, hi, tw: (i, pair)),
                pl.BlockSpec((1, PAIR, BLOCK), lambda i, lo, hi, tw: (i // inner, pair, i % inner)),
                pl.BlockSpec((1, PAIR, BLOCK), lambda i, lo, hi, tw: (i // inner, pair, i % inner)),
                pl.BlockSpec((8, BLOCK), lambda i, lo, hi, tw: (0, i)),
                pl.BlockSpec((length, PAIR), lambda i, lo, hi, tw: (0, 3 * pair + 1)),
                pl.BlockSpec((length, PAIR), lambda i, lo, hi, tw: (0, 3 * pair + 2)),
                pl.BlockSpec((PAIR, length), lambda i, lo, hi, tw: (3 * pair + 1, 0)),
                pl.BlockSpec((1, BLOCK), lambda i, lo, hi, tw: (0, i)),
                pl.BlockSpec((length, PAIR), lambda i, lo, hi, tw: (0, 0)),
            ]
            + [pl.BlockSpec(memory_space=pl.ANY) for _ in before],
            out_specs=pl.BlockSpec((length, 3 * PAIR), lambda i, lo, hi, tw: (0, pair)),
            scratch_shapes=[
                pltpu.VMEM((length, PAIR), jnp.float32),
                pltpu.VMEM((length, PAIR), jnp.float32),
            ],
        ),
        input_output_aliases={14: 0} if before else {},
        compiler_params=pltpu.CompilerParams(vmem_limit_bytes=VMEM_LIMIT),
        cost_estimate=pl.CostEstimate(
            flops=area * 256 * 24, bytes_accessed=6 << 20, transcendentals=2 * area
        ),
    )(
        *scalars,
        qkv,
        qkv_t,
        grads,
        grads_t,
        out_t,
        log_total,
        qkv,
        qkv,
        qkv_t,
        labels,
        wide_labels,
        *before,
    )


def assemble(pieces, shapes, moves):
    count = len(shapes)

    def kernel(*refs):
        sources, rest = refs[: len(pieces)], refs[len(pieces) :]
        outs, held, arrived, left = rest[:count], rest[count : 2 * count], rest[-2], rest[-1]
        inward, outward = [], []
        for n, (piece, rows, columns, out, row, column) in enumerate(moves):
            at = (pl.ds(row, rows[1] - rows[0]), pl.ds(column, columns[1] - columns[0]))
            source = sources[piece].at[rows[0] : rows[1], columns[0] : columns[1]]
            inward.append(pltpu.make_async_copy(source, held[out].at[at], arrived.at[n]))
            outward.append(pltpu.make_async_copy(held[out].at[at], outs[out].at[at], left.at[n]))
        for copy in inward:
            copy.start()
        for copy, onward in zip(inward, outward):
            copy.wait()
            onward.start()
        for copy in outward:
            copy.wait()

    any_space = pl.BlockSpec(memory_space=pl.ANY)
    total = sum(2 * a * b for a, b in shapes)
    return pl.pallas_call(
        kernel,
        out_shape=tuple(jax.ShapeDtypeStruct(shape, jnp.bfloat16) for shape in shapes),
        in_specs=[any_space] * len(pieces),
        out_specs=(any_space,) * len(shapes),
        scratch_shapes=[pltpu.VMEM(shape, jnp.bfloat16) for shape in shapes]
        + [pltpu.SemaphoreType.DMA((len(moves),))] * 2,
        compiler_params=pltpu.CompilerParams(vmem_limit_bytes=16 << 20),
        cost_estimate=pl.CostEstimate(flops=0, bytes_accessed=2 * total, transcendentals=0),
    )(*pieces)


def projections(planes, row, late):
    _, kinds, rows, width = planes[0].shape
    pairs = width // PAIR

    def kernel(row_ref, late_ref, *refs):
        plain, scaled = refs[-2:]
        for j, plane in enumerate(refs[:-2]):
            for i in range(4):
                base = ((j // 2) ^ late_ref[0]) * 2 + j % 2
                at = pl.multiple_of((base * 4 + (i ^ row_ref[0])) * rows, rows)
                for kind in range(kinds):
                    for pair in range(pairs):
                        column = (pair * kinds + kind) * PAIR
                        part = plane[i, kind, :, pair * PAIR : (pair + 1) * PAIR]
                        plain[pl.ds(at, rows), column : column + PAIR] = part
                        if kind == 0:
                            part = part * jnp.asarray(SCALE, part.dtype)
                        scaled[pl.ds(at, rows), column : column + PAIR] = part

    shape = jax.ShapeDtypeStruct((16 * rows, kinds * width), jnp.bfloat16)
    held = pl.BlockSpec(memory_space=pltpu.VMEM)
    return pl.pallas_call(
        kernel,
        out_shape=(shape, shape),
        in_specs=[pl.BlockSpec(memory_space=pltpu.SMEM)] * 2 + [held] * 4,
        out_specs=(held, held),
        compiler_params=pltpu.CompilerParams(vmem_limit_bytes=24 << 20),
        cost_estimate=pl.CostEstimate(flops=0, bytes_accessed=6 << 20, transcendentals=0),
    )(row.reshape(1), late.reshape(1), *planes)


def swap(values):
    return lax.ppermute(values, "col", [(0, 1), (1, 0)])


def flip(values, axis, bit, size=4):
    return lax.ppermute(values, axis, [(i, i ^ bit) for i in range(size)])


def pick(values, index, axis=0):
    return lax.dynamic_index_in_dim(values, index, axis, keepdims=False)


def together(*values):
    return lax.optimization_barrier(values)


def gather_start(block):
    rows = block.shape[0] // 2
    top, low = block[:rows], block[rows:]
    return top, low, flip(top, "dp", 1), flip(low, "dp", 2)


def gather_second(state):
    top, low, top_x, low_y = state
    top_y = flip(jnp.concatenate([top, top_x]), "dp", 2)
    low_x = flip(jnp.concatenate([low, low_y]), "dp", 1)
    return top_y, low_x


def gather_end(state, second, parts):
    pieces = (*state, *second)
    rows = pieces[0].shape[0]
    whole, head, tail = (0, rows), (0, rows), (rows, 2 * rows)
    order = ((0, whole), (1, whole), (2, whole), (5, head), (4, head), (3, whole), (4, tail), (5, tail))
    moves = [
        (piece, span, part, n, place * rows, 0)
        for place, (piece, span) in enumerate(order)
        for n, part in enumerate(parts)
    ]
    return assemble(pieces, [(8 * rows, stop - start) for start, stop in parts], moves)


def scatter_split(*grads):
    rows = grads[0].shape[0] // 8
    moves, column = [], 0
    order = (((0, 0),), ((1, 0),), ((0, 1),), ((2, 1),), ((2, 0), (3, 0)), ((1, 1), (3, 1)))
    for piece, array in enumerate(grads):
        columns = array.shape[1]
        for out, parts in enumerate(order):
            for place, (block, second) in enumerate(parts):
                at = (2 * block + second) * rows
                moves.append((piece, (at, at + rows), (0, columns), out, place * rows, column))
        column += columns
    shapes = [(len(parts) * rows, column) for parts in order]
    return assemble(grads, shapes, moves)


def scatter_start(parts):
    *kept, send_y, send_x = parts
    return *kept, flip(send_y, "dp", 2), flip(send_x, "dp", 1)


def scatter_second(state):
    f32, half = jnp.float32, jnp.bfloat16
    top, top_pass, low, low_pass, top_y, low_x = state
    rows = top.shape[0]
    top_x = flip((top_pass.astype(f32) + top_y[rows:].astype(f32)).astype(half), "dp", 1)
    low_y = flip((low_pass.astype(f32) + low_x[rows:].astype(f32)).astype(half), "dp", 2)
    return top_x, low_y


def scatter_end(state, second):
    f32, half = jnp.float32, jnp.bfloat16
    top, _, low, _, top_y, low_x = state
    top_x, low_y = second
    rows = top.shape[0]
    top = top.astype(f32) + top_y[:rows].astype(f32) + top_x.astype(f32)
    low = low.astype(f32) + low_x[:rows].astype(f32) + low_y.astype(f32)
    return jnp.concatenate([top, low]).astype(half)


def whole_norm(summed, gain, shift):
    average = jnp.mean(summed, axis=-1, keepdims=True)
    spread = jnp.mean(summed * summed, axis=-1, keepdims=True) - average * average
    scaling = lax.rsqrt(spread + EPS)
    normed = (summed - average) * scaling
    return (normed * gain + shift, normed, scaling)


def whole_norm_back(upstream, normed, scaling, gain):
    scaled = upstream * gain
    offset = jnp.mean(scaled, axis=-1, keepdims=True)
    slope = jnp.mean(scaled * normed, axis=-1, keepdims=True)
    return scaling * (scaled - offset - normed * slope)


def fast_local(
    tokens,
    segment,
    w_query,
    w_key,
    w_value,
    w_out,
    w_up,
    w_down,
    inner_gain,
    inner_shift,
    outer_gain,
    outer_shift,
    cotangent,
):
    f32 = jnp.float32
    half = jnp.bfloat16
    me = lax.axis_index("dp")
    core = lax.axis_index("col")
    row = lax.axis_index("row")
    which, parity = row // 2, row % 2
    first_core = core == 0
    crossed = me % 2 == 1
    leading = core == me // 2
    row_count = tokens.shape[1]
    length = segment.shape[1]
    block_rows, half_width = w_query.shape
    width = D // 4
    hidden_half = w_up.shape[1]
    stack, cat = jnp.stack, jnp.concatenate

    def turn(values):
        left, right = values[..., :width], values[..., width:]
        return jnp.where(crossed, cat([right, left], axis=-1), values)

    def merge(mine, other):
        return jnp.where(leading, cat([mine, other], axis=-1), cat([other, mine], axis=-1))

    def divide(values):
        left, right = values[..., :half_width], values[..., half_width:]
        return jnp.where(leading, left, right), jnp.where(leading, right, left)

    def by_core(mine, other):
        return jnp.where(first_core, stack([mine, other]), stack([other, mine]))

    tokens = turn(tokens)
    near_0 = pick(tokens, which)
    near_2 = flip(pick(tokens, 1 - which), "row", 2)
    near_1 = flip(near_0, "row", 1)
    own_tokens = merge(pick(tokens, core), swap(pick(tokens, 1 - core)))
    labels = pick(segment, which)
    scalars = (*key_ranges(labels), row.reshape(1))
    wide_labels = jnp.broadcast_to(labels[:, None], (length, PAIR))
    labels = labels[None]

    thirds = stack([w_query, w_key, w_value]).reshape(3, block_rows, 2, width)
    blocks = by_core(pick(thirds, core, 2), swap(pick(thirds, 1 - core, 2)))
    same, cross = pick(blocks, parity), pick(blocks, 1 - parity)
    near = [same] + [flip(same if bit == 2 else cross, "row", bit) for bit in (1, 2, 3)]
    odd = row % 2 == 1
    strips = stack(near)
    packed, plain_down, near_1, near_2, strips = together(
        cat([w_out, w_up], axis=1), w_down, near_1, near_2, strips
    )
    near_3 = flip(near_2, "row", 1)
    out_up_rows = lax.all_gather(packed, "row", axis=0, tiled=True)
    down_rows = lax.all_gather(plain_down, "row", axis=0, tiled=True)
    out_up = gather_start(out_up_rows)
    planes = [strips] + [flip(strips, "dp", bit) for bit in (1, 2, 3)]
    near_3, planes = together(near_3, planes)
    pieces = [near_0, near_1, near_2, near_3]
    pieces += [swap(piece) for piece in pieces]
    whole = (0, row_count), (0, half_width)
    (series,) = assemble(
        pieces,
        [(length, D)],
        [(n, *whole, 0, n % 4 * row_count, n // 4 * half_width) for n in range(8)],
    )
    w_qkv, w_scaled = projections(planes, row, core ^ (me // 2))
    w_mine, w_other = w_qkv[:half_width], w_qkv[half_width:]

    vectors = turn(stack([inner_gain, inner_shift, outer_gain, outer_shift]))
    vectors = merge(vectors, swap(vectors))
    inner_gain, inner_shift, outer_gain, outer_shift = (vectors[i : i + 1] for i in range(4))
    cotangent = turn(cotangent)
    upstream = merge(pick(cotangent, core), swap(pick(cotangent, 1 - core)))

    qkv = dot(series, w_scaled).astype(half)
    qkv_t = qkv.T
    out_0, total_0 = attend(0, qkv, qkv_t, labels, wide_labels, scalars)
    scalars_1, out_up, out_0 = together(scalars, out_up, out_0)
    out_t, total_1 = attend(1, qkv, qkv_t, labels, wide_labels, scalars_1, (out_0,))
    out_up_second = gather_second(out_up)
    down_first = gather_start(down_rows)
    down_second = gather_second(down_first)
    out_t, out_up_second = together(out_t, out_up_second)
    mixed = lax.all_to_all(out_t, "row", 0, 0, tiled=True)
    out_half, up = gather_end(
        out_up, out_up_second, ((0, half_width), (half_width, half_width + hidden_half))
    )
    full_out = cat([out_half, swap(out_half)], axis=1)
    mixed, down_second = together(mixed, down_second)
    (down,) = gather_end(down_first, down_second, ((0, hidden_half),))
    mixed = mixed.reshape(2, 2, width, row_count)
    kept, passed = pick(mixed, core), swap(pick(mixed, 1 - core))
    mixture_t = jnp.where(
        first_core,
        cat([kept[0], passed[0], kept[1], passed[1]]),
        cat([passed[1], kept[1], passed[0], kept[0]]),
    )

    summed = own_tokens.astype(f32) + jnp.einsum(
        "eq,de->qd", mixture_t, full_out, preferred_element_type=f32
    )
    middle, inner_normed, inner_scaling = whole_norm(summed, inner_gain, inner_shift)

    middle_own = middle.astype(half)
    middle_other = swap(middle_own)
    hidden_own = dot(middle_own, up)
    hidden_other = dot(middle_other, up)
    active_own = gelu_value(hidden_own).astype(half)
    active_other = gelu_value(hidden_other).astype(half)
    down_other = jnp.einsum("qf,df->qd", active_other, down, preferred_element_type=f32)
    down_swapped = swap(down_other.astype(half))
    down_own = jnp.einsum("qf,df->qd", active_own, down, preferred_element_type=f32)
    second_sum = middle + (down_own + down_swapped.astype(f32))
    result, outer_normed, outer_scaling = whole_norm(second_sum, outer_gain, outer_shift)
    kept, passed = divide(result.astype(half))
    layer_out = turn(by_core(kept, swap(passed)))

    outer_gain_grad = jnp.sum(upstream * outer_normed, axis=0)
    outer_shift_grad = jnp.sum(upstream, axis=0)
    second_grad = whole_norm_back(upstream, outer_normed, outer_scaling, outer_gain)
    second_own = second_grad.astype(half)
    second_other = swap(second_own)

    def weight_grad(left, right):
        return jnp.einsum("qd,qf->df", left, right, preferred_element_type=f32)

    grad_down = weight_grad(second_own, active_own) + weight_grad(second_other, active_other)
    down_parts = scatter_split(grad_down.astype(half))
    down_parts, second_own, second_other = together(down_parts, second_own, second_other)
    down_first = scatter_start(down_parts)
    active_grad_own = (dot(second_own, down) * gelu_slope(hidden_own)).astype(half)
    active_grad_other = (dot(second_other, down) * gelu_slope(hidden_other)).astype(half)
    middle_grad_other = jnp.einsum("qf,df->qd", active_grad_other, up, preferred_element_type=f32)
    middle_swapped = swap(middle_grad_other.astype(half))
    middle_swapped, down_first = together(middle_swapped, down_first)
    middle_grad_own = jnp.einsum("qf,df->qd", active_grad_own, up, preferred_element_type=f32)

    middle_grad = second_grad + (middle_grad_own + middle_swapped.astype(f32))
    inner_gain_grad = jnp.sum(middle_grad * inner_normed, axis=0)
    inner_shift_grad = jnp.sum(middle_grad, axis=0)
    summed_grad = whole_norm_back(middle_grad, inner_normed, inner_scaling, inner_gain)
    summed_half = summed_grad.astype(half)
    grads_t = jnp.einsum("qd,de->eq", summed_half, full_out, preferred_element_type=f32)
    grads_t = grads_t.astype(half).reshape(4, width, row_count)
    kept = jnp.where(
        first_core, stack([grads_t[0], grads_t[2]]), stack([grads_t[3], grads_t[1]])
    )
    passed = jnp.where(
        first_core, stack([grads_t[1], grads_t[3]]), stack([grads_t[2], grads_t[0]])
    )
    grads_t = by_core(kept, swap(passed)).reshape(4, width, row_count)
    down_second = scatter_second(down_first)
    grads_t, down_second = together(grads_t, down_second)
    grads_t = lax.all_to_all(grads_t, "row", 0, 0, tiled=True)

    grad_up = weight_grad(middle_own, active_grad_own) + weight_grad(
        middle_other, active_grad_other
    )
    grad_out = jnp.einsum("qd,eq->de", summed_half, mixture_t, preferred_element_type=f32)
    grad_out = grad_out[:, :half_width] + swap(grad_out[:, half_width:].astype(half)).astype(f32)
    out_up_parts = scatter_split(grad_out.astype(half), grad_up.astype(half))
    kept, passed = divide(summed_grad)
    base = turn(by_core(kept, swap(passed)))
    out_up_first = scatter_start(out_up_parts)
    grads_t, down_second, out_up_first = together(grads_t, down_second, out_up_first)
    grads = grads_t.transpose(0, 2, 1).reshape(length, width)
    qkv_grad = attend_back(
        0, qkv, qkv_t, labels, wide_labels, scalars, out_t, total_0, grads, grads_t
    )
    grad_down = lax.psum_scatter(
        scatter_end(down_first, down_second), "row", scatter_dimension=0, tiled=True
    )
    out_up_second = scatter_second(out_up_first)
    out_up_plane = scatter_end(out_up_first, out_up_second)
    scalars_1, grad_down, out_up_plane, qkv_grad, base, layer_out = together(
        scalars, grad_down, out_up_plane, qkv_grad, base, layer_out
    )
    out_up_grad = lax.psum_scatter(out_up_plane, "row", scatter_dimension=0, tiled=True)
    qkv_grad = attend_back(
        1, qkv, qkv_t, labels, wide_labels, scalars_1, out_t, total_1, grads, grads_t, (qkv_grad,)
    )
    qkv_grad, out_up_grad = together(qkv_grad, out_up_grad)
    grad_down, out_up_grad = grad_down.astype(f32), out_up_grad.astype(f32)
    grad_out, grad_up = out_up_grad[:, :half_width], out_up_grad[:, half_width:]

    def back_part(rows):
        return jnp.einsum("le,de->ld", qkv_grad, rows, preferred_element_type=f32)

    back_other = swap(back_part(w_other).astype(half))
    norm_local = stack([inner_gain_grad, inner_shift_grad, outer_gain_grad, outer_shift_grad])
    back = back_part(w_mine) + back_other.astype(f32)
    back = back.reshape(4, row_count, half_width)
    pass_on = turn(back[2] + flip(back[3].astype(half), "row", 1).astype(f32)).astype(half)
    pass_on, qkv_grad, norm_local = together(pass_on, qkv_grad, norm_local)
    from_far = flip(pass_on, "row", 2)
    from_near = turn(back[0] + flip(back[1].astype(half), "row", 1).astype(f32))
    slot = jnp.arange(2).reshape(2, 1, 1)
    base = base + jnp.where(slot == which, from_near[None], 0.0)

    grads = jnp.einsum("ld,le->de", series, qkv_grad, preferred_element_type=f32)
    grads_mine, grads_other = grads[:half_width], grads[half_width:]

    def plane_part(j):
        rows = slice((j % 2) * width, (j % 2 + 1) * width)
        if j < 2:
            return jnp.where(leading, grads_mine[rows], grads_other[rows])
        return jnp.where(leading, grads_other[rows], grads_mine[rows])

    arrived = [flip(plane_part(bit).astype(half), "dp", bit) for bit in (1, 2, 3)]
    arrived, base, from_far = together(arrived, base, from_far)
    total = plane_part(0)
    for part in arrived:
        total = total + part.astype(f32)
    total = total.reshape(4, block_rows, 3 * width)
    sends = tuple(pick(total, row ^ bit).astype(half) for bit in (1, 2, 3))
    near_1, near_2, near_3 = (flip(part, "row", bit) for bit, part in zip((1, 2, 3), sends))
    own_part = (pick(total, row) + near_2.astype(f32)).astype(half)
    other_part = (near_1.astype(f32) + near_3.astype(f32)).astype(half)
    strip = jnp.where(odd, stack([other_part, own_part]), stack([own_part, other_part]))
    kept, passed = pick(strip, core), swap(pick(strip, 1 - core))

    def by_kind(values):
        values = values.reshape(block_rows, width // PAIR, 3, PAIR).transpose(2, 0, 1, 3)
        return values.reshape(3, block_rows, width)

    kept, passed = by_kind(kept), by_kind(passed)
    qkv_grads = jnp.where(first_core, cat([kept, passed], axis=2), cat([passed, kept], axis=2))
    qkv_grads = qkv_grads.astype(f32)

    input_grad = base + jnp.where(slot == which, 0.0, from_far[None].astype(f32))

    kept, passed = divide(norm_local)
    norm_grads = turn(kept + swap(passed))
    for axis in ("row", "dp"):
        one, two, three = (flip(norm_grads, axis, bit) for bit in (1, 2, 3))
        norm_grads = (norm_grads + one) + (two + three)
    return (
        layer_out,
        input_grad,
        qkv_grads[0],
        qkv_grads[1],
        qkv_grads[2],
        grad_out,
        grad_up,
        grad_down,
        norm_grads,
    )


def solution(mesh):
    placed = (
        P("dp", "row", "col"),
        P("dp", None),
        P(("dp", "row"), "col"),
        P(("dp", "row"), "col"),
        P(("dp", "row"), "col"),
        P(("dp", "row"), "col"),
        P(("dp", "row"), "col"),
        P(("dp", "row"), "col"),
        P("col"),
        P("col"),
        P("col"),
        P("col"),
        P("dp", "row", "col"),
    )
    body = fast_local if fits(mesh) else local
    return jax.shard_map(
        body,
        mesh=mesh,
        in_specs=placed,
        out_specs=(
            P("dp", "row", "col"),
            P("dp", "row", "col"),
            P(("dp", "row"), "col"),
            P(("dp", "row"), "col"),
            P(("dp", "row"), "col"),
            P(("dp", "row"), "col"),
            P(("dp", "row"), "col"),
            P(("dp", "row"), "col"),
            P(None, "col"),
        ),
        check_vma=False,
    )
```

```python
import jax
import jax.numpy as jnp
from jax import lax
from jax.experimental import pallas as pl
from jax.experimental.pallas import tpu as pltpu
from jax.sharding import PartitionSpec as P

D = 1024
HEAD_DIM = 64


EPS = 1e-05
ROOT_HALF = 0.7071067811865476
INV_ROOT_TAU = 0.3989422804014327


def gelu_value(inputs):
    return 0.5 * inputs * (1.0 + lax.erf(inputs * ROOT_HALF))


def gelu_slope(inputs):
    return (
        0.5 * (1.0 + lax.erf(inputs * ROOT_HALF))
        + inputs * jnp.exp(-0.5 * inputs * inputs) * INV_ROOT_TAU
    )


def widen(values):
    return lax.all_gather(values, "col", axis=2, tiled=True)


def narrow(partial_value):
    return lax.psum_scatter(partial_value, "col", scatter_dimension=2, tiled=True)


def norm_forward(summed, norm_gain, norm_shift):
    row_sums, squares = lax.psum(
        (jnp.sum(summed, axis=-1, keepdims=True), jnp.sum(summed * summed, axis=-1, keepdims=True)),
        "col",
    )
    average = row_sums / D
    spread = squares / D - average * average
    scaling = lax.rsqrt(spread + EPS)
    normed = (summed - average) * scaling
    return (normed * norm_gain + norm_shift, normed, scaling)


def norm_backward(upstream, normed, scaling, norm_gain):
    scaled = upstream * norm_gain
    offset_sum, slope_sum = lax.psum(
        (jnp.sum(scaled, axis=-1, keepdims=True), jnp.sum(scaled * normed, axis=-1, keepdims=True)),
        "col",
    )
    return scaling * (scaled - offset_sum / D - normed * (slope_sum / D))


def head_view(values):
    return values.reshape(values.shape[0], values.shape[1] // HEAD_DIM, HEAD_DIM)


def masked_scores(queries, key_rows, own_labels, all_labels):
    scores = jnp.einsum(
        "qhe,khe->hqk", head_view(queries), head_view(key_rows), preferred_element_type=jnp.float32
    ) * HEAD_DIM ** (-0.5)
    inside = own_labels[:, None] == all_labels[None, :]
    return jnp.where(inside[None], scores, -jnp.inf)


def attend_forward(inputs):
    queries, key_rows, value_rows, own_labels, all_labels = inputs
    scores = masked_scores(queries, key_rows, own_labels, all_labels)
    highest = jnp.max(scores, axis=-1, keepdims=True)
    log_total = highest + jnp.log(jnp.sum(jnp.exp(scores - highest), axis=-1, keepdims=True))
    attention = jnp.exp(scores - log_total).astype(jnp.bfloat16)
    mixture = jnp.einsum(
        "hqk,khe->qhe", attention, head_view(value_rows), preferred_element_type=jnp.float32
    )
    return (mixture.reshape(queries.shape).astype(jnp.bfloat16), log_total)


def attend_backward(inputs):
    queries, key_rows, value_rows, own_labels, all_labels, log_total, mixture_grad = inputs
    scores = masked_scores(queries, key_rows, own_labels, all_labels)
    chance = jnp.exp(scores - log_total)
    attention = chance.astype(jnp.bfloat16)
    chance_grad = jnp.einsum(
        "qhe,khe->hqk",
        head_view(mixture_grad),
        head_view(value_rows),
        preferred_element_type=jnp.float32,
    )
    within = jnp.sum(chance * chance_grad, axis=-1, keepdims=True)
    score_grad = (chance * (chance_grad - within) * HEAD_DIM ** (-0.5)).astype(jnp.bfloat16)
    query_grad = jnp.einsum(
        "hqk,khe->qhe", score_grad, head_view(key_rows), preferred_element_type=jnp.float32
    )
    key_part = jnp.einsum(
        "hqk,qhe->khe", score_grad, head_view(queries), preferred_element_type=jnp.float32
    )
    value_part = jnp.einsum(
        "hqk,qhe->khe", attention, head_view(mixture_grad), preferred_element_type=jnp.float32
    )
    return (
        query_grad.reshape(queries.shape).astype(jnp.bfloat16),
        key_part.reshape(key_rows.shape),
        value_part.reshape(value_rows.shape),
    )


def local(
    tokens,
    segment,
    w_query,
    w_key,
    w_value,
    w_out,
    w_up,
    w_down,
    inner_gain,
    inner_shift,
    outer_gain,
    outer_shift,
    cotangent,
):
    f32 = jnp.float32
    half = jnp.bfloat16
    gathered = (
        lax.all_gather(w_query, ("dp", "row"), axis=0, tiled=True),
        lax.all_gather(w_key, ("dp", "row"), axis=0, tiled=True),
        lax.all_gather(w_value, ("dp", "row"), axis=0, tiled=True),
        lax.all_gather(w_out, ("dp", "row"), axis=0, tiled=True),
        lax.all_gather(w_up, ("dp", "row"), axis=0, tiled=True),
        lax.all_gather(w_down, ("dp", "row"), axis=0, tiled=True),
    )
    full_query, full_key, full_value, full_out, full_up, full_down = gathered
    row_count = tokens.shape[1]
    own_labels = lax.dynamic_slice_in_dim(segment, lax.axis_index("row") * row_count, row_count, 1)
    wide_tokens = widen(tokens)
    queries = jnp.einsum("sqd,de->sqe", wide_tokens, full_query, preferred_element_type=f32).astype(
        half
    )
    key_rows = jnp.einsum("sqd,de->sqe", wide_tokens, full_key, preferred_element_type=f32).astype(
        half
    )
    value_rows = jnp.einsum(
        "sqd,de->sqe", wide_tokens, full_value, preferred_element_type=f32
    ).astype(half)
    all_keys, all_values = (
        lax.all_gather(key_rows, "row", axis=1, tiled=True),
        lax.all_gather(value_rows, "row", axis=1, tiled=True),
    )
    mixture, log_total = lax.map(
        attend_forward, (queries, all_keys, all_values, own_labels, segment)
    )
    summed = tokens.astype(f32) + narrow(
        jnp.einsum("sqe,de->sqd", mixture, full_out, preferred_element_type=f32)
    )
    middle, inner_normed, inner_scaling = norm_forward(summed, inner_gain, inner_shift)
    wide_middle = widen(middle.astype(half))
    hidden = jnp.einsum("sqd,df->sqf", wide_middle, full_up, preferred_element_type=f32)
    active = gelu_value(hidden).astype(half)
    second_sum = middle + narrow(
        jnp.einsum("sqf,df->sqd", active, full_down, preferred_element_type=f32)
    )
    result, outer_normed, outer_scaling = norm_forward(second_sum, outer_gain, outer_shift)
    layer_out = result.astype(half)
    outer_gain_grad = jnp.sum(cotangent * outer_normed, axis=(0, 1))
    outer_shift_grad = jnp.sum(cotangent, axis=(0, 1))
    second_grad = norm_backward(cotangent, outer_normed, outer_scaling, outer_gain)
    wide_second = widen(second_grad.astype(half))
    grad_down = jnp.einsum("sqd,sqf->df", wide_second, active, preferred_element_type=f32)
    active_grad = (
        jnp.einsum("sqd,df->sqf", wide_second, full_down, preferred_element_type=f32)
        * gelu_slope(hidden)
    ).astype(half)
    grad_up = jnp.einsum("sqd,sqf->df", wide_middle, active_grad, preferred_element_type=f32)
    middle_grad = second_grad + narrow(
        jnp.einsum("sqf,df->sqd", active_grad, full_up, preferred_element_type=f32)
    )
    inner_gain_grad = jnp.sum(middle_grad * inner_normed, axis=(0, 1))
    inner_shift_grad = jnp.sum(middle_grad, axis=(0, 1))
    summed_grad = norm_backward(middle_grad, inner_normed, inner_scaling, inner_gain)
    wide_summed = widen(summed_grad.astype(half))
    grad_out = jnp.einsum("sqd,sqe->de", wide_summed, mixture, preferred_element_type=f32)
    mixture_grad = jnp.einsum(
        "sqd,de->sqe", wide_summed, full_out, preferred_element_type=f32
    ).astype(half)
    query_grad, key_part, value_part = lax.map(
        attend_backward,
        (queries, all_keys, all_values, own_labels, segment, log_total, mixture_grad),
    )
    key_sums, value_sums = (
        lax.psum_scatter(key_part, "row", scatter_dimension=1, tiled=True),
        lax.psum_scatter(value_part, "row", scatter_dimension=1, tiled=True),
    )
    key_grad = key_sums.astype(half)
    value_grad = value_sums.astype(half)
    grad_query = jnp.einsum("sqd,sqe->de", wide_tokens, query_grad, preferred_element_type=f32)
    grad_key = jnp.einsum("sqd,sqe->de", wide_tokens, key_grad, preferred_element_type=f32)
    grad_value = jnp.einsum("sqd,sqe->de", wide_tokens, value_grad, preferred_element_type=f32)
    back_sum = jnp.einsum("sqe,de->sqd", query_grad, full_query, preferred_element_type=f32)
    back_sum = back_sum + jnp.einsum("sqe,de->sqd", key_grad, full_key, preferred_element_type=f32)
    back_sum = back_sum + jnp.einsum(
        "sqe,de->sqd", value_grad, full_value, preferred_element_type=f32
    )
    input_grad = summed_grad + narrow(back_sum)
    norm_local = jnp.stack([inner_gain_grad, inner_shift_grad, outer_gain_grad, outer_shift_grad])
    weight_grads = (
        lax.psum_scatter(grad_query, ("dp", "row"), scatter_dimension=0, tiled=True),
        lax.psum_scatter(grad_key, ("dp", "row"), scatter_dimension=0, tiled=True),
        lax.psum_scatter(grad_value, ("dp", "row"), scatter_dimension=0, tiled=True),
        lax.psum_scatter(grad_out, ("dp", "row"), scatter_dimension=0, tiled=True),
        lax.psum_scatter(grad_up, ("dp", "row"), scatter_dimension=0, tiled=True),
        lax.psum_scatter(grad_down, ("dp", "row"), scatter_dimension=0, tiled=True),
    )
    norm_grads = lax.psum(norm_local, ("dp", "row"))
    return (
        layer_out,
        input_grad,
        weight_grads[0],
        weight_grads[1],
        weight_grads[2],
        weight_grads[3],
        weight_grads[4],
        weight_grads[5],
        norm_grads,
    )


PAIR = 128
BLOCK = 256
NEG = -1e30
HEADS = 16
SCALE = HEAD_DIM ** (-0.5)
VMEM_LIMIT = 48 << 20


def fits(mesh):
    sizes = dict(mesh.shape)
    return sizes["col"] == 2 and sizes["dp"] == 4 and sizes["row"] == 4


def head_mask(values, head):
    lane = lax.broadcasted_iota(jnp.int32, values.shape, 1)
    keep = (lane < HEAD_DIM) if head == 0 else (lane >= HEAD_DIM)
    return jnp.where(keep, values, jnp.zeros_like(values))


def dot(left, right):
    return jnp.dot(left, right, preferred_element_type=jnp.float32)


def forward_kernel(low, high, twist, q_t, k, v_t, own, others, *refs):
    out_t, log_total = refs[-2:]
    step = pl.program_id(0)
    queries = q_t[...]
    own_labels = own[...]
    inner = out_t.shape[2]
    per = k.shape[0] // 4 // BLOCK

    def block_at(j):
        start = ((j // per) ^ twist[0]) * per + j % per
        return pl.multiple_of(start * BLOCK, BLOCK)

    def body(n, carry):
        j = low[step] + 2 * n
        later = jnp.minimum(j + 1, high[step] - 1)
        starts = block_at(j), block_at(later)
        masks = []
        for index, extra in ((j, False), (later, later == j)):
            labels = others[pl.ds(pl.multiple_of(index * BLOCK, BLOCK), BLOCK), :]
            labels = jnp.where(extra, -1, labels)
            masks.append(jnp.concatenate([labels] * (BLOCK // PAIR), axis=1) == own_labels)
        keys = [k[pl.ds(start, BLOCK), :] for start in starts]
        state = []
        for head in range(2):
            highest, total, mixed = carry[head]
            scores = [
                jnp.where(inside, dot(head_mask(part, head), queries), NEG)
                for part, inside in zip(keys, masks)
            ]
            fresh = jnp.max(jnp.maximum(*scores), axis=0, keepdims=True)
            fresh = jnp.maximum(highest, fresh)
            fade = jnp.exp(highest - fresh)
            total, mixed = total * fade, mixed * fade
            for part, start in zip(scores, starts):
                chance = jnp.exp(part - fresh)
                values = v_t[head * HEAD_DIM : (head + 1) * HEAD_DIM, pl.ds(start, BLOCK)]
                total = total + jnp.sum(chance, axis=0, keepdims=True)
                mixed = mixed + dot(values, chance.astype(jnp.bfloat16))
            state.append((fresh, total, mixed))
        return tuple(state)

    one = (
        jnp.full((1, inner), NEG, jnp.float32),
        jnp.zeros((1, inner), jnp.float32),
        jnp.zeros((HEAD_DIM, inner), jnp.float32),
    )
    final = lax.fori_loop(0, (high[step] - low[step] + 1) // 2, body, (one, one))
    for head in range(2):
        highest, total, mixed = final[head]
        out_t[0, head * HEAD_DIM : (head + 1) * HEAD_DIM, :] = (mixed / total).astype(jnp.bfloat16)
        log_total[head : head + 1, :] = highest + jnp.log(total)


def backward_kernel(
    low,
    high,
    twist,
    q,
    q_t,
    g,
    g_t,
    out_t,
    log_total,
    k,
    v,
    k_t,
    own,
    others,
    *refs,
):
    result, dk_sum, dv_sum = refs[-3:]
    step = pl.program_id(0)
    per = k.shape[0] // 4 // BLOCK

    @pl.when(step == 0)
    def _():
        dk_sum[...] = jnp.zeros_like(dk_sum)
        dv_sum[...] = jnp.zeros_like(dv_sum)

    half = jnp.bfloat16
    queries_t = q_t[...]
    grads_t = g_t[0]
    own_labels = own[...]
    product = grads_t.astype(jnp.float32) * out_t[0].astype(jnp.float32)
    heads = []
    for head in range(2):
        rows = slice(head * HEAD_DIM, (head + 1) * HEAD_DIM)
        heads.append(
            (
                head_mask(q[...], head),
                head_mask(g[...], head),
                jnp.sum(product[rows], axis=0, keepdims=True),
                log_total[head : head + 1, :],
            )
        )

    def block_at(j):
        start = ((j // per) ^ twist[0]) * per + j % per
        return pl.multiple_of(start * BLOCK, BLOCK)

    def body(n, carry):
        j = low[step] + 2 * n
        later = jnp.minimum(j + 1, high[step] - 1)
        sums = list(carry)
        parts = []
        for index, extra in ((j, False), (later, later == j)):
            start = block_at(index)
            keys = k[pl.ds(start, BLOCK), :]
            values = v[pl.ds(start, BLOCK), :]
            labels = others[pl.ds(pl.multiple_of(index * BLOCK, BLOCK), BLOCK), :]
            labels = jnp.where(extra, -1, labels)
            inside = jnp.concatenate([labels] * (BLOCK // PAIR), axis=1) == own_labels
            key_part, value_part = None, None
            for head in range(2):
                own_q, own_g, within, total = heads[head]
                scores = dot(head_mask(keys, head), queries_t)
                chance = jnp.where(inside, jnp.exp(scores - total), 0.0)
                chance_grad = dot(head_mask(values, head), grads_t)
                score_grad = (chance * (chance_grad - within)).astype(half)
                value_new = dot(chance.astype(half), own_g)
                key_new = dot(score_grad, own_q)
                keys_t = k_t[head * HEAD_DIM : (head + 1) * HEAD_DIM, pl.ds(start, BLOCK)]
                sums[head] = sums[head] + dot(keys_t, score_grad)
                key_part = key_new if key_part is None else key_part + key_new
                value_part = value_new if value_part is None else value_part + value_new
            parts.append((start, key_part, value_part))
        for start, key_part, value_part in parts:
            dk_sum[pl.ds(start, BLOCK), :] += key_part
            dv_sum[pl.ds(start, BLOCK), :] += value_part
        return tuple(sums)

    zero = jnp.zeros((HEAD_DIM, own_labels.shape[1]), jnp.float32)
    first, second = lax.fori_loop(0, (high[step] - low[step] + 1) // 2, body, (zero, zero))
    both = jnp.concatenate([first, second], axis=0) * SCALE
    held = pl.multiple_of((((step // per) ^ twist[0]) * per + step % per) * BLOCK, BLOCK)
    result[pl.ds(held, BLOCK), :PAIR] = jnp.transpose(both).astype(half)

    @pl.when(step == pl.num_programs(0) - 1)
    def _():
        result[:, PAIR : 2 * PAIR] = dk_sum[...].astype(half)
        result[:, 2 * PAIR :] = dv_sum[...].astype(half)


def key_ranges(labels):
    blocks = labels.reshape(-1, BLOCK)
    first, last = blocks[:, :1], blocks[:, -1:]
    before = jnp.sum((labels[None, :] < first).astype(jnp.int32), axis=1)
    upto = jnp.sum((labels[None, :] <= last).astype(jnp.int32), axis=1)
    return before // BLOCK, (upto + BLOCK - 1) // BLOCK


def attend(pair, qkv, qkv_t, labels, wide_labels, scalars, before=()):
    length, width = qkv.shape
    pairs = width // 3 // PAIR
    row_count = length // 4
    inner = row_count // BLOCK

    def held(i, twist):
        return ((i // inner) ^ twist[0]) * inner + i % inner

    area = length * length
    return pl.pallas_call(
        forward_kernel,
        out_shape=(
            jax.ShapeDtypeStruct((4, pairs * PAIR, row_count), jnp.bfloat16),
            jax.ShapeDtypeStruct((8, length), jnp.float32),
        ),
        grid_spec=pltpu.PrefetchScalarGridSpec(
            num_scalar_prefetch=3,
            grid=(length // BLOCK,),
            in_specs=[
                pl.BlockSpec((PAIR, BLOCK), lambda i, lo, hi, tw: (3 * pair, held(i, tw))),
                pl.BlockSpec((length, PAIR), lambda i, lo, hi, tw: (0, 3 * pair + 1)),
                pl.BlockSpec((PAIR, length), lambda i, lo, hi, tw: (3 * pair + 2, 0)),
                pl.BlockSpec((1, BLOCK), lambda i, lo, hi, tw: (0, i)),
                pl.BlockSpec((length, PAIR), lambda i, lo, hi, tw: (0, 0)),
            ]
            + [pl.BlockSpec(memory_space=pl.ANY) for _ in before],
            out_specs=(
                pl.BlockSpec((1, PAIR, BLOCK), lambda i, lo, hi, tw: (i // inner, pair, i % inner)),
                pl.BlockSpec((8, BLOCK), lambda i, lo, hi, tw: (0, i)),
            ),
        ),
        input_output_aliases={8: 0} if before else {},
        compiler_params=pltpu.CompilerParams(vmem_limit_bytes=VMEM_LIMIT),
        cost_estimate=pl.CostEstimate(
            flops=area * 256 * 24, bytes_accessed=4 << 20, transcendentals=2 * area
        ),
    )(*scalars, qkv_t, qkv, qkv_t, labels, wide_labels, *before)


def attend_back(
    pair, qkv, qkv_t, labels, wide_labels, scalars, out_t, log_total, grads, grads_t, before=()
):
    length, width = grads.shape
    pairs = width // PAIR
    row_count = length // 4
    inner = row_count // BLOCK

    def held(i, twist):
        return ((i // inner) ^ twist[0]) * inner + i % inner

    area = length * length
    return pl.pallas_call(
        backward_kernel,
        out_shape=jax.ShapeDtypeStruct(qkv.shape, jnp.bfloat16),
        grid_spec=pltpu.PrefetchScalarGridSpec(
            num_scalar_prefetch=3,
            grid=(length // BLOCK,),
            in_specs=[
                pl.BlockSpec((BLOCK, PAIR), lambda i, lo, hi, tw: (held(i, tw), 3 * pair)),
                pl.BlockSpec((PAIR, BLOCK), lambda i, lo, hi, tw: (3 * pair, held(i, tw))),
                pl.BlockSpec((BLOCK, PAIR), lambda i, lo, hi, tw: (i, pair)),
                pl.BlockSpec((1, PAIR, BLOCK), lambda i, lo, hi, tw: (i // inner, pair, i % inner)),
                pl.BlockSpec((1, PAIR, BLOCK), lambda i, lo, hi, tw: (i // inner, pair, i % inner)),
                pl.BlockSpec((8, BLOCK), lambda i, lo, hi, tw: (0, i)),
                pl.BlockSpec((length, PAIR), lambda i, lo, hi, tw: (0, 3 * pair + 1)),
                pl.BlockSpec((length, PAIR), lambda i, lo, hi, tw: (0, 3 * pair + 2)),
                pl.BlockSpec((PAIR, length), lambda i, lo, hi, tw: (3 * pair + 1, 0)),
                pl.BlockSpec((1, BLOCK), lambda i, lo, hi, tw: (0, i)),
                pl.BlockSpec((length, PAIR), lambda i, lo, hi, tw: (0, 0)),
            ]
            + [pl.BlockSpec(memory_space=pl.ANY) for _ in before],
            out_specs=pl.BlockSpec((length, 3 * PAIR), lambda i, lo, hi, tw: (0, pair)),
            scratch_shapes=[
                pltpu.VMEM((length, PAIR), jnp.float32),
                pltpu.VMEM((length, PAIR), jnp.float32),
            ],
        ),
        input_output_aliases={14: 0} if before else {},
        compiler_params=pltpu.CompilerParams(vmem_limit_bytes=VMEM_LIMIT),
        cost_estimate=pl.CostEstimate(
            flops=area * 256 * 24, bytes_accessed=6 << 20, transcendentals=2 * area
        ),
    )(
        *scalars,
        qkv,
        qkv_t,
        grads,
        grads_t,
        out_t,
        log_total,
        qkv,
        qkv,
        qkv_t,
        labels,
        wide_labels,
        *before,
    )


def assemble(pieces, shapes, moves):
    count = len(shapes)

    def kernel(*refs):
        sources, rest = refs[: len(pieces)], refs[len(pieces) :]
        outs, held, arrived, left = rest[:count], rest[count : 2 * count], rest[-2], rest[-1]
        inward, outward = [], []
        for n, (piece, rows, columns, out, row, column) in enumerate(moves):
            at = (pl.ds(row, rows[1] - rows[0]), pl.ds(column, columns[1] - columns[0]))
            source = sources[piece].at[rows[0] : rows[1], columns[0] : columns[1]]
            inward.append(pltpu.make_async_copy(source, held[out].at[at], arrived.at[n]))
            outward.append(pltpu.make_async_copy(held[out].at[at], outs[out].at[at], left.at[n]))
        for copy in inward:
            copy.start()
        for copy, onward in zip(inward, outward):
            copy.wait()
            onward.start()
        for copy in outward:
            copy.wait()

    any_space = pl.BlockSpec(memory_space=pl.ANY)
    total = sum(2 * a * b for a, b in shapes)
    return pl.pallas_call(
        kernel,
        out_shape=tuple(jax.ShapeDtypeStruct(shape, jnp.bfloat16) for shape in shapes),
        in_specs=[any_space] * len(pieces),
        out_specs=(any_space,) * len(shapes),
        scratch_shapes=[pltpu.VMEM(shape, jnp.bfloat16) for shape in shapes]
        + [pltpu.SemaphoreType.DMA((len(moves),))] * 2,
        compiler_params=pltpu.CompilerParams(vmem_limit_bytes=16 << 20),
        cost_estimate=pl.CostEstimate(flops=0, bytes_accessed=2 * total, transcendentals=0),
    )(*pieces)


def projections(planes, row, late):
    _, kinds, rows, width = planes[0].shape
    pairs = width // PAIR

    def kernel(row_ref, late_ref, *refs):
        plain, scaled = refs[-2:]
        for j, plane in enumerate(refs[:-2]):
            for i in range(4):
                base = ((j // 2) ^ late_ref[0]) * 2 + j % 2
                at = pl.multiple_of((base * 4 + (i ^ row_ref[0])) * rows, rows)
                for kind in range(kinds):
                    for pair in range(pairs):
                        column = (pair * kinds + kind) * PAIR
                        part = plane[i, kind, :, pair * PAIR : (pair + 1) * PAIR]
                        plain[pl.ds(at, rows), column : column + PAIR] = part
                        if kind == 0:
                            part = part * jnp.asarray(SCALE, part.dtype)
                        scaled[pl.ds(at, rows), column : column + PAIR] = part

    shape = jax.ShapeDtypeStruct((16 * rows, kinds * width), jnp.bfloat16)
    held = pl.BlockSpec(memory_space=pltpu.VMEM)
    return pl.pallas_call(
        kernel,
        out_shape=(shape, shape),
        in_specs=[pl.BlockSpec(memory_space=pltpu.SMEM)] * 2 + [held] * 4,
        out_specs=(held, held),
        compiler_params=pltpu.CompilerParams(vmem_limit_bytes=24 << 20),
        cost_estimate=pl.CostEstimate(flops=0, bytes_accessed=6 << 20, transcendentals=0),
    )(row.reshape(1), late.reshape(1), *planes)


def swap(values):
    return lax.ppermute(values, "col", [(0, 1), (1, 0)])


def flip(values, axis, bit, size=4):
    return lax.ppermute(values, axis, [(i, i ^ bit) for i in range(size)])


def pick(values, index, axis=0):
    return lax.dynamic_index_in_dim(values, index, axis, keepdims=False)


def together(*values):
    return lax.optimization_barrier(values)


def gather_start(block):
    rows = block.shape[0] // 2
    top, low = block[:rows], block[rows:]
    return top, low, flip(top, "dp", 1), flip(low, "dp", 2)


def gather_second(state):
    top, low, top_x, low_y = state
    top_y = flip(jnp.concatenate([top, top_x]), "dp", 2)
    low_x = flip(jnp.concatenate([low, low_y]), "dp", 1)
    return top_y, low_x


def gather_end(state, second, parts):
    pieces = (*state, *second)
    rows = pieces[0].shape[0]
    whole, head, tail = (0, rows), (0, rows), (rows, 2 * rows)
    order = ((0, whole), (1, whole), (2, whole), (5, head), (4, head), (3, whole), (4, tail), (5, tail))
    moves = [
        (piece, span, part, n, place * rows, 0)
        for place, (piece, span) in enumerate(order)
        for n, part in enumerate(parts)
    ]
    return assemble(pieces, [(8 * rows, stop - start) for start, stop in parts], moves)


def scatter_split(*grads):
    rows = grads[0].shape[0] // 8
    moves, column = [], 0
    order = (((0, 0),), ((1, 0),), ((0, 1),), ((2, 1),), ((2, 0), (3, 0)), ((1, 1), (3, 1)))
    for piece, array in enumerate(grads):
        columns = array.shape[1]
        for out, parts in enumerate(order):
            for place, (block, second) in enumerate(parts):
                at = (2 * block + second) * rows
                moves.append((piece, (at, at + rows), (0, columns), out, place * rows, column))
        column += columns
    shapes = [(len(parts) * rows, column) for parts in order]
    return assemble(grads, shapes, moves)


def scatter_start(parts):
    *kept, send_y, send_x = parts
    return *kept, flip(send_y, "dp", 2), flip(send_x, "dp", 1)


def scatter_second(state):
    f32, half = jnp.float32, jnp.bfloat16
    top, top_pass, low, low_pass, top_y, low_x = state
    rows = top.shape[0]
    top_x = flip((top_pass.astype(f32) + top_y[rows:].astype(f32)).astype(half), "dp", 1)
    low_y = flip((low_pass.astype(f32) + low_x[rows:].astype(f32)).astype(half), "dp", 2)
    return top_x, low_y


def scatter_end(state, second):
    f32, half = jnp.float32, jnp.bfloat16
    top, _, low, _, top_y, low_x = state
    top_x, low_y = second
    rows = top.shape[0]
    top = top.astype(f32) + top_y[:rows].astype(f32) + top_x.astype(f32)
    low = low.astype(f32) + low_x[:rows].astype(f32) + low_y.astype(f32)
    return jnp.concatenate([top, low]).astype(half)


def whole_norm(summed, gain, shift):
    average = jnp.mean(summed, axis=-1, keepdims=True)
    spread = jnp.mean(summed * summed, axis=-1, keepdims=True) - average * average
    scaling = lax.rsqrt(spread + EPS)
    normed = (summed - average) * scaling
    return (normed * gain + shift, normed, scaling)


def whole_norm_back(upstream, normed, scaling, gain):
    scaled = upstream * gain
    offset = jnp.mean(scaled, axis=-1, keepdims=True)
    slope = jnp.mean(scaled * normed, axis=-1, keepdims=True)
    return scaling * (scaled - offset - normed * slope)


def fast_local(
    tokens,
    segment,
    w_query,
    w_key,
    w_value,
    w_out,
    w_up,
    w_down,
    inner_gain,
    inner_shift,
    outer_gain,
    outer_shift,
    cotangent,
):
    f32 = jnp.float32
    half = jnp.bfloat16
    me = lax.axis_index("dp")
    core = lax.axis_index("col")
    row = lax.axis_index("row")
    which, parity = row // 2, row % 2
    first_core = core == 0
    crossed = me % 2 == 1
    leading = core == me // 2
    row_count = tokens.shape[1]
    length = segment.shape[1]
    block_rows, half_width = w_query.shape
    width = D // 4
    hidden_half = w_up.shape[1]
    stack, cat = jnp.stack, jnp.concatenate

    def turn(values):
        left, right = values[..., :width], values[..., width:]
        return jnp.where(crossed, cat([right, left], axis=-1), values)

    def merge(mine, other):
        return jnp.where(leading, cat([mine, other], axis=-1), cat([other, mine], axis=-1))

    def divide(values):
        left, right = values[..., :half_width], values[..., half_width:]
        return jnp.where(leading, left, right), jnp.where(leading, right, left)

    def by_core(mine, other):
        return jnp.where(first_core, stack([mine, other]), stack([other, mine]))

    tokens = turn(tokens)
    near_0 = pick(tokens, which)
    near_2 = flip(pick(tokens, 1 - which), "row", 2)
    near_1 = flip(near_0, "row", 1)
    own_tokens = merge(pick(tokens, core), swap(pick(tokens, 1 - core)))
    labels = pick(segment, which)
    scalars = (*key_ranges(labels), row.reshape(1))
    wide_labels = jnp.broadcast_to(labels[:, None], (length, PAIR))
    labels = labels[None]

    thirds = stack([w_query, w_key, w_value]).reshape(3, block_rows, 2, width)
    blocks = by_core(pick(thirds, core, 2), swap(pick(thirds, 1 - core, 2)))
    same, cross = pick(blocks, parity), pick(blocks, 1 - parity)
    near = [same] + [flip(same if bit == 2 else cross, "row", bit) for bit in (1, 2, 3)]
    odd = row % 2 == 1
    strips = stack(near)
    packed, plain_down, near_1, near_2, strips = together(
        cat([w_out, w_up], axis=1), w_down, near_1, near_2, strips
    )
    near_3 = flip(near_2, "row", 1)
    out_up_rows = lax.all_gather(packed, "row", axis=0, tiled=True)
    down_rows = lax.all_gather(plain_down, "row", axis=0, tiled=True)
    out_up = gather_start(out_up_rows)
    planes = [strips] + [flip(strips, "dp", bit) for bit in (1, 2, 3)]
    near_3, planes = together(near_3, planes)
    pieces = [near_0, near_1, near_2, near_3]
    pieces += [swap(piece) for piece in pieces]
    whole = (0, row_count), (0, half_width)
    (series,) = assemble(
        pieces,
        [(length, D)],
        [(n, *whole, 0, n % 4 * row_count, n // 4 * half_width) for n in range(8)],
    )
    w_qkv, w_scaled = projections(planes, row, core ^ (me // 2))
    w_mine, w_other = w_qkv[:half_width], w_qkv[half_width:]

    vectors = turn(stack([inner_gain, inner_shift, outer_gain, outer_shift]))
    vectors = merge(vectors, swap(vectors))
    inner_gain, inner_shift, outer_gain, outer_shift = (vectors[i : i + 1] for i in range(4))
    cotangent = turn(cotangent)
    upstream = merge(pick(cotangent, core), swap(pick(cotangent, 1 - core)))

    qkv = dot(series, w_scaled).astype(half)
    qkv_t = qkv.T
    out_0, total_0 = attend(0, qkv, qkv_t, labels, wide_labels, scalars)
    scalars_1, out_up, out_0 = together(scalars, out_up, out_0)
    out_t, total_1 = attend(1, qkv, qkv_t, labels, wide_labels, scalars_1, (out_0,))
    out_up_second = gather_second(out_up)
    down_rows, out_t = together(down_rows, out_t)
    down_first = gather_start(down_rows)
    down_second = gather_second(down_first)
    out_t, out_up_second = together(out_t, out_up_second)
    mixed = lax.all_to_all(out_t, "row", 0, 0, tiled=True)
    out_half, up = gather_end(
        out_up, out_up_second, ((0, half_width), (half_width, half_width + hidden_half))
    )
    full_out = cat([out_half, swap(out_half)], axis=1)
    mixed, down_second = together(mixed, down_second)
    (down,) = gather_end(down_first, down_second, ((0, hidden_half),))
    mixed = mixed.reshape(2, 2, width, row_count)
    kept, passed = pick(mixed, core), swap(pick(mixed, 1 - core))
    mixture_t = jnp.where(
        first_core,
        cat([kept[0], passed[0], kept[1], passed[1]]),
        cat([passed[1], kept[1], passed[0], kept[0]]),
    )

    summed = own_tokens.astype(f32) + jnp.einsum(
        "eq,de->qd", mixture_t, full_out, preferred_element_type=f32
    )
    middle, inner_normed, inner_scaling = whole_norm(summed, inner_gain, inner_shift)

    middle_own = middle.astype(half)
    middle_other = swap(middle_own)
    hidden_own = dot(middle_own, up)
    hidden_other = dot(middle_other, up)
    active_own = gelu_value(hidden_own).astype(half)
    active_other = gelu_value(hidden_other).astype(half)
    down_other = jnp.einsum("qf,df->qd", active_other, down, preferred_element_type=f32)
    down_swapped = swap(down_other.astype(half))
    down_own = jnp.einsum("qf,df->qd", active_own, down, preferred_element_type=f32)
    second_sum = middle + (down_own + down_swapped.astype(f32))
    result, outer_normed, outer_scaling = whole_norm(second_sum, outer_gain, outer_shift)
    kept, passed = divide(result.astype(half))
    layer_out = turn(by_core(kept, swap(passed)))

    outer_gain_grad = jnp.sum(upstream * outer_normed, axis=0)
    outer_shift_grad = jnp.sum(upstream, axis=0)
    second_grad = whole_norm_back(upstream, outer_normed, outer_scaling, outer_gain)
    second_own = second_grad.astype(half)
    second_other = swap(second_own)

    def weight_grad(left, right):
        return jnp.einsum("qd,qf->df", left, right, preferred_element_type=f32)

    grad_down = weight_grad(second_own, active_own) + weight_grad(second_other, active_other)
    down_parts = scatter_split(grad_down.astype(half))
    down_parts, second_own, second_other = together(down_parts, second_own, second_other)
    down_first = scatter_start(down_parts)
    active_grad_own = (dot(second_own, down) * gelu_slope(hidden_own)).astype(half)
    active_grad_other = (dot(second_other, down) * gelu_slope(hidden_other)).astype(half)
    middle_grad_other = jnp.einsum("qf,df->qd", active_grad_other, up, preferred_element_type=f32)
    middle_swapped = swap(middle_grad_other.astype(half))
    middle_swapped, down_first = together(middle_swapped, down_first)
    middle_grad_own = jnp.einsum("qf,df->qd", active_grad_own, up, preferred_element_type=f32)

    middle_grad = second_grad + (middle_grad_own + middle_swapped.astype(f32))
    inner_gain_grad = jnp.sum(middle_grad * inner_normed, axis=0)
    inner_shift_grad = jnp.sum(middle_grad, axis=0)
    summed_grad = whole_norm_back(middle_grad, inner_normed, inner_scaling, inner_gain)
    summed_half = summed_grad.astype(half)
    grads_t = jnp.einsum("qd,de->eq", summed_half, full_out, preferred_element_type=f32)
    grads_t = grads_t.astype(half).reshape(4, width, row_count)
    kept = jnp.where(
        first_core, stack([grads_t[0], grads_t[2]]), stack([grads_t[3], grads_t[1]])
    )
    passed = jnp.where(
        first_core, stack([grads_t[1], grads_t[3]]), stack([grads_t[2], grads_t[0]])
    )
    grads_t = by_core(kept, swap(passed)).reshape(4, width, row_count)
    down_second = scatter_second(down_first)
    grads_t, down_second = together(grads_t, down_second)
    grads_t = lax.all_to_all(grads_t, "row", 0, 0, tiled=True)

    grad_up = weight_grad(middle_own, active_grad_own) + weight_grad(
        middle_other, active_grad_other
    )
    grad_out = jnp.einsum("qd,eq->de", summed_half, mixture_t, preferred_element_type=f32)
    grad_out = grad_out[:, :half_width] + swap(grad_out[:, half_width:].astype(half)).astype(f32)
    out_up_parts = scatter_split(grad_out.astype(half), grad_up.astype(half))
    kept, passed = divide(summed_grad)
    base = turn(by_core(kept, swap(passed)))
    out_up_first = scatter_start(out_up_parts)
    grads_t, down_second, out_up_first = together(grads_t, down_second, out_up_first)
    grads = grads_t.transpose(0, 2, 1).reshape(length, width)
    qkv_grad = attend_back(
        0, qkv, qkv_t, labels, wide_labels, scalars, out_t, total_0, grads, grads_t
    )
    grad_down = lax.psum_scatter(
        scatter_end(down_first, down_second), "row", scatter_dimension=0, tiled=True
    )
    out_up_second = scatter_second(out_up_first)
    out_up_plane = scatter_end(out_up_first, out_up_second)
    scalars_1, grad_down, out_up_plane, qkv_grad, base, layer_out = together(
        scalars, grad_down, out_up_plane, qkv_grad, base, layer_out
    )
    out_up_grad = lax.psum_scatter(out_up_plane, "row", scatter_dimension=0, tiled=True)
    qkv_grad = attend_back(
        1, qkv, qkv_t, labels, wide_labels, scalars_1, out_t, total_1, grads, grads_t, (qkv_grad,)
    )
    qkv_grad, out_up_grad = together(qkv_grad, out_up_grad)
    grad_down, out_up_grad = grad_down.astype(f32), out_up_grad.astype(f32)
    grad_out, grad_up = out_up_grad[:, :half_width], out_up_grad[:, half_width:]

    def back_part(rows):
        return jnp.einsum("le,de->ld", qkv_grad, rows, preferred_element_type=f32)

    back_other = swap(back_part(w_other).astype(half))
    norm_local = stack([inner_gain_grad, inner_shift_grad, outer_gain_grad, outer_shift_grad])
    back = back_part(w_mine) + back_other.astype(f32)
    back = back.reshape(4, row_count, half_width)
    pass_on = turn(back[2] + flip(back[3].astype(half), "row", 1).astype(f32)).astype(half)
    pass_on, qkv_grad, norm_local = together(pass_on, qkv_grad, norm_local)
    from_far = flip(pass_on, "row", 2)
    from_near = turn(back[0] + flip(back[1].astype(half), "row", 1).astype(f32))
    slot = jnp.arange(2).reshape(2, 1, 1)
    base = base + jnp.where(slot == which, from_near[None], 0.0)

    grads = jnp.einsum("ld,le->de", series, qkv_grad, preferred_element_type=f32)
    grads_mine, grads_other = grads[:half_width], grads[half_width:]

    def plane_part(j):
        rows = slice((j % 2) * width, (j % 2 + 1) * width)
        if j < 2:
            return jnp.where(leading, grads_mine[rows], grads_other[rows])
        return jnp.where(leading, grads_other[rows], grads_mine[rows])

    arrived = [flip(plane_part(bit).astype(half), "dp", bit) for bit in (1, 2, 3)]
    arrived, base, from_far = together(arrived, base, from_far)
    total = plane_part(0)
    for part in arrived:
        total = total + part.astype(f32)
    total = total.reshape(4, block_rows, 3 * width)
    sends = tuple(pick(total, row ^ bit).astype(half) for bit in (1, 2, 3))
    near_1, near_2, near_3 = (flip(part, "row", bit) for bit, part in zip((1, 2, 3), sends))
    own_part = (pick(total, row) + near_2.astype(f32)).astype(half)
    other_part = (near_1.astype(f32) + near_3.astype(f32)).astype(half)
    strip = jnp.where(odd, stack([other_part, own_part]), stack([own_part, other_part]))
    kept, passed = pick(strip, core), swap(pick(strip, 1 - core))

    def by_kind(values):
        values = values.reshape(block_rows, width // PAIR, 3, PAIR).transpose(2, 0, 1, 3)
        return values.reshape(3, block_rows, width)

    kept, passed = by_kind(kept), by_kind(passed)
    qkv_grads = jnp.where(first_core, cat([kept, passed], axis=2), cat([passed, kept], axis=2))
    qkv_grads = qkv_grads.astype(f32)

    input_grad = base + jnp.where(slot == which, 0.0, from_far[None].astype(f32))

    kept, passed = divide(norm_local)
    norm_grads = turn(kept + swap(passed))
    for axis in ("row", "dp"):
        one, two, three = (flip(norm_grads, axis, bit) for bit in (1, 2, 3))
        norm_grads = (norm_grads + one) + (two + three)
    return (
        layer_out,
        input_grad,
        qkv_grads[0],
        qkv_grads[1],
        qkv_grads[2],
        grad_out,
        grad_up,
        grad_down,
        norm_grads,
    )


def solution(mesh):
    placed = (
        P("dp", "row", "col"),
        P("dp", None),
        P(("dp", "row"), "col"),
        P(("dp", "row"), "col"),
        P(("dp", "row"), "col"),
        P(("dp", "row"), "col"),
        P(("dp", "row"), "col"),
        P(("dp", "row"), "col"),
        P("col"),
        P("col"),
        P("col"),
        P("col"),
        P("dp", "row", "col"),
    )
    body = fast_local if fits(mesh) else local
    return jax.shard_map(
        body,
        mesh=mesh,
        in_specs=placed,
        out_specs=(
            P("dp", "row", "col"),
            P("dp", "row", "col"),
            P(("dp", "row"), "col"),
            P(("dp", "row"), "col"),
            P(("dp", "row"), "col"),
            P(("dp", "row"), "col"),
            P(("dp", "row"), "col"),
            P(("dp", "row"), "col"),
            P(None, "col"),
        ),
        check_vma=False,
    )
```

```python
import jax
import jax.numpy as jnp
from jax import lax
from jax.experimental import pallas as pl
from jax.experimental.pallas import tpu as pltpu
from jax.sharding import PartitionSpec as P

D = 1024
HEAD_DIM = 64


EPS = 1e-05
ROOT_HALF = 0.7071067811865476
INV_ROOT_TAU = 0.3989422804014327


def gelu_value(inputs):
    return 0.5 * inputs * (1.0 + lax.erf(inputs * ROOT_HALF))


def gelu_slope(inputs):
    return (
        0.5 * (1.0 + lax.erf(inputs * ROOT_HALF))
        + inputs * jnp.exp(-0.5 * inputs * inputs) * INV_ROOT_TAU
    )


def widen(values):
    return lax.all_gather(values, "col", axis=2, tiled=True)


def narrow(partial_value):
    return lax.psum_scatter(partial_value, "col", scatter_dimension=2, tiled=True)


def norm_forward(summed, norm_gain, norm_shift):
    row_sums, squares = lax.psum(
        (jnp.sum(summed, axis=-1, keepdims=True), jnp.sum(summed * summed, axis=-1, keepdims=True)),
        "col",
    )
    average = row_sums / D
    spread = squares / D - average * average
    scaling = lax.rsqrt(spread + EPS)
    normed = (summed - average) * scaling
    return (normed * norm_gain + norm_shift, normed, scaling)


def norm_backward(upstream, normed, scaling, norm_gain):
    scaled = upstream * norm_gain
    offset_sum, slope_sum = lax.psum(
        (jnp.sum(scaled, axis=-1, keepdims=True), jnp.sum(scaled * normed, axis=-1, keepdims=True)),
        "col",
    )
    return scaling * (scaled - offset_sum / D - normed * (slope_sum / D))


def head_view(values):
    return values.reshape(values.shape[0], values.shape[1] // HEAD_DIM, HEAD_DIM)


def masked_scores(queries, key_rows, own_labels, all_labels):
    scores = jnp.einsum(
        "qhe,khe->hqk", head_view(queries), head_view(key_rows), preferred_element_type=jnp.float32
    ) * HEAD_DIM ** (-0.5)
    inside = own_labels[:, None] == all_labels[None, :]
    return jnp.where(inside[None], scores, -jnp.inf)


def attend_forward(inputs):
    queries, key_rows, value_rows, own_labels, all_labels = inputs
    scores = masked_scores(queries, key_rows, own_labels, all_labels)
    highest = jnp.max(scores, axis=-1, keepdims=True)
    log_total = highest + jnp.log(jnp.sum(jnp.exp(scores - highest), axis=-1, keepdims=True))
    attention = jnp.exp(scores - log_total).astype(jnp.bfloat16)
    mixture = jnp.einsum(
        "hqk,khe->qhe", attention, head_view(value_rows), preferred_element_type=jnp.float32
    )
    return (mixture.reshape(queries.shape).astype(jnp.bfloat16), log_total)


def attend_backward(inputs):
    queries, key_rows, value_rows, own_labels, all_labels, log_total, mixture_grad = inputs
    scores = masked_scores(queries, key_rows, own_labels, all_labels)
    chance = jnp.exp(scores - log_total)
    attention = chance.astype(jnp.bfloat16)
    chance_grad = jnp.einsum(
        "qhe,khe->hqk",
        head_view(mixture_grad),
        head_view(value_rows),
        preferred_element_type=jnp.float32,
    )
    within = jnp.sum(chance * chance_grad, axis=-1, keepdims=True)
    score_grad = (chance * (chance_grad - within) * HEAD_DIM ** (-0.5)).astype(jnp.bfloat16)
    query_grad = jnp.einsum(
        "hqk,khe->qhe", score_grad, head_view(key_rows), preferred_element_type=jnp.float32
    )
    key_part = jnp.einsum(
        "hqk,qhe->khe", score_grad, head_view(queries), preferred_element_type=jnp.float32
    )
    value_part = jnp.einsum(
        "hqk,qhe->khe", attention, head_view(mixture_grad), preferred_element_type=jnp.float32
    )
    return (
        query_grad.reshape(queries.shape).astype(jnp.bfloat16),
        key_part.reshape(key_rows.shape),
        value_part.reshape(value_rows.shape),
    )


def local(
    tokens,
    segment,
    w_query,
    w_key,
    w_value,
    w_out,
    w_up,
    w_down,
    inner_gain,
    inner_shift,
    outer_gain,
    outer_shift,
    cotangent,
):
    f32 = jnp.float32
    half = jnp.bfloat16
    gathered = (
        lax.all_gather(w_query, ("dp", "row"), axis=0, tiled=True),
        lax.all_gather(w_key, ("dp", "row"), axis=0, tiled=True),
        lax.all_gather(w_value, ("dp", "row"), axis=0, tiled=True),
        lax.all_gather(w_out, ("dp", "row"), axis=0, tiled=True),
        lax.all_gather(w_up, ("dp", "row"), axis=0, tiled=True),
        lax.all_gather(w_down, ("dp", "row"), axis=0, tiled=True),
    )
    full_query, full_key, full_value, full_out, full_up, full_down = gathered
    row_count = tokens.shape[1]
    own_labels = lax.dynamic_slice_in_dim(segment, lax.axis_index("row") * row_count, row_count, 1)
    wide_tokens = widen(tokens)
    queries = jnp.einsum("sqd,de->sqe", wide_tokens, full_query, preferred_element_type=f32).astype(
        half
    )
    key_rows = jnp.einsum("sqd,de->sqe", wide_tokens, full_key, preferred_element_type=f32).astype(
        half
    )
    value_rows = jnp.einsum(
        "sqd,de->sqe", wide_tokens, full_value, preferred_element_type=f32
    ).astype(half)
    all_keys, all_values = (
        lax.all_gather(key_rows, "row", axis=1, tiled=True),
        lax.all_gather(value_rows, "row", axis=1, tiled=True),
    )
    mixture, log_total = lax.map(
        attend_forward, (queries, all_keys, all_values, own_labels, segment)
    )
    summed = tokens.astype(f32) + narrow(
        jnp.einsum("sqe,de->sqd", mixture, full_out, preferred_element_type=f32)
    )
    middle, inner_normed, inner_scaling = norm_forward(summed, inner_gain, inner_shift)
    wide_middle = widen(middle.astype(half))
    hidden = jnp.einsum("sqd,df->sqf", wide_middle, full_up, preferred_element_type=f32)
    active = gelu_value(hidden).astype(half)
    second_sum = middle + narrow(
        jnp.einsum("sqf,df->sqd", active, full_down, preferred_element_type=f32)
    )
    result, outer_normed, outer_scaling = norm_forward(second_sum, outer_gain, outer_shift)
    layer_out = result.astype(half)
    outer_gain_grad = jnp.sum(cotangent * outer_normed, axis=(0, 1))
    outer_shift_grad = jnp.sum(cotangent, axis=(0, 1))
    second_grad = norm_backward(cotangent, outer_normed, outer_scaling, outer_gain)
    wide_second = widen(second_grad.astype(half))
    grad_down = jnp.einsum("sqd,sqf->df", wide_second, active, preferred_element_type=f32)
    active_grad = (
        jnp.einsum("sqd,df->sqf", wide_second, full_down, preferred_element_type=f32)
        * gelu_slope(hidden)
    ).astype(half)
    grad_up = jnp.einsum("sqd,sqf->df", wide_middle, active_grad, preferred_element_type=f32)
    middle_grad = second_grad + narrow(
        jnp.einsum("sqf,df->sqd", active_grad, full_up, preferred_element_type=f32)
    )
    inner_gain_grad = jnp.sum(middle_grad * inner_normed, axis=(0, 1))
    inner_shift_grad = jnp.sum(middle_grad, axis=(0, 1))
    summed_grad = norm_backward(middle_grad, inner_normed, inner_scaling, inner_gain)
    wide_summed = widen(summed_grad.astype(half))
    grad_out = jnp.einsum("sqd,sqe->de", wide_summed, mixture, preferred_element_type=f32)
    mixture_grad = jnp.einsum(
        "sqd,de->sqe", wide_summed, full_out, preferred_element_type=f32
    ).astype(half)
    query_grad, key_part, value_part = lax.map(
        attend_backward,
        (queries, all_keys, all_values, own_labels, segment, log_total, mixture_grad),
    )
    key_sums, value_sums = (
        lax.psum_scatter(key_part, "row", scatter_dimension=1, tiled=True),
        lax.psum_scatter(value_part, "row", scatter_dimension=1, tiled=True),
    )
    key_grad = key_sums.astype(half)
    value_grad = value_sums.astype(half)
    grad_query = jnp.einsum("sqd,sqe->de", wide_tokens, query_grad, preferred_element_type=f32)
    grad_key = jnp.einsum("sqd,sqe->de", wide_tokens, key_grad, preferred_element_type=f32)
    grad_value = jnp.einsum("sqd,sqe->de", wide_tokens, value_grad, preferred_element_type=f32)
    back_sum = jnp.einsum("sqe,de->sqd", query_grad, full_query, preferred_element_type=f32)
    back_sum = back_sum + jnp.einsum("sqe,de->sqd", key_grad, full_key, preferred_element_type=f32)
    back_sum = back_sum + jnp.einsum(
        "sqe,de->sqd", value_grad, full_value, preferred_element_type=f32
    )
    input_grad = summed_grad + narrow(back_sum)
    norm_local = jnp.stack([inner_gain_grad, inner_shift_grad, outer_gain_grad, outer_shift_grad])
    weight_grads = (
        lax.psum_scatter(grad_query, ("dp", "row"), scatter_dimension=0, tiled=True),
        lax.psum_scatter(grad_key, ("dp", "row"), scatter_dimension=0, tiled=True),
        lax.psum_scatter(grad_value, ("dp", "row"), scatter_dimension=0, tiled=True),
        lax.psum_scatter(grad_out, ("dp", "row"), scatter_dimension=0, tiled=True),
        lax.psum_scatter(grad_up, ("dp", "row"), scatter_dimension=0, tiled=True),
        lax.psum_scatter(grad_down, ("dp", "row"), scatter_dimension=0, tiled=True),
    )
    norm_grads = lax.psum(norm_local, ("dp", "row"))
    return (
        layer_out,
        input_grad,
        weight_grads[0],
        weight_grads[1],
        weight_grads[2],
        weight_grads[3],
        weight_grads[4],
        weight_grads[5],
        norm_grads,
    )


PAIR = 128
BLOCK = 256
NEG = -1e30
HEADS = 16
SCALE = HEAD_DIM ** (-0.5)
VMEM_LIMIT = 48 << 20


def fits(mesh):
    sizes = dict(mesh.shape)
    return sizes["col"] == 2 and sizes["dp"] == 4 and sizes["row"] == 4


def head_mask(values, head):
    lane = lax.broadcasted_iota(jnp.int32, values.shape, 1)
    keep = (lane < HEAD_DIM) if head == 0 else (lane >= HEAD_DIM)
    return jnp.where(keep, values, jnp.zeros_like(values))


def dot(left, right):
    return jnp.dot(left, right, preferred_element_type=jnp.float32)


def forward_kernel(low, high, twist, q_t, k, v_t, own, others, *refs):
    out_t, log_total = refs[-2:]
    step = pl.program_id(0)
    queries = q_t[...]
    own_labels = own[...]
    inner = out_t.shape[2]
    per = k.shape[0] // 4 // BLOCK

    def block_at(j):
        start = ((j // per) ^ twist[0]) * per + j % per
        return pl.multiple_of(start * BLOCK, BLOCK)

    def body(n, carry):
        j = low[step] + 2 * n
        later = jnp.minimum(j + 1, high[step] - 1)
        starts = block_at(j), block_at(later)
        masks = []
        for index, extra in ((j, False), (later, later == j)):
            labels = others[pl.ds(pl.multiple_of(index * BLOCK, BLOCK), BLOCK), :]
            labels = jnp.where(extra, -1, labels)
            masks.append(jnp.concatenate([labels] * (BLOCK // PAIR), axis=1) == own_labels)
        keys = [k[pl.ds(start, BLOCK), :] for start in starts]
        state = []
        for head in range(2):
            highest, total, mixed = carry[head]
            scores = [
                jnp.where(inside, dot(head_mask(part, head), queries), NEG)
                for part, inside in zip(keys, masks)
            ]
            fresh = jnp.max(jnp.maximum(*scores), axis=0, keepdims=True)
            fresh = jnp.maximum(highest, fresh)
            fade = jnp.exp(highest - fresh)
            total, mixed = total * fade, mixed * fade
            for part, start in zip(scores, starts):
                chance = jnp.exp(part - fresh)
                values = v_t[head * HEAD_DIM : (head + 1) * HEAD_DIM, pl.ds(start, BLOCK)]
                total = total + jnp.sum(chance, axis=0, keepdims=True)
                mixed = mixed + dot(values, chance.astype(jnp.bfloat16))
            state.append((fresh, total, mixed))
        return tuple(state)

    one = (
        jnp.full((1, inner), NEG, jnp.float32),
        jnp.zeros((1, inner), jnp.float32),
        jnp.zeros((HEAD_DIM, inner), jnp.float32),
    )
    final = lax.fori_loop(0, (high[step] - low[step] + 1) // 2, body, (one, one))
    for head in range(2):
        highest, total, mixed = final[head]
        out_t[0, head * HEAD_DIM : (head + 1) * HEAD_DIM, :] = (mixed / total).astype(jnp.bfloat16)
        log_total[head : head + 1, :] = highest + jnp.log(total)


def backward_kernel(
    low,
    high,
    twist,
    q,
    q_t,
    g,
    g_t,
    out_t,
    log_total,
    k,
    v,
    k_t,
    own,
    others,
    *refs,
):
    result, dk_sum, dv_sum = refs[-3:]
    step = pl.program_id(0)
    per = k.shape[0] // 4 // BLOCK

    @pl.when(step == 0)
    def _():
        dk_sum[...] = jnp.zeros_like(dk_sum)
        dv_sum[...] = jnp.zeros_like(dv_sum)

    half = jnp.bfloat16
    queries_t = q_t[...]
    grads_t = g_t[0]
    own_labels = own[...]
    product = grads_t.astype(jnp.float32) * out_t[0].astype(jnp.float32)
    heads = []
    for head in range(2):
        rows = slice(head * HEAD_DIM, (head + 1) * HEAD_DIM)
        heads.append(
            (
                head_mask(q[...], head),
                head_mask(g[...], head),
                jnp.sum(product[rows], axis=0, keepdims=True),
                log_total[head : head + 1, :],
            )
        )

    def block_at(j):
        start = ((j // per) ^ twist[0]) * per + j % per
        return pl.multiple_of(start * BLOCK, BLOCK)

    def body(n, carry):
        j = low[step] + 2 * n
        later = jnp.minimum(j + 1, high[step] - 1)
        sums = list(carry)
        parts = []
        for index, extra in ((j, False), (later, later == j)):
            start = block_at(index)
            keys = k[pl.ds(start, BLOCK), :]
            values = v[pl.ds(start, BLOCK), :]
            labels = others[pl.ds(pl.multiple_of(index * BLOCK, BLOCK), BLOCK), :]
            labels = jnp.where(extra, -1, labels)
            inside = jnp.concatenate([labels] * (BLOCK // PAIR), axis=1) == own_labels
            key_part, value_part = None, None
            for head in range(2):
                own_q, own_g, within, total = heads[head]
                scores = dot(head_mask(keys, head), queries_t)
                chance = jnp.where(inside, jnp.exp(scores - total), 0.0)
                chance_grad = dot(head_mask(values, head), grads_t)
                score_grad = (chance * (chance_grad - within)).astype(half)
                value_new = dot(chance.astype(half), own_g)
                key_new = dot(score_grad, own_q)
                keys_t = k_t[head * HEAD_DIM : (head + 1) * HEAD_DIM, pl.ds(start, BLOCK)]
                sums[head] = sums[head] + dot(keys_t, score_grad)
                key_part = key_new if key_part is None else key_part + key_new
                value_part = value_new if value_part is None else value_part + value_new
            parts.append((start, key_part, value_part))
        for start, key_part, value_part in parts:
            dk_sum[pl.ds(start, BLOCK), :] += key_part
            dv_sum[pl.ds(start, BLOCK), :] += value_part
        return tuple(sums)

    zero = jnp.zeros((HEAD_DIM, own_labels.shape[1]), jnp.float32)
    first, second = lax.fori_loop(0, (high[step] - low[step] + 1) // 2, body, (zero, zero))
    both = jnp.concatenate([first, second], axis=0) * SCALE
    held = pl.multiple_of((((step // per) ^ twist[0]) * per + step % per) * BLOCK, BLOCK)
    result[pl.ds(held, BLOCK), :PAIR] = jnp.transpose(both).astype(half)

    @pl.when(step == pl.num_programs(0) - 1)
    def _():
        result[:, PAIR : 2 * PAIR] = dk_sum[...].astype(half)
        result[:, 2 * PAIR :] = dv_sum[...].astype(half)


def key_ranges(labels):
    blocks = labels.reshape(-1, BLOCK)
    first, last = blocks[:, :1], blocks[:, -1:]
    before = jnp.sum((labels[None, :] < first).astype(jnp.int32), axis=1)
    upto = jnp.sum((labels[None, :] <= last).astype(jnp.int32), axis=1)
    return before // BLOCK, (upto + BLOCK - 1) // BLOCK


def attend(pair, qkv, qkv_t, labels, wide_labels, scalars, before=()):
    length, width = qkv.shape
    pairs = width // 3 // PAIR
    row_count = length // 4
    inner = row_count // BLOCK

    def held(i, twist):
        return ((i // inner) ^ twist[0]) * inner + i % inner

    area = length * length
    return pl.pallas_call(
        forward_kernel,
        out_shape=(
            jax.ShapeDtypeStruct((4, pairs * PAIR, row_count), jnp.bfloat16),
            jax.ShapeDtypeStruct((8, length), jnp.float32),
        ),
        grid_spec=pltpu.PrefetchScalarGridSpec(
            num_scalar_prefetch=3,
            grid=(length // BLOCK,),
            in_specs=[
                pl.BlockSpec((PAIR, BLOCK), lambda i, lo, hi, tw: (3 * pair, held(i, tw))),
                pl.BlockSpec((length, PAIR), lambda i, lo, hi, tw: (0, 3 * pair + 1)),
                pl.BlockSpec((PAIR, length), lambda i, lo, hi, tw: (3 * pair + 2, 0)),
                pl.BlockSpec((1, BLOCK), lambda i, lo, hi, tw: (0, i)),
                pl.BlockSpec((length, PAIR), lambda i, lo, hi, tw: (0, 0)),
            ]
            + [pl.BlockSpec(memory_space=pl.ANY) for _ in before],
            out_specs=(
                pl.BlockSpec((1, PAIR, BLOCK), lambda i, lo, hi, tw: (i // inner, pair, i % inner)),
                pl.BlockSpec((8, BLOCK), lambda i, lo, hi, tw: (0, i)),
            ),
        ),
        input_output_aliases={8: 0} if before else {},
        compiler_params=pltpu.CompilerParams(vmem_limit_bytes=VMEM_LIMIT),
        cost_estimate=pl.CostEstimate(
            flops=area * 256 * 24, bytes_accessed=4 << 20, transcendentals=2 * area
        ),
    )(*scalars, qkv_t, qkv, qkv_t, labels, wide_labels, *before)


def attend_back(
    pair, qkv, qkv_t, labels, wide_labels, scalars, out_t, log_total, grads, grads_t, before=()
):
    length, width = grads.shape
    pairs = width // PAIR
    row_count = length // 4
    inner = row_count // BLOCK

    def held(i, twist):
        return ((i // inner) ^ twist[0]) * inner + i % inner

    area = length * length
    return pl.pallas_call(
        backward_kernel,
        out_shape=jax.ShapeDtypeStruct(qkv.shape, jnp.bfloat16),
        grid_spec=pltpu.PrefetchScalarGridSpec(
            num_scalar_prefetch=3,
            grid=(length // BLOCK,),
            in_specs=[
                pl.BlockSpec((BLOCK, PAIR), lambda i, lo, hi, tw: (held(i, tw), 3 * pair)),
                pl.BlockSpec((PAIR, BLOCK), lambda i, lo, hi, tw: (3 * pair, held(i, tw))),
                pl.BlockSpec((BLOCK, PAIR), lambda i, lo, hi, tw: (i, pair)),
                pl.BlockSpec((1, PAIR, BLOCK), lambda i, lo, hi, tw: (i // inner, pair, i % inner)),
                pl.BlockSpec((1, PAIR, BLOCK), lambda i, lo, hi, tw: (i // inner, pair, i % inner)),
                pl.BlockSpec((8, BLOCK), lambda i, lo, hi, tw: (0, i)),
                pl.BlockSpec((length, PAIR), lambda i, lo, hi, tw: (0, 3 * pair + 1)),
                pl.BlockSpec((length, PAIR), lambda i, lo, hi, tw: (0, 3 * pair + 2)),
                pl.BlockSpec((PAIR, length), lambda i, lo, hi, tw: (3 * pair + 1, 0)),
                pl.BlockSpec((1, BLOCK), lambda i, lo, hi, tw: (0, i)),
                pl.BlockSpec((length, PAIR), lambda i, lo, hi, tw: (0, 0)),
            ]
            + [pl.BlockSpec(memory_space=pl.ANY) for _ in before],
            out_specs=pl.BlockSpec((length, 3 * PAIR), lambda i, lo, hi, tw: (0, pair)),
            scratch_shapes=[
                pltpu.VMEM((length, PAIR), jnp.float32),
                pltpu.VMEM((length, PAIR), jnp.float32),
            ],
        ),
        input_output_aliases={14: 0} if before else {},
        compiler_params=pltpu.CompilerParams(vmem_limit_bytes=VMEM_LIMIT),
        cost_estimate=pl.CostEstimate(
            flops=area * 256 * 24, bytes_accessed=6 << 20, transcendentals=2 * area
        ),
    )(
        *scalars,
        qkv,
        qkv_t,
        grads,
        grads_t,
        out_t,
        log_total,
        qkv,
        qkv,
        qkv_t,
        labels,
        wide_labels,
        *before,
    )


def assemble(pieces, shapes, moves):
    count = len(shapes)

    def kernel(*refs):
        sources, rest = refs[: len(pieces)], refs[len(pieces) :]
        outs, held, arrived, left = rest[:count], rest[count : 2 * count], rest[-2], rest[-1]
        inward, outward = [], []
        for n, (piece, rows, columns, out, row, column) in enumerate(moves):
            at = (pl.ds(row, rows[1] - rows[0]), pl.ds(column, columns[1] - columns[0]))
            source = sources[piece].at[rows[0] : rows[1], columns[0] : columns[1]]
            inward.append(pltpu.make_async_copy(source, held[out].at[at], arrived.at[n]))
            outward.append(pltpu.make_async_copy(held[out].at[at], outs[out].at[at], left.at[n]))
        for copy in inward:
            copy.start()
        for copy, onward in zip(inward, outward):
            copy.wait()
            onward.start()
        for copy in outward:
            copy.wait()

    any_space = pl.BlockSpec(memory_space=pl.ANY)
    total = sum(2 * a * b for a, b in shapes)
    return pl.pallas_call(
        kernel,
        out_shape=tuple(jax.ShapeDtypeStruct(shape, jnp.bfloat16) for shape in shapes),
        in_specs=[any_space] * len(pieces),
        out_specs=(any_space,) * len(shapes),
        scratch_shapes=[pltpu.VMEM(shape, jnp.bfloat16) for shape in shapes]
        + [pltpu.SemaphoreType.DMA((len(moves),))] * 2,
        compiler_params=pltpu.CompilerParams(vmem_limit_bytes=16 << 20),
        cost_estimate=pl.CostEstimate(flops=0, bytes_accessed=2 * total, transcendentals=0),
    )(*pieces)


def projections(planes, row, late):
    _, kinds, rows, width = planes[0].shape
    pairs = width // PAIR

    def kernel(row_ref, late_ref, *refs):
        plain, scaled = refs[-2:]
        for j, plane in enumerate(refs[:-2]):
            for i in range(4):
                base = ((j // 2) ^ late_ref[0]) * 2 + j % 2
                at = pl.multiple_of((base * 4 + (i ^ row_ref[0])) * rows, rows)
                for kind in range(kinds):
                    for pair in range(pairs):
                        column = (pair * kinds + kind) * PAIR
                        part = plane[i, kind, :, pair * PAIR : (pair + 1) * PAIR]
                        plain[pl.ds(at, rows), column : column + PAIR] = part
                        if kind == 0:
                            part = part * jnp.asarray(SCALE, part.dtype)
                        scaled[pl.ds(at, rows), column : column + PAIR] = part

    shape = jax.ShapeDtypeStruct((16 * rows, kinds * width), jnp.bfloat16)
    held = pl.BlockSpec(memory_space=pltpu.VMEM)
    return pl.pallas_call(
        kernel,
        out_shape=(shape, shape),
        in_specs=[pl.BlockSpec(memory_space=pltpu.SMEM)] * 2 + [held] * 4,
        out_specs=(held, held),
        compiler_params=pltpu.CompilerParams(vmem_limit_bytes=24 << 20),
        cost_estimate=pl.CostEstimate(flops=0, bytes_accessed=6 << 20, transcendentals=0),
    )(row.reshape(1), late.reshape(1), *planes)


def swap(values):
    return lax.ppermute(values, "col", [(0, 1), (1, 0)])


def flip(values, axis, bit, size=4):
    return lax.ppermute(values, axis, [(i, i ^ bit) for i in range(size)])


def pick(values, index, axis=0):
    return lax.dynamic_index_in_dim(values, index, axis, keepdims=False)


def together(*values):
    return lax.optimization_barrier(values)


def gather_start(block):
    rows = block.shape[0] // 2
    top, low = block[:rows], block[rows:]
    return top, low, flip(top, "dp", 1), flip(low, "dp", 2)


def gather_second(state):
    top, low, top_x, low_y = state
    top_y = flip(jnp.concatenate([top, top_x]), "dp", 2)
    low_x = flip(jnp.concatenate([low, low_y]), "dp", 1)
    return top_y, low_x


def gather_end(state, second, parts):
    pieces = (*state, *second)
    rows = pieces[0].shape[0]
    whole, head, tail = (0, rows), (0, rows), (rows, 2 * rows)
    order = ((0, whole), (1, whole), (2, whole), (5, head), (4, head), (3, whole), (4, tail), (5, tail))
    moves = [
        (piece, span, part, n, place * rows, 0)
        for place, (piece, span) in enumerate(order)
        for n, part in enumerate(parts)
    ]
    return assemble(pieces, [(8 * rows, stop - start) for start, stop in parts], moves)


def scatter_split(*grads):
    rows = grads[0].shape[0] // 8
    moves, column = [], 0
    order = (((0, 0),), ((1, 0),), ((0, 1),), ((2, 1),), ((2, 0), (3, 0)), ((1, 1), (3, 1)))
    for piece, array in enumerate(grads):
        columns = array.shape[1]
        for out, parts in enumerate(order):
            for place, (block, second) in enumerate(parts):
                at = (2 * block + second) * rows
                moves.append((piece, (at, at + rows), (0, columns), out, place * rows, column))
        column += columns
    shapes = [(len(parts) * rows, column) for parts in order]
    return assemble(grads, shapes, moves)


def scatter_start(parts):
    *kept, send_y, send_x = parts
    return *kept, flip(send_y, "dp", 2), flip(send_x, "dp", 1)


def scatter_second(state):
    f32, half = jnp.float32, jnp.bfloat16
    top, top_pass, low, low_pass, top_y, low_x = state
    rows = top.shape[0]
    top_x = flip((top_pass.astype(f32) + top_y[rows:].astype(f32)).astype(half), "dp", 1)
    low_y = flip((low_pass.astype(f32) + low_x[rows:].astype(f32)).astype(half), "dp", 2)
    return top_x, low_y


def scatter_end(state, second):
    f32, half = jnp.float32, jnp.bfloat16
    top, _, low, _, top_y, low_x = state
    top_x, low_y = second
    rows = top.shape[0]
    top = top.astype(f32) + top_y[:rows].astype(f32) + top_x.astype(f32)
    low = low.astype(f32) + low_x[:rows].astype(f32) + low_y.astype(f32)
    return jnp.concatenate([top, low]).astype(half)


def whole_norm(summed, gain, shift):
    average = jnp.mean(summed, axis=-1, keepdims=True)
    spread = jnp.mean(summed * summed, axis=-1, keepdims=True) - average * average
    scaling = lax.rsqrt(spread + EPS)
    normed = (summed - average) * scaling
    return (normed * gain + shift, normed, scaling)


def whole_norm_back(upstream, normed, scaling, gain):
    scaled = upstream * gain
    offset = jnp.mean(scaled, axis=-1, keepdims=True)
    slope = jnp.mean(scaled * normed, axis=-1, keepdims=True)
    return scaling * (scaled - offset - normed * slope)


def fast_local(
    tokens,
    segment,
    w_query,
    w_key,
    w_value,
    w_out,
    w_up,
    w_down,
    inner_gain,
    inner_shift,
    outer_gain,
    outer_shift,
    cotangent,
):
    f32 = jnp.float32
    half = jnp.bfloat16
    me = lax.axis_index("dp")
    core = lax.axis_index("col")
    row = lax.axis_index("row")
    which, parity = row // 2, row % 2
    first_core = core == 0
    crossed = me % 2 == 1
    leading = core == me // 2
    row_count = tokens.shape[1]
    length = segment.shape[1]
    block_rows, half_width = w_query.shape
    width = D // 4
    hidden_half = w_up.shape[1]
    stack, cat = jnp.stack, jnp.concatenate

    def turn(values):
        left, right = values[..., :width], values[..., width:]
        return jnp.where(crossed, cat([right, left], axis=-1), values)

    def merge(mine, other):
        return jnp.where(leading, cat([mine, other], axis=-1), cat([other, mine], axis=-1))

    def divide(values):
        left, right = values[..., :half_width], values[..., half_width:]
        return jnp.where(leading, left, right), jnp.where(leading, right, left)

    def by_core(mine, other):
        return jnp.where(first_core, stack([mine, other]), stack([other, mine]))

    tokens = turn(tokens)
    near_0 = pick(tokens, which)
    near_2 = flip(pick(tokens, 1 - which), "row", 2)
    near_1 = flip(near_0, "row", 1)
    own_tokens = merge(pick(tokens, core), swap(pick(tokens, 1 - core)))
    labels = pick(segment, which)
    scalars = (*key_ranges(labels), row.reshape(1))
    wide_labels = jnp.broadcast_to(labels[:, None], (length, PAIR))
    labels = labels[None]

    thirds = stack([w_query, w_key, w_value]).reshape(3, block_rows, 2, width)
    blocks = by_core(pick(thirds, core, 2), swap(pick(thirds, 1 - core, 2)))
    same, cross = pick(blocks, parity), pick(blocks, 1 - parity)
    near = [same] + [flip(same if bit == 2 else cross, "row", bit) for bit in (1, 2, 3)]
    odd = row % 2 == 1
    strips = stack(near)
    packed, plain_down, near_1, near_2, strips = together(
        cat([w_out, w_up], axis=1), w_down, near_1, near_2, strips
    )
    near_3 = flip(near_2, "row", 1)
    out_up_rows = lax.all_gather(packed, "row", axis=0, tiled=True)
    down_rows = lax.all_gather(plain_down, "row", axis=0, tiled=True)
    out_up = gather_start(out_up_rows)
    planes = [strips] + [flip(strips, "dp", bit) for bit in (1, 2, 3)]
    near_3, planes = together(near_3, planes)
    pieces = [near_0, near_1, near_2, near_3]
    pieces += [swap(piece) for piece in pieces]
    whole = (0, row_count), (0, half_width)
    (series,) = assemble(
        pieces,
        [(length, D)],
        [(n, *whole, 0, n % 4 * row_count, n // 4 * half_width) for n in range(8)],
    )
    w_qkv, w_scaled = projections(planes, row, core ^ (me // 2))
    w_mine, w_other = w_qkv[:half_width], w_qkv[half_width:]

    vectors = turn(stack([inner_gain, inner_shift, outer_gain, outer_shift]))
    vectors = merge(vectors, swap(vectors))
    inner_gain, inner_shift, outer_gain, outer_shift = (vectors[i : i + 1] for i in range(4))
    cotangent = turn(cotangent)
    upstream = merge(pick(cotangent, core), swap(pick(cotangent, 1 - core)))

    qkv = dot(series, w_scaled).astype(half)
    qkv_t = qkv.T
    out_0, total_0 = attend(0, qkv, qkv_t, labels, wide_labels, scalars)
    scalars_1, out_up, out_0 = together(scalars, out_up, out_0)
    out_t, total_1 = attend(1, qkv, qkv_t, labels, wide_labels, scalars_1, (out_0,))
    out_up_second = gather_second(out_up)
    down_rows, out_t = together(down_rows, out_t)
    down_first = gather_start(down_rows)
    down_second = gather_second(down_first)
    out_t, out_up_second = together(out_t, out_up_second)
    mixed = lax.all_to_all(out_t, "row", 0, 0, tiled=True)
    out_half, up = gather_end(
        out_up, out_up_second, ((0, half_width), (half_width, half_width + hidden_half))
    )
    full_out = cat([out_half, swap(out_half)], axis=1)
    mixed, down_second = together(mixed, down_second)
    (down,) = gather_end(down_first, down_second, ((0, hidden_half),))
    mixed = mixed.reshape(2, 2, width, row_count)
    kept, passed = pick(mixed, core), swap(pick(mixed, 1 - core))
    mixture_t = jnp.where(
        first_core,
        cat([kept[0], passed[0], kept[1], passed[1]]),
        cat([passed[1], kept[1], passed[0], kept[0]]),
    )

    summed = own_tokens.astype(f32) + jnp.einsum(
        "eq,de->qd", mixture_t, full_out, preferred_element_type=f32
    )
    middle, inner_normed, inner_scaling = whole_norm(summed, inner_gain, inner_shift)

    middle_own = middle.astype(half)
    middle_other = swap(middle_own)
    hidden_own = dot(middle_own, up)
    hidden_other = dot(middle_other, up)
    active_own = gelu_value(hidden_own).astype(half)
    active_other = gelu_value(hidden_other).astype(half)
    down_other = jnp.einsum("qf,df->qd", active_other, down, preferred_element_type=f32)
    down_swapped = swap(down_other.astype(half))
    down_own = jnp.einsum("qf,df->qd", active_own, down, preferred_element_type=f32)
    second_sum = middle + (down_own + down_swapped.astype(f32))
    result, outer_normed, outer_scaling = whole_norm(second_sum, outer_gain, outer_shift)
    kept, passed = divide(result.astype(half))
    layer_out = turn(by_core(kept, swap(passed)))

    outer_gain_grad = jnp.sum(upstream * outer_normed, axis=0)
    outer_shift_grad = jnp.sum(upstream, axis=0)
    second_grad = whole_norm_back(upstream, outer_normed, outer_scaling, outer_gain)
    second_own = second_grad.astype(half)
    second_other = swap(second_own)

    def weight_grad(left, right):
        return jnp.einsum("qd,qf->df", left, right, preferred_element_type=f32)

    grad_down = weight_grad(second_own, active_own) + weight_grad(second_other, active_other)
    down_parts = scatter_split(grad_down.astype(half))
    down_parts, second_own, second_other = together(down_parts, second_own, second_other)
    down_first = scatter_start(down_parts)
    active_grad_own = (dot(second_own, down) * gelu_slope(hidden_own)).astype(half)
    active_grad_other = (dot(second_other, down) * gelu_slope(hidden_other)).astype(half)
    middle_grad_other = jnp.einsum("qf,df->qd", active_grad_other, up, preferred_element_type=f32)
    middle_swapped = swap(middle_grad_other.astype(half))
    middle_swapped, down_first = together(middle_swapped, down_first)
    middle_grad_own = jnp.einsum("qf,df->qd", active_grad_own, up, preferred_element_type=f32)

    middle_grad = second_grad + (middle_grad_own + middle_swapped.astype(f32))
    inner_gain_grad = jnp.sum(middle_grad * inner_normed, axis=0)
    inner_shift_grad = jnp.sum(middle_grad, axis=0)
    summed_grad = whole_norm_back(middle_grad, inner_normed, inner_scaling, inner_gain)
    summed_half = summed_grad.astype(half)
    grads_t = jnp.einsum("qd,de->eq", summed_half, full_out, preferred_element_type=f32)
    grads_t = grads_t.astype(half).reshape(4, width, row_count)
    kept = jnp.where(
        first_core, stack([grads_t[0], grads_t[2]]), stack([grads_t[3], grads_t[1]])
    )
    passed = jnp.where(
        first_core, stack([grads_t[1], grads_t[3]]), stack([grads_t[2], grads_t[0]])
    )
    grads_t = by_core(kept, swap(passed)).reshape(4, width, row_count)
    down_second = scatter_second(down_first)
    grads_t, down_second = together(grads_t, down_second)
    grads_t = lax.all_to_all(grads_t, "row", 0, 0, tiled=True)

    grad_up = weight_grad(middle_own, active_grad_own) + weight_grad(
        middle_other, active_grad_other
    )
    grad_out = jnp.einsum("qd,eq->de", summed_half, mixture_t, preferred_element_type=f32)
    grad_out = grad_out[:, :half_width] + swap(grad_out[:, half_width:].astype(half)).astype(f32)
    out_up_parts = scatter_split(grad_out.astype(half), grad_up.astype(half))
    kept, passed = divide(summed_grad)
    base = turn(by_core(kept, swap(passed)))
    out_up_first = scatter_start(out_up_parts)
    grads_t, down_second = together(grads_t, down_second)
    grads = grads_t.transpose(0, 2, 1).reshape(length, width)
    qkv_grad = attend_back(
        0, qkv, qkv_t, labels, wide_labels, scalars, out_t, total_0, grads, grads_t
    )
    grad_down = lax.psum_scatter(
        scatter_end(down_first, down_second), "row", scatter_dimension=0, tiled=True
    )
    out_up_second = scatter_second(out_up_first)
    out_up_plane = scatter_end(out_up_first, out_up_second)
    scalars_1, grad_down, out_up_plane, qkv_grad, base, layer_out = together(
        scalars, grad_down, out_up_plane, qkv_grad, base, layer_out
    )
    out_up_grad = lax.psum_scatter(out_up_plane, "row", scatter_dimension=0, tiled=True)
    qkv_grad = attend_back(
        1, qkv, qkv_t, labels, wide_labels, scalars_1, out_t, total_1, grads, grads_t, (qkv_grad,)
    )
    qkv_grad, out_up_grad = together(qkv_grad, out_up_grad)
    grad_down, out_up_grad = grad_down.astype(f32), out_up_grad.astype(f32)
    grad_out, grad_up = out_up_grad[:, :half_width], out_up_grad[:, half_width:]

    def back_part(rows):
        return jnp.einsum("le,de->ld", qkv_grad, rows, preferred_element_type=f32)

    back_other = swap(back_part(w_other).astype(half))
    norm_local = stack([inner_gain_grad, inner_shift_grad, outer_gain_grad, outer_shift_grad])
    back = back_part(w_mine) + back_other.astype(f32)
    back = back.reshape(4, row_count, half_width)
    pass_on = turn(back[2] + flip(back[3].astype(half), "row", 1).astype(f32)).astype(half)
    pass_on, qkv_grad, norm_local = together(pass_on, qkv_grad, norm_local)
    from_far = flip(pass_on, "row", 2)
    from_near = turn(back[0] + flip(back[1].astype(half), "row", 1).astype(f32))
    slot = jnp.arange(2).reshape(2, 1, 1)
    base = base + jnp.where(slot == which, from_near[None], 0.0)

    grads = jnp.einsum("ld,le->de", series, qkv_grad, preferred_element_type=f32)
    grads_mine, grads_other = grads[:half_width], grads[half_width:]

    def plane_part(j):
        rows = slice((j % 2) * width, (j % 2 + 1) * width)
        if j < 2:
            return jnp.where(leading, grads_mine[rows], grads_other[rows])
        return jnp.where(leading, grads_other[rows], grads_mine[rows])

    arrived = [flip(plane_part(bit).astype(half), "dp", bit) for bit in (1, 2, 3)]
    arrived, base, from_far = together(arrived, base, from_far)
    total = plane_part(0)
    for part in arrived:
        total = total + part.astype(f32)
    total = total.reshape(4, block_rows, 3 * width)
    sends = tuple(pick(total, row ^ bit).astype(half) for bit in (1, 2, 3))
    near_1, near_2, near_3 = (flip(part, "row", bit) for bit, part in zip((1, 2, 3), sends))
    own_part = (pick(total, row) + near_2.astype(f32)).astype(half)
    other_part = (near_1.astype(f32) + near_3.astype(f32)).astype(half)
    strip = jnp.where(odd, stack([other_part, own_part]), stack([own_part, other_part]))
    kept, passed = pick(strip, core), swap(pick(strip, 1 - core))

    def by_kind(values):
        values = values.reshape(block_rows, width // PAIR, 3, PAIR).transpose(2, 0, 1, 3)
        return values.reshape(3, block_rows, width)

    kept, passed = by_kind(kept), by_kind(passed)
    qkv_grads = jnp.where(first_core, cat([kept, passed], axis=2), cat([passed, kept], axis=2))
    qkv_grads = qkv_grads.astype(f32)

    input_grad = base + jnp.where(slot == which, 0.0, from_far[None].astype(f32))

    kept, passed = divide(norm_local)
    norm_grads = turn(kept + swap(passed))
    for axis in ("row", "dp"):
        one, two, three = (flip(norm_grads, axis, bit) for bit in (1, 2, 3))
        norm_grads = (norm_grads + one) + (two + three)
    return (
        layer_out,
        input_grad,
        qkv_grads[0],
        qkv_grads[1],
        qkv_grads[2],
        grad_out,
        grad_up,
        grad_down,
        norm_grads,
    )


def solution(mesh):
    placed = (
        P("dp", "row", "col"),
        P("dp", None),
        P(("dp", "row"), "col"),
        P(("dp", "row"), "col"),
        P(("dp", "row"), "col"),
        P(("dp", "row"), "col"),
        P(("dp", "row"), "col"),
        P(("dp", "row"), "col"),
        P("col"),
        P("col"),
        P("col"),
        P("col"),
        P("dp", "row", "col"),
    )
    body = fast_local if fits(mesh) else local
    return jax.shard_map(
        body,
        mesh=mesh,
        in_specs=placed,
        out_specs=(
            P("dp", "row", "col"),
            P("dp", "row", "col"),
            P(("dp", "row"), "col"),
            P(("dp", "row"), "col"),
            P(("dp", "row"), "col"),
            P(("dp", "row"), "col"),
            P(("dp", "row"), "col"),
            P(("dp", "row"), "col"),
            P(None, "col"),
        ),
        check_vma=False,
    )
```
